32 devices in a mesh: dp: 8 (over z, x), ctx: 4 (over y, core).
Axes of the slice: x: 2, y: 2, z: 4, core: 2. Of those that a mesh axis runs over, the one named last changes fastest.
Arguments:
- features: bfloat16 [8, 2048, 768], P('dp', 'ctx'), may hold values from -24 to 24
- bases: int32 [8, 2048], P('dp', 'ctx'), may hold values from 0 to 3
- dna_table: bfloat16 [4, 768], replicated, may hold values from -6 to 6
- norm_gain: bfloat16 [768], replicated, may hold values from 0.099609375 to 1.8984375
- w_conv: bfloat16 [5, 768, 768], replicated, may hold values from -0.09375 to 0.09375
- w_query: bfloat16 [768, 768], replicated, may hold values from -0.21875 to 0.21875
- w_key: bfloat16 [768, 768], replicated, may hold values from -0.21875 to 0.21875
- w_value: bfloat16 [768, 768], replicated, may hold values from -0.21875 to 0.21875
- w_out: bfloat16 [768, 768], replicated, may hold values from -0.21875 to 0.21875
- cotangent: bfloat16 [8, 128, 768], P('dp', 'ctx'), may hold values from -48 to 48
Outputs:
- grad_features: bfloat16 [8, 2048, 768], P('dp', 'ctx')
- grad_conv: float32 [768, 5, 768], P('ctx', None, 'dp')
The draws below stay inside these ranges and needn't reach their ends.
All inputs are finite; a program needn't handle non-finite values.
Results may differ from the reference program's by a relative error of at most 0.025.
The reference program's roundings to bfloat16 on the way count: a program that leaves them out, or rounds other values in their place, can miss the bound.
Values may be sent and summed in bfloat16 or wider, within the bound.
No kernel may reach another device: no remote copies, remote signals or barrier semaphores. Data moves between devices by JAX's collectives and lax.ppermute only.
A program may use at most 128 MiB of HBM per device.

```python
import jax
import jax.numpy as jnp
from jax import lax

C = 768
HEADS = 6
DH = 128
KW = 5
POOL = 16
LEN = 2048
TOKENS = 128
SEGS = 8


def draw_features(key, part):
    rough_key = jax.random.fold_in(jax.random.fold_in(key, 11), 0)
    blocks = LEN // POOL
    values = jax.random.normal(rough_key, (SEGS, blocks, POOL, C), jnp.float32)
    return jnp.clip(values.reshape(SEGS, LEN, C), -24.0, 24.0).astype(jnp.bfloat16)


def with_ends(array, rng, least, largest):
    index_at = [jax.random.randint(jax.random.fold_in(rng, axis), (), 0, length) for axis, length in enumerate(array.shape)]
    longest = array.shape.index(max(array.shape))
    beside = index_at[:longest] + [(index_at[longest] + 1) % array.shape[longest]] + index_at[longest + 1:]
    return array.at[tuple(index_at)].set(least).at[tuple(beside)].set(largest)


def shard_levels(stream_key, extent, pieces, low, largest):
    factor_of, own = 1.0, jax.random.fold_in(stream_key, 6)
    for position, blocks in pieces:
        steps = jnp.exp(jax.random.uniform(jax.random.fold_in(own, position), (blocks,), jnp.float32, low / len(pieces), largest / len(pieces)))
        factor_of = factor_of * jnp.repeat(steps, extent[position] // blocks).reshape([-1 if axis == position else 1 for axis in range(len(extent))])
    return factor_of


def noise(own_key, shape, deviation, bound, cuts=(), kind=jnp.bfloat16):
    loudness = shard_levels(own_key, shape, cuts, -0.22, 0.18) if cuts else 1.0
    entries = jax.random.normal(own_key, shape, jnp.float32) * deviation * loudness
    return jnp.minimum(jnp.maximum(entries, -bound), bound).astype(kind)


def setup_inputs(seed: int = 0) -> dict:
    key_of = jax.random.split(jax.random.key(seed), 11)
    return {
        "features": draw_features(jax.random.fold_in(key_of[10], 71), 0),
        "bases": with_ends(jax.random.randint(key_of[1], (SEGS, LEN), 0, 4), jax.random.fold_in(key_of[1], 1), 0, 3).astype(jnp.int32),
        "dna_table": noise(key_of[2], (4, C), 1.0, 6.0),
        "norm_gain": jnp.clip(1.0 + 0.18 * jax.random.normal(key_of[3], (C,), jnp.float32), 0.099609375, 1.8984375).astype(jnp.bfloat16),
        "w_conv": noise(key_of[4], (KW, C, C), (KW * C) ** -0.5, 0.09375),
        "w_query": noise(key_of[5], (C, C), C ** -0.5, 0.21875),
        "w_key": noise(key_of[6], (C, C), C ** -0.5, 0.21875),
        "w_value": noise(key_of[7], (C, C), C ** -0.5, 0.21875),
        "w_out": noise(key_of[8], (C, C), C ** -0.5, 0.21875),
        "cotangent": noise(key_of[9], (SEGS, TOKENS, C), 8.0, 48.0, ((0, 8), (1, 4))),
    }


EPSILON = 1e-06
GELU_SCALE = 0.7978845608028654
CUBIC = 0.044715

def gelu_pair(inputs):
    inner = GELU_SCALE * (inputs + CUBIC * inputs ** 3)
    tanh_val = jnp.tanh(inner)
    values = 0.5 * inputs * (1.0 + tanh_val)
    slopes = 0.5 * (1.0 + tanh_val) + 0.5 * inputs * (1.0 - tanh_val ** 2) * GELU_SCALE * (1.0 + 3.0 * CUBIC * inputs ** 2)
    return (values, slopes)

def heads_split(matrix):
    return matrix.reshape(matrix.shape[0], HEADS, DH).astype(jnp.float32)

def dot_right_t(left, right):
    return lax.dot_general(left, right, (((1,), (1,)), ((), ())), preferred_element_type=jnp.float32)

def dot_left_t(left, right):
    return lax.dot_general(left, right, (((0,), (0,)), ((), ())), preferred_element_type=jnp.float32)

def segment(seg_feat, seg_base, seg_cot, dna_table, norm_gain, w_conv, w_query, w_key, w_value, w_out):
    half_width = KW // 2
    onehot = (seg_base[:, None] == jnp.arange(4, dtype=jnp.int32)[None, :]).astype(jnp.bfloat16)
    summed_in = seg_feat.astype(jnp.float32) + jnp.dot(onehot, dna_table, preferred_element_type=jnp.float32)
    inv_rms = lax.rsqrt(lax.optimization_barrier(jnp.mean(summed_in * summed_in, axis=-1, keepdims=True)) + EPSILON)
    normed = summed_in * inv_rms
    gain_f = norm_gain.astype(jnp.float32)
    pre_gelu = normed * gain_f
    gelu_val, slopes = gelu_pair(pre_gelu)
    act = gelu_val.astype(jnp.bfloat16)
    length = act.shape[0]
    padded = jnp.pad(act, ((half_width, half_width), (0, 0)))
    conv = jnp.zeros((length, C), jnp.float32)
    for offset in range(KW):
        conv = conv + jnp.dot(padded[offset:offset + length], w_conv[offset], preferred_element_type=jnp.float32)
    resid = summed_in + conv
    pooled = resid.reshape(-1, POOL, C).mean(axis=1).astype(jnp.bfloat16)
    queries = jnp.dot(pooled, w_query, preferred_element_type=jnp.float32).astype(jnp.bfloat16)
    keys_all = jnp.dot(pooled, w_key, preferred_element_type=jnp.float32).astype(jnp.bfloat16)
    values_all = jnp.dot(pooled, w_value, preferred_element_type=jnp.float32).astype(jnp.bfloat16)
    scale = 1.0 / DH ** 0.5
    scores = jnp.einsum('qhd,khd->hqk', heads_split(queries), heads_split(keys_all)) * scale
    probs = jax.nn.softmax(scores, axis=-1)
    probs_b = probs.astype(jnp.bfloat16)
    attn_out = jnp.einsum('hqk,khd->qhd', probs_b.astype(jnp.float32), heads_split(values_all))
    attn_out = attn_out.reshape(-1, C).astype(jnp.bfloat16)
    grad_attn = dot_right_t(seg_cot, w_out).astype(jnp.bfloat16)
    grad_prob = jnp.einsum('qhd,khd->hqk', heads_split(grad_attn), heads_split(values_all))
    row_delta = lax.optimization_barrier(jnp.sum(heads_split(grad_attn) * heads_split(attn_out), axis=-1)).transpose(1, 0)[:, :, None]
    grad_score = (probs * (grad_prob - row_delta) * scale).astype(jnp.bfloat16).astype(jnp.float32)
    grad_q = jnp.einsum('hqk,khd->qhd', grad_score, heads_split(keys_all)).reshape(-1, C).astype(jnp.bfloat16)
    grad_k = jnp.einsum('hqk,qhd->khd', grad_score, heads_split(queries)).reshape(-1, C).astype(jnp.bfloat16)
    grad_v = jnp.einsum('hqk,qhd->khd', probs_b.astype(jnp.float32), heads_split(grad_attn)).reshape(-1, C).astype(jnp.bfloat16)
    grad_pooled = seg_cot.astype(jnp.float32) + dot_right_t(grad_q, w_query) + dot_right_t(grad_k, w_key) + dot_right_t(grad_v, w_value)
    grad_rows = jnp.repeat((grad_pooled / POOL).astype(jnp.bfloat16), POOL, axis=0)
    grad_pad = jnp.pad(grad_rows, ((half_width, half_width), (0, 0)))
    grad_act = jnp.zeros((length, C), jnp.float32)
    wgrad_list = []
    for offset in range(KW):
        begin = 2 * half_width - offset
        grad_act = grad_act + dot_right_t(grad_pad[begin:begin + length], w_conv[offset])
        wgrad_list.append(dot_left_t(padded[offset:offset + length], grad_rows))
    wgrad = jnp.stack(wgrad_list, axis=1)
    grad_norm = grad_act * slopes * gain_f
    grad_in = grad_rows.astype(jnp.float32) + inv_rms * (grad_norm - normed * lax.optimization_barrier(jnp.mean(grad_norm * normed, axis=-1, keepdims=True)))
    return (grad_in.astype(jnp.bfloat16), wgrad)

def reference(features, bases, dna_table, norm_gain, w_conv, w_query, w_key, w_value, w_out, cotangent):

    def segment_step(totals, slices):
        seg_feat, seg_base, seg_cot = slices
        grad_in, wgrad = segment(seg_feat, seg_base, seg_cot, dna_table, norm_gain, w_conv, w_query, w_key, w_value, w_out)
        return (totals + wgrad, grad_in)
    totals, grad_list = lax.scan(segment_step, jnp.zeros((C, KW, C), jnp.float32), (features, bases, cotangent))
    factor = 1.0 / (SEGS * LEN) ** 0.5
    return (grad_list, totals * factor)
```

```python
import functools

import jax
import jax.numpy as jnp
import numpy as np
from jax import lax
from jax.experimental import pallas as pl
from jax.experimental.pallas import tpu as pltpu
from jax.sharding import PartitionSpec as P

HEADS = 6
DH = 128

EPSILON = 1e-06
GELU_SCALE = 0.7978845608028654
CUBIC = 0.044715
F32 = jnp.float32
BF16 = jnp.bfloat16


def dot_nn(left, right):
    return lax.dot_general(left, right, (((1,), (0,)), ((), ())), preferred_element_type=F32)


def dot_nt(left, right):
    return lax.dot_general(left, right, (((1,), (1,)), ((), ())), preferred_element_type=F32)


def dot_tn(left, right):
    return lax.dot_general(left, right, (((0,), (0,)), ((), ())), preferred_element_type=F32)


def split2(value):
    high = value.astype(BF16)
    return high, (value - high.astype(F32)).astype(BF16)


def iota(shape, dim):
    return lax.broadcasted_iota(jnp.int32, shape, dim)


def normed_of(summed):
    inv_rms = lax.rsqrt(jnp.mean(summed * summed, axis=-1, keepdims=True) + EPSILON)
    return inv_rms, summed * inv_rms


def gelu_of(u):
    tanh_val = jnp.tanh(GELU_SCALE * (u + CUBIC * (u * u * u)))
    return tanh_val, 0.5 * u * (1.0 + tanh_val)


def first_kernel(
    kernel, pool, tok_rows, blocks, scal, feat, base, table, gain, near, far, w_hbm,
    pooled, sent, slope_out, normed_out,
    w_buf, act_buf, high_buf, low_buf, taps, sums, sem,
):
    step = pl.program_id(0)
    half = kernel // 2
    rows, channels = feat.shape
    copy = pltpu.make_async_copy(w_hbm, w_buf, sem)

    @pl.when(step == 0)
    def _():
        copy.start()
        taps[...] = jnp.zeros_like(taps)
        sums[...] = jnp.zeros_like(sums)

    gain_f = gain[...].astype(F32)
    onehot = (iota((table.shape[0], rows), 0) == base[...]).astype(BF16)
    embed = dot_tn(onehot, table[...])
    chunk = 32
    for begin in range(0, rows, chunk):
        part = slice(begin, begin + chunk)
        summed = feat[part, :].astype(F32) + embed[part, :]
        inv_rms, normed = normed_of(summed)
        u = normed * gain_f
        tanh_val, value = gelu_of(u)
        slopes = 0.5 * (1.0 + tanh_val) + 0.5 * u * (1.0 - tanh_val * tanh_val) * GELU_SCALE * (
            1.0 + 3.0 * CUBIC * (u * u)
        )
        act_buf[part, :] = value.astype(BF16)
        high_buf[part, :], low_buf[part, :] = split2(summed)
        slope_out[part, :] = inv_rms * (slopes * gain_f)
        normed_out[part, :] = normed
    shape = (kernel * tok_rows, rows)
    row = iota(shape, 0)
    tap = sum((row >= tok_rows * j).astype(jnp.int32) for j in range(1, kernel))
    token = row - tap * tok_rows
    offset = iota(shape, 1) + step * rows - tap + half - token * pool
    spread = ((offset >= 0) & (offset < pool)).astype(BF16)
    taps[...] += dot_nn(spread, act_buf[...])
    plain = spread[half * tok_rows : (half + 1) * tok_rows, :]
    sums[...] += dot_nn(plain, high_buf[...]) + dot_nn(plain, low_buf[...])

    @pl.when(step == pl.num_programs(0) - 1)
    def _():
        me = scal[0]
        edges = []
        for edge in (near, far):
            _, normed = normed_of(edge[...])
            edges.append(gelu_of(normed * gain_f)[1].astype(BF16).astype(F32))
        odd = (me % 2) == 1
        before = jnp.where(odd, edges[0], edges[1])
        after = jnp.where(odd, edges[1], edges[0])
        for j in range(half):
            at = j * tok_rows
            taps[at : at + 1, :] += jnp.sum(before[j:, :], axis=0, keepdims=True)
            at = (kernel - j) * tok_rows - 1
            taps[at : at + 1, :] += jnp.sum(after[: half - j, :], axis=0, keepdims=True)
        copy.wait()
        total = jnp.zeros((2 * tok_rows, channels), F32)
        highs = []
        for j in range(kernel):
            high, low = split2(taps[j * tok_rows : (j + 1) * tok_rows, :])
            highs.append(high)
            total = total + dot_nn(jnp.concatenate([high, low], axis=0), w_buf[j])
        conv = total[:tok_rows] + total[tok_rows:]
        pooled[...] = ((sums[...] + conv) * (1.0 / pool)).astype(BF16)
        width = channels // blocks
        for b in range(blocks):
            block = jnp.concatenate([h[:, b * width : (b + 1) * width] for h in highs], axis=1)
            sent[b ^ me] = block


def attention_kernel(
    pool, steps, scal, pooled_ref, cot_ref, wq_hbm, wk_hbm, wv_hbm, wo_hbm,
    g_out, gt_out, w_buf, q_buf, k_buf, v_buf, ga_buf, gq_buf, gk_buf, gv_buf, sems,
):
    copies = [
        pltpu.make_async_copy(src, w_buf.at[i], sems.at[i])
        for i, src in enumerate((wq_hbm, wk_hbm, wv_hbm, wo_hbm))
    ]
    for copy in copies:
        copy.start()
    pooled = pooled_ref[...]
    for i, dst in enumerate((q_buf, k_buf, v_buf)):
        copies[i].wait()
        dst[...] = dot_nn(pooled, w_buf[i]).astype(BF16)
    copies[3].wait()
    ga_buf[...] = dot_nt(cot_ref[...], w_buf[3]).astype(BF16)
    scale = 1.0 / DH**0.5
    for h in range(HEADS):
        cols = slice(h * DH, (h + 1) * DH)
        q, k, v, ga = q_buf[:, cols], k_buf[:, cols], v_buf[:, cols], ga_buf[:, cols]
        scores = dot_nt(q, k) * scale
        expo = jnp.exp(scores - jnp.max(scores, axis=-1, keepdims=True))
        probs = expo / jnp.sum(expo, axis=-1, keepdims=True)
        probs_b = probs.astype(BF16)
        out = dot_nn(probs_b, v).astype(BF16)
        delta = jnp.sum(ga.astype(F32) * out.astype(F32), axis=-1, keepdims=True)
        grad_score = (probs * (dot_nt(ga, v) - delta) * scale).astype(BF16)
        gq_buf[:, cols] = dot_nn(grad_score, k).astype(BF16)
        gk_buf[:, cols] = dot_tn(grad_score, q).astype(BF16)
        gv_buf[:, cols] = dot_tn(probs_b, ga).astype(BF16)
    grad = cot_ref[...].astype(F32)
    for i, src in enumerate((gq_buf, gk_buf, gv_buf)):
        grad = grad + dot_nt(src[...], w_buf[i])
    g = (grad * (1.0 / pool)).astype(BF16)
    g_out[...] = g
    tokens = g.shape[0]
    eye = (iota((tokens, tokens), 0) == iota((tokens, tokens), 1)).astype(BF16)
    turned = dot_tn(g, eye).astype(BF16)
    span = turned.shape[0] // steps
    for z in range(steps):
        gt_out[scal[z]] = turned[z * span : (z + 1) * span, :]


def input_grad_kernel(
    kernel, pool, tok_rows, padded, scal, g_ref, slope, normed, w_hbm,
    out, w_buf, high_buf, low_buf, rows_buf, sems,
):
    step = pl.program_id(0)
    half = kernel // 2
    rows = out.shape[0]
    tokens = g_ref.shape[0]

    @pl.when(step == 0)
    def _():
        copies = [pltpu.make_async_copy(w_hbm.at[j], w_buf.at[j], sems.at[j]) for j in range(kernel)]
        for copy in copies:
            copy.start()
        row = iota((padded, tokens), 0)
        source = jnp.where(row == 0, scal[1], jnp.where(row == tok_rows + 1, scal[2], row - 1))
        source = jnp.where(row > tok_rows + 1, -1, source)
        pick = (source == iota((padded, tokens), 1)).astype(BF16)
        near = dot_nn(pick, g_ref[...]).astype(BF16)
        rows_buf[...] = near
        for j in range(kernel):
            copies[j].wait()
            part = slice(j * padded, (j + 1) * padded)
            high_buf[part, :], low_buf[part, :] = split2(dot_nt(near, w_buf[j]))

    shape = (rows, kernel * padded)
    col = iota(shape, 1)
    tap = sum((col >= padded * j).astype(jnp.int32) for j in range(1, kernel))
    token = col - tap * padded - 1
    offset = iota(shape, 0) + step * rows - tap + half - token * pool
    spread = ((offset >= 0) & (offset < pool)).astype(BF16)
    grad_act = dot_nn(spread, high_buf[...]) + dot_nn(spread, low_buf[...])
    plain = spread[:, half * padded : (half + 1) * padded]
    grad_rows = dot_nn(plain, rows_buf[...])
    scaled = grad_act * slope[...]
    unit = normed[...]
    mean = jnp.mean(scaled * unit, axis=-1, keepdims=True)
    out[...] = (grad_rows + scaled - unit * mean).astype(BF16)


def partial_kernel(factor, scal, acts, gts, mine, theirs):
    span = gts.shape[1] // 2
    own = scal[3]
    total = None
    for s in range(acts.shape[0]):
        term = lax.dot_general(
            acts[s], gts[s], (((0,), (1,)), ((), ())), preferred_element_type=F32
        )
        total = term if total is None else total + term
    total = total * factor
    low, high = total[:, :span], total[:, span:]
    first = own == 0
    mine[...] = jnp.where(first, low, high)
    theirs[...] = jnp.where(first, high, low).astype(BF16)


def join_kernel(kernel, mine, other, out):
    width = out.shape[1]
    for j in range(kernel):
        part = slice(j * width, (j + 1) * width)
        out[j] = mine[part, :] + other[part, :].astype(F32)


def xor_order(count):
    order = [0]
    bit = count // 2
    while bit:
        order = order + [v ^ bit for v in order]
        bit //= 2
    return order


def bits_of(count):
    bit = count // 2
    while bit:
        yield bit
        bit //= 2


def swap(value, axis, bit):
    count = lax.axis_size(axis)
    return lax.ppermute(value, axis, [(i, i ^ bit) for i in range(count)])


def ring_of(count):
    odds = [z for z in range(count) if z % 2]
    evens = [z for z in range(2, count) if z % 2 == 0]
    return [0] + odds + evens[::-1]


def per_device(
    features, bases, dna_table, norm_gain, w_conv, w_query, w_key, w_value, w_out, cotangent
):
    feat, cot = features[0], cotangent[0]
    kernel = w_conv.shape[0]
    half = kernel // 2
    length, channels = feat.shape
    tok_rows = cot.shape[0]
    pool = length // tok_rows
    n_ctx, n_dp = lax.axis_size("ctx"), lax.axis_size("dp")
    pair = 2
    n_ring = n_dp // pair
    tokens = n_ctx * tok_rows
    width = channels // n_ctx
    span = channels // n_ring
    ctx = lax.axis_index("ctx")
    dp = lax.axis_index("dp")

    order = xor_order(n_ctx)
    place = {rel: at for at, rel in enumerate(order)}
    ctx_rows = []
    for c in range(n_ctx):
        before = place[c ^ (c - 1)] * tok_rows + tok_rows - 1 if c else -1
        after = place[c ^ (c + 1)] * tok_rows if c + 1 < n_ctx else -1
        ctx_rows.append([c, before, after])
    ring = ring_of(n_ring)
    where = {z: r for r, z in enumerate(ring)}
    dp_rows = [
        [(where[z] - where[d // pair]) % n_ring for z in range(n_ring)] + [d % pair] for d in range(n_dp)
    ]
    ctx_scal = jnp.asarray(np.array(ctx_rows, np.int32))[ctx]
    dp_scal = jnp.asarray(np.array(dp_rows, np.int32))[dp]
    scal3 = jnp.concatenate([ctx_scal, dp_scal[n_ring:]])

    odd = ctx % 2 == 1
    ends = jnp.concatenate([feat[:half], feat[length - half :]], axis=0).astype(F32)
    end_base = jnp.concatenate([bases[0, :half], bases[0, length - half :]])
    table_f = dna_table.astype(F32)
    for b in range(table_f.shape[0]):
        ends = ends + jnp.where((end_base == b)[:, None], table_f[b][None, :], 0.0)
    first, last = ends[:half], ends[half:]
    near = swap(jnp.where(odd, first, last), "ctx", 1)
    steps = [(i, i + 1) for i in range(1, n_ctx - 1, 2)]
    far = lax.ppermute(
        jnp.where(odd, last, first), "ctx", steps + [(b, a) for a, b in steps]
    )

    grid = 4
    block = length // grid
    smem = pl.BlockSpec(memory_space=pltpu.SMEM)
    anywhere = pl.BlockSpec(memory_space=pl.ANY)
    whole = pl.BlockSpec(memory_space=pltpu.VMEM)
    by_rows = pl.BlockSpec((block, channels), lambda i: (i, 0))
    pooled, acts, slope, normed = pl.pallas_call(
        functools.partial(first_kernel, kernel, pool, tok_rows, n_ctx),
        grid=(grid,),
        in_specs=[
            smem,
            by_rows,
            pl.BlockSpec((1, block), lambda i: (0, i)),
            whole, whole, whole, whole, anywhere,
        ],
        out_specs=[whole, whole, by_rows, by_rows],
        out_shape=[
            jax.ShapeDtypeStruct((tok_rows, channels), BF16),
            jax.ShapeDtypeStruct((n_ctx, tok_rows, kernel * width), BF16),
            jax.ShapeDtypeStruct((length, channels), F32),
            jax.ShapeDtypeStruct((length, channels), F32),
        ],
        scratch_shapes=[
            pltpu.VMEM((kernel, channels, channels), BF16),
            pltpu.VMEM((block, channels), BF16),
            pltpu.VMEM((block, channels), BF16),
            pltpu.VMEM((block, channels), BF16),
            pltpu.VMEM((kernel * tok_rows, channels), F32),
            pltpu.VMEM((tok_rows, channels), F32),
            pltpu.SemaphoreType.DMA,
        ],
        name="first_pass",
    )(ctx_scal, feat, bases, dna_table, norm_gain[None], near, far, w_conv)

    rows = jnp.stack([pooled, cot])
    for bit in bits_of(n_ctx):
        rows = jnp.concatenate([rows, swap(rows, "ctx", bit)], axis=1)

    for bit in bits_of(n_ctx):
        got = swap(acts[bit:], "ctx", bit)
        acts = jnp.concatenate([acts[:bit], got], axis=1)

    g_all, gts = pl.pallas_call(
        functools.partial(attention_kernel, pool, n_ring),
        in_specs=[smem, whole, whole, anywhere, anywhere, anywhere, anywhere],
        out_specs=[whole, whole],
        out_shape=[
            jax.ShapeDtypeStruct((tokens, channels), BF16),
            jax.ShapeDtypeStruct((n_ring, span, tokens), BF16),
        ],
        scratch_shapes=[pltpu.VMEM((4, channels, channels), BF16)]
        + [pltpu.VMEM((tokens, channels), BF16)] * 7
        + [pltpu.SemaphoreType.DMA((4,))],
        name="attention",
    )(dp_scal, rows[0], rows[1], w_query, w_key, w_value, w_out)

    def ring_perm(shift):
        pairs = []
        for r in range(n_ring):
            for x in range(pair):
                pairs.append((ring[r] * pair + x, ring[(r + shift) % n_ring] * pair + x))
        return pairs

    held = [acts[0]]
    for _ in range(1, n_ring):
        held.append(lax.ppermute(held[-1], "dp", ring_perm(1)))
    grads = [gts[0]]
    for shift in range(1, n_ring):
        grads.append(lax.ppermute(gts[shift], "dp", ring_perm(shift)))

    padded = -(-(tok_rows + 2) // 8) * 8
    grad_in = pl.pallas_call(
        functools.partial(input_grad_kernel, kernel, pool, tok_rows, padded),
        grid=(grid,),
        in_specs=[smem, whole, by_rows, by_rows, anywhere],
        out_specs=by_rows,
        out_shape=jax.ShapeDtypeStruct((length, channels), BF16),
        scratch_shapes=[
            pltpu.VMEM((kernel, channels, channels), BF16),
            pltpu.VMEM((kernel * padded, channels), BF16),
            pltpu.VMEM((kernel * padded, channels), BF16),
            pltpu.VMEM((padded, channels), BF16),
            pltpu.SemaphoreType.DMA((kernel,)),
        ],
        name="input_grad",
    )(scal3, g_all, slope, normed, w_conv)

    factor = 1.0 / (n_dp * length * n_ctx) ** 0.5
    acts_all = jnp.stack(held)
    gts_all = jnp.stack(grads)
    mine, theirs = pl.pallas_call(
        functools.partial(partial_kernel, factor),
        in_specs=[smem, whole, whole],
        out_specs=[whole, whole],
        out_shape=[
            jax.ShapeDtypeStruct((kernel * width, span // pair), F32),
            jax.ShapeDtypeStruct((kernel * width, span // pair), BF16),
        ],
        name="kernel_grad",
    )(scal3, acts_all, gts_all)
    other = swap(theirs, "dp", 1)
    grad_conv = pl.pallas_call(
        functools.partial(join_kernel, kernel),
        in_specs=[whole, whole],
        out_specs=whole,
        out_shape=jax.ShapeDtypeStruct((kernel, width, span // pair), F32),
        name="kernel_grad_join",
    )(mine, other)
    return grad_in[None], jnp.transpose(grad_conv, (1, 0, 2))


def solution(mesh):
    in_specs = (
        P("dp", "ctx", None),
        P("dp", "ctx"),
        P(),
        P(),
        P(),
        P(),
        P(),
        P(),
        P(),
        P("dp", "ctx", None),
    )
    out_specs = (P("dp", "ctx", None), P("ctx", None, "dp"))
    return jax.shard_map(
        per_device, mesh=mesh, in_specs=in_specs, out_specs=out_specs, check_vma=False
    )
```

```python
import functools

import jax
import jax.numpy as jnp
from jax import lax
from jax.experimental import pallas as pl
from jax.experimental.pallas import tpu as pltpu
from jax.sharding import PartitionSpec as P

HEADS = 6
DH = 128

EPSILON = 1e-06
GELU_SCALE = 0.7978845608028654
CUBIC = 0.044715
F32 = jnp.float32
BF16 = jnp.bfloat16
VMEM_LIMIT = 20 << 20
PAIR = 2


def dot_nn(left, right):
    return lax.dot_general(left, right, (((1,), (0,)), ((), ())), preferred_element_type=F32)


def dot_nt(left, right):
    return lax.dot_general(left, right, (((1,), (1,)), ((), ())), preferred_element_type=F32)


def dot_tn(left, right):
    return lax.dot_general(left, right, (((0,), (0,)), ((), ())), preferred_element_type=F32)


def split2(value):
    high = value.astype(BF16)
    return high, (value - high.astype(F32)).astype(BF16)


def iota(shape, dim):
    return lax.broadcasted_iota(jnp.int32, shape, dim)


def normed_of(summed):
    inv_rms = lax.rsqrt(jnp.mean(summed * summed, axis=-1, keepdims=True) + EPSILON)
    return inv_rms, summed * inv_rms


def gelu_of(u):
    tanh_val = jnp.tanh(GELU_SCALE * (u + CUBIC * (u * u * u)))
    return tanh_val, 0.5 * u * (1.0 + tanh_val)


def pick(index, values):
    out = jnp.int32(values[0])
    for at, value in enumerate(values[1:], 1):
        out = jnp.where(index == at, jnp.int32(value), out)
    return out


def edge_kernel(half, top, bottom, base, table, near, far):
    odd = lax.axis_index("ctx") % 2 == 1
    length = base.shape[1]
    edge = top.shape[0]
    table_f = table[...].astype(F32)
    kinds = table_f.shape[0]

    def row(values, at, position):
        code = base[0, position]
        out = values[at : at + 1, :]
        for b in range(kinds):
            out = out + jnp.where(code == b, table_f[b : b + 1, :], 0.0)
        return out

    top_f, bottom_f = top[...].astype(F32), bottom[...].astype(F32)
    for i in range(half):
        first = row(top_f, i, i)
        last = row(bottom_f, edge - half + i, length - half + i)
        near[i : i + 1, :] = jnp.where(odd, first, last)
        far[i : i + 1, :] = jnp.where(odd, last, first)


def act_kernel(
    kernel, pool, tok_rows, feat, base, table, gain,
    taps, sums, slope_out, normed_out, act_buf, high_buf, low_buf,
):
    half = kernel // 2
    rows, channels = feat.shape
    block = act_buf.shape[0]
    gain_f = gain[...].reshape(1, channels).astype(F32)
    taps[...] = jnp.zeros_like(taps)
    sums[...] = jnp.zeros_like(sums)
    chunk = 32

    @pl.loop(0, rows // block)
    def _(step):
        start = pl.multiple_of(step * block, block)
        onehot = (iota((table.shape[0], block), 0) == base[:, pl.ds(start, block)]).astype(BF16)
        embed = dot_tn(onehot, table[...])
        for begin in range(0, block, chunk):
            part = slice(begin, begin + chunk)
            here = pl.ds(start + begin, chunk)
            summed = feat[here, :].astype(F32) + embed[part, :]
            inv_rms, normed = normed_of(summed)
            u = normed * gain_f
            tanh_val, value = gelu_of(u)
            slopes = 0.5 * (1.0 + tanh_val) + 0.5 * u * (1.0 - tanh_val * tanh_val) * GELU_SCALE * (
                1.0 + 3.0 * CUBIC * (u * u)
            )
            act_buf[part, :] = value.astype(BF16)
            high_buf[part, :], low_buf[part, :] = split2(summed)
            slope_out[here, :] = inv_rms * (slopes * gain_f)
            normed_out[here, :] = normed
        shape = (kernel * tok_rows, block)
        row = iota(shape, 0)
        tap = sum((row >= tok_rows * j).astype(jnp.int32) for j in range(1, kernel))
        token = row - tap * tok_rows
        offset = iota(shape, 1) + start - tap + half - token * pool
        spread = ((offset >= 0) & (offset < pool)).astype(BF16)
        taps[...] += dot_nn(spread, act_buf[...])
        plain = spread[half * tok_rows : (half + 1) * tok_rows, :]
        sums[...] += dot_nn(plain, high_buf[...]) + dot_nn(plain, low_buf[...])


def taps_kernel(kernel, tok_rows, blocks, taps, gain, near, far, pairs, *rest):
    outs, turn = rest[:blocks], rest[blocks]
    half = kernel // 2
    me = lax.axis_index("ctx")
    odd = me % 2 == 1
    channels = taps.shape[1]
    gain_f = gain[...].reshape(1, channels).astype(F32)
    edges = []
    for edge in (near, far):
        _, normed = normed_of(edge[...])
        edges.append(gelu_of(normed * gain_f)[1].astype(BF16).astype(F32))
    before = jnp.where(odd, edges[0], edges[1])
    after = jnp.where(odd, edges[1], edges[0])
    row = iota((tok_rows, channels), 0)
    highs = []
    for j in range(kernel):
        value = taps[j * tok_rows : (j + 1) * tok_rows, :]
        if j < half:
            extra = jnp.sum(before[j:, :], axis=0, keepdims=True)
            value = value + jnp.where(row == 0, extra, 0.0)
        if j > half:
            extra = jnp.sum(after[: j - half, :], axis=0, keepdims=True)
            value = value + jnp.where(row == tok_rows - 1, extra, 0.0)
        high, low = split2(value)
        highs.append(high)
        pairs[j] = jnp.concatenate([high, low], axis=0)
    width = channels // blocks
    for b in range(blocks):
        turn[b ^ me] = jnp.concatenate([h[:, b * width : (b + 1) * width] for h in highs], axis=1)
    for b in range(blocks):
        outs[b][...] = turn[b]


def pool_kernel(pool, pairs, sums, weights, cot, rows):
    tok_rows = sums.shape[0]
    total = dot_nn(pairs[0], weights[0])
    for j in range(1, pairs.shape[0]):
        total = total + dot_nn(pairs[j], weights[j])
    conv = total[:tok_rows] + total[tok_rows:]
    rows[0] = ((sums[...] + conv) * (1.0 / pool)).astype(BF16)
    rows[1] = cot[...]


def pack_kernel(*refs):
    *parts, out = refs
    at = 0
    for part in parts:
        out[at : at + part.shape[0], :] = part[...]
        at += part.shape[0]


def attention_kernel(pool, blocks, ring, *refs):
    parts, refs = refs[:blocks], refs[blocks:]
    weights, refs = refs[:4], refs[4:]
    g_out, refs = refs[0], refs[1:]
    steps = len(ring)
    gts, refs = refs[:steps], refs[steps:]
    p_buf, c_buf, q_buf, k_buf, v_buf, ga_buf, gq_buf, gk_buf, gv_buf, turn = refs
    size = parts[0].shape[1]
    for at, part in enumerate(parts):
        p_buf[at * size : (at + 1) * size, :] = part[0]
        c_buf[at * size : (at + 1) * size, :] = part[1]
    for i, dst in enumerate((q_buf, k_buf, v_buf)):
        dst[...] = dot_nn(p_buf[...], weights[i][...]).astype(BF16)
    ga_buf[...] = dot_nt(c_buf[...], weights[3][...]).astype(BF16)
    scale = 1.0 / DH**0.5
    for h in range(HEADS):
        cols = slice(h * DH, (h + 1) * DH)
        q, k, v, ga = q_buf[:, cols], k_buf[:, cols], v_buf[:, cols], ga_buf[:, cols]
        scores = dot_nt(q, k) * scale
        expo = jnp.exp(scores - jnp.max(scores, axis=-1, keepdims=True))
        probs = expo / jnp.sum(expo, axis=-1, keepdims=True)
        probs_b = probs.astype(BF16)
        out = dot_nn(probs_b, v).astype(BF16)
        delta = jnp.sum(ga.astype(F32) * out.astype(F32), axis=-1, keepdims=True)
        grad_score = (probs * (dot_nt(ga, v) - delta) * scale).astype(BF16)
        gq_buf[:, cols] = dot_nn(grad_score, k).astype(BF16)
        gk_buf[:, cols] = dot_tn(grad_score, q).astype(BF16)
        gv_buf[:, cols] = dot_tn(probs_b, ga).astype(BF16)
    grad = c_buf[...].astype(F32)
    for i, src in enumerate((gq_buf, gk_buf, gv_buf)):
        grad = grad + dot_nt(src[...], weights[i][...])
    g = (grad * (1.0 / pool)).astype(BF16)
    g_out[...] = g
    tokens = g.shape[0]
    eye = (iota((tokens, tokens), 0) == iota((tokens, tokens), 1)).astype(BF16)
    turned = dot_tn(g, eye).astype(BF16)
    span = turned.shape[0] // steps
    here = pick(lax.axis_index("dp") // PAIR, [ring.index(z) for z in range(steps)])
    for r in range(steps):
        z = ring[r]
        turn[lax.rem(r - here + steps, steps)] = turned[z * span : (z + 1) * span, :]
    for r in range(steps):
        gts[r][...] = turn[r]


def spread_kernel(kernel, tok_rows, befores, afters, g_ref, weights, highs, lows, near):
    tokens = g_ref.shape[0]
    padded = near.shape[0]
    me = lax.axis_index("ctx")
    row = iota((padded, tokens), 0)
    source = jnp.where(
        row == 0, pick(me, befores), jnp.where(row == tok_rows + 1, pick(me, afters), row - 1)
    )
    source = jnp.where(row > tok_rows + 1, -1, source)
    chosen = (source == iota((padded, tokens), 1)).astype(BF16)
    rows = dot_nn(chosen, g_ref[...]).astype(BF16)
    near[...] = rows
    for j in range(kernel):
        part = slice(j * padded, (j + 1) * padded)
        highs[part, :], lows[part, :] = split2(dot_nt(rows, weights[j]))


def input_grad_kernel(kernel, pool, highs, lows, near, slope, normed, out):
    half = kernel // 2
    rows = out.shape[0]
    padded = near.shape[0]
    start = pl.program_id(0) * rows
    here = pl.ds(pl.multiple_of(start, rows), rows)
    shape = (rows, kernel * padded)
    col = iota(shape, 1)
    tap = sum((col >= padded * j).astype(jnp.int32) for j in range(1, kernel))
    token = col - tap * padded - 1
    offset = iota(shape, 0) + start - tap + half - token * pool
    spread = ((offset >= 0) & (offset < pool)).astype(BF16)
    grad_act = dot_nn(spread, highs[...]) + dot_nn(spread, lows[...])
    plain = spread[:, half * padded : (half + 1) * padded]
    grad_rows = dot_nn(plain, near[...])
    scaled = grad_act * slope[here, :]
    unit = normed[here, :]
    mean = jnp.mean(scaled * unit, axis=-1, keepdims=True)
    out[...] = (grad_rows + scaled - unit * mean).astype(BF16)


def kernel_grad_kernel(factor, steps, *refs):
    acts, gts, (mine, theirs, buf) = refs[:steps], refs[steps : 2 * steps], refs[2 * steps :]
    own = lax.axis_index("dp") % PAIR
    total = None
    for act, gt in zip(acts, gts):
        term = dot_nn(gt[...], act[...])
        total = term if total is None else total + term
    span = mine.shape[0]
    for i in range(PAIR):
        buf[i] = total[i * span : (i + 1) * span, :] * factor
    mine[...] = buf[own]
    theirs[...] = buf[1 - own].astype(BF16)


def join_kernel(kernel, mine, other, out):
    width = out.shape[1]
    total = jnp.transpose(mine[...] + other[...].astype(F32))
    for j in range(kernel):
        out[j] = total[j * width : (j + 1) * width, :]


def xor_order(count):
    order = [0]
    bit = count // 2
    while bit:
        order = order + [v ^ bit for v in order]
        bit //= 2
    return order


def swap(value, axis, bit):
    count = lax.axis_size(axis)
    return lax.ppermute(value, axis, [(i, i ^ bit) for i in range(count)])


def ring_of(count):
    odds = [z for z in range(count) if z % 2]
    evens = [z for z in range(2, count) if z % 2 == 0]
    return [0] + odds + evens[::-1]


WHOLE = pl.BlockSpec(memory_space=pltpu.VMEM)


def call(body, name, args, outs, scratch=(), **options):
    options.setdefault("in_specs", [WHOLE] * len(args))
    options.setdefault("out_specs", [WHOLE] * len(outs))
    return pl.pallas_call(
        body,
        out_shape=list(outs),
        scratch_shapes=list(scratch),
        compiler_params=pltpu.CompilerParams(vmem_limit_bytes=VMEM_LIMIT),
        name=name,
        **options,
    )(*args)


def held(value):
    return pltpu.with_memory_space_constraint(value, pltpu.VMEM)


def per_device(
    features, bases, dna_table, norm_gain, w_conv, w_query, w_key, w_value, w_out, cotangent
):
    feat, cot = features[0], cotangent[0]
    kernel = w_conv.shape[0]
    half = kernel // 2
    length, channels = feat.shape
    tok_rows = cot.shape[0]
    pool = length // tok_rows
    n_ctx, n_dp = lax.axis_size("ctx"), lax.axis_size("dp")
    n_ring = n_dp // PAIR
    tokens = n_ctx * tok_rows
    width = channels // n_ctx
    span = channels // n_ring

    order = xor_order(n_ctx)
    place = {rel: at for at, rel in enumerate(order)}
    befores = [-1] + [place[c ^ (c - 1)] * tok_rows + tok_rows - 1 for c in range(1, n_ctx)]
    afters = [place[c ^ (c + 1)] * tok_rows for c in range(n_ctx - 1)] + [-1]
    ring = ring_of(n_ring)

    feat_v = held(feat)
    w_conv_v = held(w_conv)
    squares = [held(w) for w in (w_query, w_key, w_value, w_out)]

    edge = 16
    near, far = call(
        functools.partial(edge_kernel, half),
        "edges",
        (feat, feat, bases, dna_table),
        [pltpu.VMEM((half, channels), F32)] * 2,
        grid=(1,),
        in_specs=[
            pl.BlockSpec((edge, channels), lambda i: (0, 0)),
            pl.BlockSpec((edge, channels), lambda i: (length // edge - 1, 0)),
            pl.BlockSpec(memory_space=pltpu.SMEM),
            WHOLE,
        ],
    )
    near = swap(near, "ctx", 1)
    links = [(i, i + 1) for i in range(1, n_ctx - 1, 2)]
    far = lax.ppermute(far, "ctx", links + [(b, a) for a, b in links])

    block = 128
    taps, sums, slope, normed = call(
        functools.partial(act_kernel, kernel, pool, tok_rows),
        "activations",
        (feat_v, bases, dna_table, norm_gain),
        [
            pltpu.VMEM((kernel * tok_rows, channels), F32),
            pltpu.VMEM((tok_rows, channels), F32),
            pltpu.VMEM((length, channels), F32),
            pltpu.VMEM((length, channels), F32),
        ],
        [pltpu.VMEM((block, channels), BF16)] * 3,
    )
    pairs, *acts = call(
        functools.partial(taps_kernel, kernel, tok_rows, n_ctx),
        "taps",
        (taps, norm_gain, near, far),
        [pltpu.VMEM((kernel, 2 * tok_rows, channels), BF16)]
        + [pltpu.VMEM((tok_rows, kernel * width), BF16)] * n_ctx,
        [pltpu.VMEM((n_ctx, tok_rows, kernel * width), BF16)],
    )
    acts = [acts[0]] + [swap(acts[rel], "ctx", rel) for rel in order[1:]]
    rows = list(call(
        functools.partial(pool_kernel, pool),
        "pooled",
        (pairs, sums, w_conv_v, cot),
        [pltpu.VMEM((2, tok_rows, channels), BF16)],
    ))
    bit = n_ctx // 2
    while bit:
        rows = rows + [swap(value, "ctx", bit) for value in rows]
        bit //= 2

    act = call(
        pack_kernel, "pack", acts, [pltpu.VMEM((tokens, kernel * width), BF16)]
    )[0]

    g_all, *gts = call(
        functools.partial(attention_kernel, pool, n_ctx, ring),
        "attention",
        (*rows, *squares),
        [pltpu.VMEM((tokens, channels), BF16)] + [pltpu.VMEM((span, tokens), BF16)] * n_ring,
        [pltpu.VMEM((tokens, channels), BF16)] * 9 + [pltpu.VMEM((n_ring, span, tokens), BF16)],
    )

    def ring_perm(shift):
        pairs = []
        for r in range(n_ring):
            for x in range(PAIR):
                pairs.append((ring[r] * PAIR + x, ring[(r + shift) % n_ring] * PAIR + x))
        return pairs

    all_acts = [act]
    for _ in range(1, n_ring):
        all_acts.append(lax.ppermute(all_acts[-1], "dp", ring_perm(1)))
    all_gts = [gts[0]]
    for shift in range(1, n_ring):
        all_gts.append(lax.ppermute(gts[shift], "dp", ring_perm(shift)))

    padded = -(-(tok_rows + 2) // 8) * 8
    highs, lows, near_g = call(
        functools.partial(spread_kernel, kernel, tok_rows, befores, afters),
        "row_terms",
        (g_all, w_conv_v),
        [pltpu.VMEM((kernel * padded, channels), BF16)] * 2
        + [pltpu.VMEM((padded, channels), BF16)],
    )
    grid = length // block
    by_rows = pl.BlockSpec((block, channels), lambda i: (i, 0))
    grad_in = call(
        functools.partial(input_grad_kernel, kernel, pool),
        "input_grad",
        (highs, lows, near_g, slope, normed),
        [jax.ShapeDtypeStruct((length, channels), BF16)],
        grid=(grid,),
        out_specs=[by_rows],
    )[0]

    factor = 1.0 / (n_dp * length * n_ctx) ** 0.5
    narrow = span // PAIR
    mine, theirs = call(
        functools.partial(kernel_grad_kernel, factor, n_ring),
        "kernel_grad",
        (*all_acts, *all_gts),
        [
            pltpu.VMEM((narrow, kernel * width), F32),
            pltpu.VMEM((narrow, kernel * width), BF16),
        ],
        [pltpu.VMEM((PAIR, narrow, kernel * width), F32)],
    )
    other = swap(theirs, "dp", 1)
    grad_conv = call(
        functools.partial(join_kernel, kernel),
        "kernel_grad_join",
        (mine, other),
        [jax.ShapeDtypeStruct((kernel, width, narrow), F32)],
    )[0]
    return grad_in[None], jnp.transpose(grad_conv, (1, 0, 2))


def solution(mesh):
    in_specs = (
        P("dp", "ctx", None),
        P("dp", "ctx"),
        P(),
        P(),
        P(),
        P(),
        P(),
        P(),
        P(),
        P("dp", "ctx", None),
    )
    out_specs = (P("dp", "ctx", None), P("ctx", None, "dp"))
    return jax.shard_map(
        per_device, mesh=mesh, in_specs=in_specs, out_specs=out_specs, check_vma=False
    )
```

```python
import functools

import jax
import jax.numpy as jnp
from jax import lax
from jax.experimental import pallas as pl
from jax.experimental.pallas import tpu as pltpu
from jax.sharding import PartitionSpec as P


HEADS = 6
DH = 128

EPSILON = 1e-06
GELU_SCALE = 0.7978845608028654
CUBIC = 0.044715
F32 = jnp.float32
BF16 = jnp.bfloat16
VMEM_LIMIT = 20 << 20
GATHER = 4


def dot_nn(left, right):
    return lax.dot_general(left, right, (((1,), (0,)), ((), ())), preferred_element_type=F32)


def dot_nt(left, right):
    return lax.dot_general(left, right, (((1,), (1,)), ((), ())), preferred_element_type=F32)


def dot_tn(left, right):
    return lax.dot_general(left, right, (((0,), (0,)), ((), ())), preferred_element_type=F32)


def split2(value):
    high = value.astype(BF16)
    return high, (value - high.astype(F32)).astype(BF16)


def iota(shape, dim):
    return lax.broadcasted_iota(jnp.int32, shape, dim)


def normed_of(summed):
    inv_rms = lax.rsqrt(jnp.mean(summed * summed, axis=-1, keepdims=True) + EPSILON)
    return inv_rms, summed * inv_rms


def gelu_of(u):
    tanh_val = jnp.tanh(GELU_SCALE * (u + CUBIC * (u * u * u)))
    return tanh_val, 0.5 * u * (1.0 + tanh_val)


def pick(index, values):
    out = jnp.int32(values[0])
    for at, value in enumerate(values[1:], 1):
        out = jnp.where(index == at, jnp.int32(value), out)
    return out


def edge_kernel(half, feat, base, table, near, far, rows_buf, base_buf, table_buf, sems):
    length = feat.shape[0]
    edge = rows_buf.shape[1]
    copies = [
        pltpu.make_async_copy(feat.at[pl.ds(0, edge)], rows_buf.at[0], sems.at[0]),
        pltpu.make_async_copy(feat.at[pl.ds(length - edge, edge)], rows_buf.at[1], sems.at[1]),
        pltpu.make_async_copy(base, base_buf, sems.at[2]),
        pltpu.make_async_copy(table, table_buf, sems.at[3]),
    ]
    for copy in copies:
        copy.start()
    for copy in copies:
        copy.wait()
    odd = lax.axis_index("ctx") % 2 == 1
    table_f = table_buf[...].astype(F32)
    kinds = table_f.shape[0]

    def row(values, at, position):
        code = base_buf[:, position : position + 1]
        out = values[at : at + 1, :]
        for b in range(kinds):
            out = out + jnp.where(code == b, table_f[b : b + 1, :], 0.0)
        return out

    top, bottom = rows_buf[0].astype(F32), rows_buf[1].astype(F32)
    for i in range(half):
        first = row(top, i, i)
        last = row(bottom, edge - half + i, length - half + i)
        near[i : i + 1, :] = jnp.where(odd, first, last)
        far[i : i + 1, :] = jnp.where(odd, last, first)


def act_kernel(
    kernel, pool, tok_rows, feat, base, table, gain,
    taps, sums, slope_out, normed_out, act_buf, high_buf, low_buf,
):
    half = kernel // 2
    rows, channels = feat.shape
    block = act_buf.shape[0]
    gain_f = gain[...].reshape(1, channels).astype(F32)
    taps[...] = jnp.zeros_like(taps)
    sums[...] = jnp.zeros_like(sums)
    chunk = 32

    @pl.loop(0, rows // block)
    def _(step):
        start = pl.multiple_of(step * block, block)
        onehot = (iota((table.shape[0], block), 0) == base[:, pl.ds(start, block)]).astype(BF16)
        embed = dot_tn(onehot, table[...])
        for begin in range(0, block, chunk):
            part = slice(begin, begin + chunk)
            here = pl.ds(start + begin, chunk)
            summed = feat[here, :].astype(F32) + embed[part, :]
            inv_rms, normed = normed_of(summed)
            u = normed * gain_f
            tanh_val, value = gelu_of(u)
            slopes = 0.5 * (1.0 + tanh_val) + 0.5 * u * (1.0 - tanh_val * tanh_val) * GELU_SCALE * (
                1.0 + 3.0 * CUBIC * (u * u)
            )
            act_buf[part, :] = value.astype(BF16)
            high_buf[part, :], low_buf[part, :] = split2(summed)
            slope_out[here, :] = inv_rms * (slopes * gain_f)
            normed_out[here, :] = normed
        shape = (kernel * tok_rows, block)
        row = iota(shape, 0)
        tap = sum((row >= tok_rows * j).astype(jnp.int32) for j in range(1, kernel))
        token = row - tap * tok_rows
        offset = iota(shape, 1) + start - tap + half - token * pool
        spread = ((offset >= 0) & (offset < pool)).astype(BF16)
        taps[...] += dot_nn(spread, act_buf[...])
        plain = spread[half * tok_rows : (half + 1) * tok_rows, :]
        sums[...] += dot_nn(plain, high_buf[...]) + dot_nn(plain, low_buf[...])


def taps_kernel(kernel, tok_rows, blocks, taps, gain, near, far, pairs, *rest):
    outs, turn = rest[:blocks], rest[blocks]
    half = kernel // 2
    me = lax.axis_index("ctx")
    odd = me % 2 == 1
    channels = taps.shape[1]
    gain_f = gain[...].reshape(1, channels).astype(F32)
    edges = []
    for edge in (near, far):
        _, normed = normed_of(edge[...])
        edges.append(gelu_of(normed * gain_f)[1].astype(BF16).astype(F32))
    before = jnp.where(odd, edges[0], edges[1])
    after = jnp.where(odd, edges[1], edges[0])
    row = iota((tok_rows, channels), 0)
    highs = []
    for j in range(kernel):
        value = taps[j * tok_rows : (j + 1) * tok_rows, :]
        if j < half:
            extra = jnp.sum(before[j:, :], axis=0, keepdims=True)
            value = value + jnp.where(row == 0, extra, 0.0)
        if j > half:
            extra = jnp.sum(after[: j - half, :], axis=0, keepdims=True)
            value = value + jnp.where(row == tok_rows - 1, extra, 0.0)
        high, low = split2(value)
        highs.append(high)
        pairs[j] = jnp.concatenate([high, low], axis=0)
    width = channels // blocks
    for b in range(blocks):
        turn[b ^ me] = jnp.concatenate([h[:, b * width : (b + 1) * width] for h in highs], axis=1)
    for b in range(blocks):
        outs[b][...] = turn[b]


def pool_kernel(pool, pairs, sums, weights, cot, rows):
    tok_rows = sums.shape[0]
    total = dot_nn(pairs[0], weights[0])
    for j in range(1, pairs.shape[0]):
        total = total + dot_nn(pairs[j], weights[j])
    conv = total[:tok_rows] + total[tok_rows:]
    rows[0] = ((sums[...] + conv) * (1.0 / pool)).astype(BF16)
    rows[1] = cot[...]


def pack_kernel(*refs):
    *parts, out = refs
    at = 0
    for part in parts:
        out[at : at + part.shape[0], :] = part[...]
        at += part.shape[0]


def attention_kernel(pool, blocks, late, *refs):
    parts, refs = refs[:blocks], refs[blocks:]
    weights, refs = refs[:4], refs[4:]
    g_out, refs = refs[0], refs[1:]
    gts, refs = refs[:GATHER], refs[GATHER:]
    p_buf, c_buf, q_buf, k_buf, v_buf, ga_buf, gq_buf, gk_buf, gv_buf, turn = refs
    size = parts[0].shape[1]
    for at, part in enumerate(parts):
        p_buf[at * size : (at + 1) * size, :] = part[0]
        c_buf[at * size : (at + 1) * size, :] = part[1]
    for i, dst in enumerate((q_buf, k_buf, v_buf)):
        dst[...] = dot_nn(p_buf[...], weights[i][...]).astype(BF16)
    ga_buf[...] = dot_nt(c_buf[...], weights[3][...]).astype(BF16)
    scale = 1.0 / DH**0.5
    for h in range(HEADS):
        cols = slice(h * DH, (h + 1) * DH)
        q, k, v, ga = q_buf[:, cols], k_buf[:, cols], v_buf[:, cols], ga_buf[:, cols]
        scores = dot_nt(q, k) * scale
        expo = jnp.exp(scores - jnp.max(scores, axis=-1, keepdims=True))
        probs = expo / jnp.sum(expo, axis=-1, keepdims=True)
        probs_b = probs.astype(BF16)
        out = dot_nn(probs_b, v).astype(BF16)
        delta = jnp.sum(ga.astype(F32) * out.astype(F32), axis=-1, keepdims=True)
        grad_score = (probs * (dot_nt(ga, v) - delta) * scale).astype(BF16)
        gq_buf[:, cols] = dot_nn(grad_score, k).astype(BF16)
        gk_buf[:, cols] = dot_tn(grad_score, q).astype(BF16)
        gv_buf[:, cols] = dot_tn(probs_b, ga).astype(BF16)
    grad = c_buf[...].astype(F32)
    for i, src in enumerate((gq_buf, gk_buf, gv_buf)):
        grad = grad + dot_nt(src[...], weights[i][...])
    g = (grad * (1.0 / pool)).astype(BF16)
    g_out[...] = g
    tokens = g.shape[0]
    eye = (iota((tokens, tokens), 0) == iota((tokens, tokens), 1)).astype(BF16)
    turned = dot_tn(g, eye).astype(BF16)
    count = turn.shape[0]
    span = turned.shape[0] // count
    me = lax.axis_index("dp")
    for o in range(count):
        turn[o ^ me] = turned[o * span : (o + 1) * span, :]
    for r in range(GATHER):
        for at, rel in enumerate(late):
            gts[r][at * span : (at + 1) * span, :] = turn[r ^ rel]


def spread_kernel(kernel, tok_rows, befores, afters, g_ref, weights, highs, lows, near):
    tokens = g_ref.shape[0]
    padded = near.shape[0]
    me = lax.axis_index("ctx")
    row = iota((padded, tokens), 0)
    source = jnp.where(
        row == 0, pick(me, befores), jnp.where(row == tok_rows + 1, pick(me, afters), row - 1)
    )
    source = jnp.where(row > tok_rows + 1, -1, source)
    chosen = (source == iota((padded, tokens), 1)).astype(BF16)
    rows = dot_nn(chosen, g_ref[...]).astype(BF16)
    near[...] = rows
    for j in range(kernel):
        part = slice(j * padded, (j + 1) * padded)
        highs[part, :], lows[part, :] = split2(dot_nt(rows, weights[j]))


def input_grad_kernel(kernel, pool, highs, lows, near, slope, normed, out):
    half = kernel // 2
    rows = out.shape[0]
    padded = near.shape[0]
    start = pl.program_id(0) * rows
    here = pl.ds(pl.multiple_of(start, rows), rows)
    shape = (rows, kernel * padded)
    col = iota(shape, 1)
    tap = sum((col >= padded * j).astype(jnp.int32) for j in range(1, kernel))
    token = col - tap * padded - 1
    offset = iota(shape, 0) + start - tap + half - token * pool
    spread = ((offset >= 0) & (offset < pool)).astype(BF16)
    grad_act = dot_nn(spread, highs[...]) + dot_nn(spread, lows[...])
    plain = spread[:, half * padded : (half + 1) * padded]
    grad_rows = dot_nn(plain, near[...])
    scaled = grad_act * slope[here, :]
    unit = normed[here, :]
    mean = jnp.mean(scaled * unit, axis=-1, keepdims=True)
    out[...] = (grad_rows + scaled - unit * mean).astype(BF16)


def kernel_grad_kernel(factor, *refs):
    acts, gts, (mine, theirs) = refs[:GATHER], refs[GATHER : 2 * GATHER], refs[2 * GATHER :]
    total = None
    for act, gt in zip(acts, gts):
        term = dot_nn(gt[...], act[...])
        total = term if total is None else total + term
    total = total * factor
    span = mine.shape[0]
    mine[...] = total[:span, :]
    theirs[...] = total[span:, :].astype(BF16)


def fold_kernel(mine, other, kept, sent):
    span = kept.shape[0]
    kept[...] = mine[:span, :] + other[:span, :].astype(F32)
    sent[...] = (mine[span:, :] + other[span:, :].astype(F32)).astype(BF16)


def join_kernel(kernel, mine, other, out):
    width = out.shape[1]
    total = jnp.transpose(mine[...] + other[...].astype(F32))
    for j in range(kernel):
        out[j] = total[j * width : (j + 1) * width, :]


def xor_order(count):
    order = [0]
    bit = count // 2
    while bit:
        order = order + [v ^ bit for v in order]
        bit //= 2
    return order


def swap(value, axis, bit):
    count = lax.axis_size(axis)
    return lax.ppermute(value, axis, [(i, i ^ bit) for i in range(count)])


WHOLE = pl.BlockSpec(memory_space=pltpu.VMEM)


def call(body, args, outs, scratch=(), **options):
    options.setdefault("in_specs", [WHOLE] * len(args))
    options.setdefault("out_specs", [WHOLE] * len(outs))
    return pl.pallas_call(
        body,
        out_shape=list(outs),
        scratch_shapes=list(scratch),
        compiler_params=pltpu.CompilerParams(vmem_limit_bytes=VMEM_LIMIT),
        **options,
    )(*args)


def held(value):
    return pltpu.with_memory_space_constraint(value, pltpu.VMEM)


def per_device(
    features, bases, dna_table, norm_gain, w_conv, w_query, w_key, w_value, w_out, cotangent
):
    feat, cot = features[0], cotangent[0]
    kernel = w_conv.shape[0]
    half = kernel // 2
    length, channels = feat.shape
    tok_rows = cot.shape[0]
    pool = length // tok_rows
    n_ctx, n_dp = lax.axis_size("ctx"), lax.axis_size("dp")
    tokens = n_ctx * tok_rows
    width = channels // n_ctx
    narrow = channels // n_dp
    late = list(range(0, n_dp, GATHER))

    order = xor_order(n_ctx)
    place = {rel: at for at, rel in enumerate(order)}
    befores = [-1] + [place[c ^ (c - 1)] * tok_rows + tok_rows - 1 for c in range(1, n_ctx)]
    afters = [place[c ^ (c + 1)] * tok_rows for c in range(n_ctx - 1)] + [-1]

    feat_v = held(feat)
    w_conv_v = held(w_conv)
    squares = [held(w) for w in (w_query, w_key, w_value, w_out)]

    edge = 16
    hbm = pl.BlockSpec(memory_space=pltpu.HBM)
    near, far = call(
        functools.partial(edge_kernel, half),
        (feat, bases, dna_table),
        [pltpu.VMEM((half, channels), F32)] * 2,
        [
            pltpu.VMEM((2, edge, channels), BF16),
            pltpu.VMEM(bases.shape, jnp.int32),
            pltpu.VMEM(dna_table.shape, BF16),
            pltpu.SemaphoreType.DMA((4,)),
        ],
        in_specs=[hbm] * 3,
    )
    near = swap(near, "ctx", 1)
    links = [(i, i + 1) for i in range(1, n_ctx - 1, 2)]
    far = lax.ppermute(far, "ctx", links + [(b, a) for a, b in links])

    block = 128
    taps, sums, slope, normed = call(
        functools.partial(act_kernel, kernel, pool, tok_rows),
        (feat_v, bases, dna_table, norm_gain),
        [
            pltpu.VMEM((kernel * tok_rows, channels), F32),
            pltpu.VMEM((tok_rows, channels), F32),
            pltpu.VMEM((length, channels), F32),
            pltpu.VMEM((length, channels), F32),
        ],
        [pltpu.VMEM((block, channels), BF16)] * 3,
    )
    pairs, *acts = call(
        functools.partial(taps_kernel, kernel, tok_rows, n_ctx),
        (taps, norm_gain, near, far),
        [pltpu.VMEM((kernel, 2 * tok_rows, channels), BF16)]
        + [pltpu.VMEM((tok_rows, kernel * width), BF16)] * n_ctx,
        [pltpu.VMEM((n_ctx, tok_rows, kernel * width), BF16)],
    )
    acts = [acts[0]] + [swap(acts[rel], "ctx", rel) for rel in order[1:]]
    rows = list(
        call(
            functools.partial(pool_kernel, pool),
            (pairs, sums, w_conv_v, cot),
            [pltpu.VMEM((2, tok_rows, channels), BF16)],
        )
    )
    bit = n_ctx // 2
    while bit:
        rows = rows + [swap(value, "ctx", bit) for value in rows]
        bit //= 2

    act = call(pack_kernel, acts, [pltpu.VMEM((tokens, kernel * width), BF16)])[0]

    act_z = swap(act, "dp", 2)
    act_x = swap(act, "dp", 1)

    g_all, *gts = call(
        functools.partial(attention_kernel, pool, n_ctx, late),
        (*rows, *squares),
        [pltpu.VMEM((tokens, channels), BF16)]
        + [pltpu.VMEM((len(late) * narrow, tokens), BF16)] * GATHER,
        [pltpu.VMEM((tokens, channels), BF16)] * 9 + [pltpu.VMEM((n_dp, narrow, tokens), BF16)],
    )

    act_zx = swap(act_z, "dp", 1)
    gts = [gts[0]] + [swap(gts[rel], "dp", rel) for rel in range(1, GATHER)]

    padded = -(-(tok_rows + 2) // 8) * 8
    highs, lows, near_g = call(
        functools.partial(spread_kernel, kernel, tok_rows, befores, afters),
        (g_all, w_conv_v),
        [pltpu.VMEM((kernel * padded, channels), BF16)] * 2
        + [pltpu.VMEM((padded, channels), BF16)],
    )
    factor = 1.0 / (n_dp * length * n_ctx) ** 0.5
    kept = len(late) // 2
    mine, theirs = call(
        functools.partial(kernel_grad_kernel, factor),
        (act, act_x, act_z, act_zx, *gts),
        [
            pltpu.VMEM((kept * narrow, kernel * width), F32),
            pltpu.VMEM((kept * narrow, kernel * width), BF16),
        ],
    )
    other = swap(theirs, "dp", GATHER * kept)
    while kept > 1:
        kept //= 2
        mine, theirs = call(
            fold_kernel,
            (mine, other),
            [
                pltpu.VMEM((kept * narrow, kernel * width), F32),
                pltpu.VMEM((kept * narrow, kernel * width), BF16),
            ],
        )
        other = swap(theirs, "dp", GATHER * kept)

    by_rows = pl.BlockSpec((block, channels), lambda i: (i, 0))
    grad_in = call(
        functools.partial(input_grad_kernel, kernel, pool),
        (highs, lows, near_g, slope, normed),
        [jax.ShapeDtypeStruct((length, channels), BF16)],
        grid=(length // block,),
        out_specs=[by_rows],
    )[0]
    grad_conv = call(
        functools.partial(join_kernel, kernel),
        (mine, other),
        [jax.ShapeDtypeStruct((kernel, width, narrow), F32)],
    )[0]
    return grad_in[None], jnp.transpose(grad_conv, (1, 0, 2))


def solution(mesh):
    in_specs = (
        P("dp", "ctx", None),
        P("dp", "ctx"),
        P(),
        P(),
        P(),
        P(),
        P(),
        P(),
        P(),
        P("dp", "ctx", None),
    )
    out_specs = (P("dp", "ctx", None), P("ctx", None, "dp"))
    return jax.shard_map(
        per_device, mesh=mesh, in_specs=in_specs, out_specs=out_specs, check_vma=False
    )
```

```python
import functools

import jax
import jax.numpy as jnp
from jax import lax
from jax.experimental import pallas as pl
from jax.experimental.pallas import tpu as pltpu
from jax.sharding import PartitionSpec as P


HEADS = 6
DH = 128

EPSILON = 1e-06
GELU_SCALE = 0.7978845608028654
CUBIC = 0.044715
F32 = jnp.float32
BF16 = jnp.bfloat16
VMEM_LIMIT = 20 << 20
X_BIT, Z_BIT = 1, 4


def dot_nn(left, right):
    return lax.dot_general(left, right, (((1,), (0,)), ((), ())), preferred_element_type=F32)


def dot_nt(left, right):
    return lax.dot_general(left, right, (((1,), (1,)), ((), ())), preferred_element_type=F32)


def dot_tn(left, right):
    return lax.dot_general(left, right, (((0,), (0,)), ((), ())), preferred_element_type=F32)


def split2(value):
    high = value.astype(BF16)
    return high, (value - high.astype(F32)).astype(BF16)


def iota(shape, dim):
    return lax.broadcasted_iota(jnp.int32, shape, dim)


def normed_of(summed):
    inv_rms = lax.rsqrt(jnp.mean(summed * summed, axis=-1, keepdims=True) + EPSILON)
    return inv_rms, summed * inv_rms


def gelu_of(u):
    tanh_val = jnp.tanh(GELU_SCALE * (u + CUBIC * (u * u * u)))
    return tanh_val, 0.5 * u * (1.0 + tanh_val)


def pick(index, values):
    out = jnp.int32(values[0])
    for at, value in enumerate(values[1:], 1):
        out = jnp.where(index == at, jnp.int32(value), out)
    return out


def start_copies(pairs, sems):
    copies = [pltpu.make_async_copy(src, dst, sems.at[i]) for i, (src, dst) in enumerate(pairs)]
    for copy in copies:
        copy.start()
    return copies


def edge_kernel(
    half, feat, base, table, gain, near, far, feat_buf, base_buf, table_buf, gain_buf, rows_buf, sems
):
    length = feat.shape[0]
    edge = rows_buf.shape[1]
    copies = [
        pltpu.make_async_copy(feat.at[pl.ds(0, edge)], rows_buf.at[0], sems.at[0]),
        pltpu.make_async_copy(feat.at[pl.ds(length - edge, edge)], rows_buf.at[1], sems.at[1]),
        pltpu.make_async_copy(base, base_buf, sems.at[2]),
        pltpu.make_async_copy(table, table_buf, sems.at[3]),
        pltpu.make_async_copy(gain, gain_buf, sems.at[4]),
        pltpu.make_async_copy(feat, feat_buf, sems.at[5]),
    ]
    for copy in copies:
        copy.start()
    for copy in copies[:4]:
        copy.wait()
    odd = lax.axis_index("ctx") % 2 == 1
    table_f = table_buf[...].astype(F32)
    kinds = table_f.shape[0]

    def row(values, at, position):
        code = base_buf[:, position : position + 1]
        out = values[at : at + 1, :]
        for b in range(kinds):
            out = out + jnp.where(code == b, table_f[b : b + 1, :], 0.0)
        return out

    top, bottom = rows_buf[0].astype(F32), rows_buf[1].astype(F32)
    for i in range(half):
        first = row(top, i, i)
        last = row(bottom, edge - half + i, length - half + i)
        near[i : i + 1, :] = jnp.where(odd, first, last)
        far[i : i + 1, :] = jnp.where(odd, last, first)
    for copy in copies[4:]:
        copy.wait()


def act_kernel(
    kernel, pool, tok_rows, feat, base, table, gain, w_a, w_b, w_c,
    taps, sums, slope_out, normed_out, v_a, v_b, v_c, act_buf, high_buf, low_buf, sems,
):
    copies = start_copies(((w_a, v_a), (w_b, v_b), (w_c, v_c)), sems)
    half = kernel // 2
    rows, channels = feat.shape
    block = act_buf.shape[0]
    gain_f = gain[...].reshape(1, channels).astype(F32)
    taps[...] = jnp.zeros_like(taps)
    sums[...] = jnp.zeros_like(sums)
    chunk = 32

    @pl.loop(0, rows // block)
    def _(step):
        start = pl.multiple_of(step * block, block)
        onehot = (iota((table.shape[0], block), 0) == base[:, pl.ds(start, block)]).astype(BF16)
        embed = dot_tn(onehot, table[...])
        for begin in range(0, block, chunk):
            part = slice(begin, begin + chunk)
            here = pl.ds(start + begin, chunk)
            summed = feat[here, :].astype(F32) + embed[part, :]
            inv_rms, normed = normed_of(summed)
            u = normed * gain_f
            tanh_val, value = gelu_of(u)
            slopes = 0.5 * (1.0 + tanh_val) + 0.5 * u * (1.0 - tanh_val * tanh_val) * GELU_SCALE * (
                1.0 + 3.0 * CUBIC * (u * u)
            )
            act_buf[part, :] = value.astype(BF16)
            high_buf[part, :], low_buf[part, :] = split2(summed)
            slope_out[here, :] = inv_rms * (slopes * gain_f)
            normed_out[here, :] = normed
        shape = (kernel * tok_rows, block)
        row = iota(shape, 0)
        tap = sum((row >= tok_rows * j).astype(jnp.int32) for j in range(1, kernel))
        token = row - tap * tok_rows
        offset = iota(shape, 1) + start - tap + half - token * pool
        spread = ((offset >= 0) & (offset < pool)).astype(BF16)
        taps[...] += dot_nn(spread, act_buf[...])
        plain = spread[half * tok_rows : (half + 1) * tok_rows, :]
        sums[...] += dot_nn(plain, high_buf[...]) + dot_nn(plain, low_buf[...])

    for copy in copies:
        copy.wait()


def taps_kernel(kernel, tok_rows, blocks, taps, gain, near, far, pairs, *rest):
    outs, turn = rest[:blocks], rest[blocks]
    half = kernel // 2
    me = lax.axis_index("ctx")
    odd = me % 2 == 1
    channels = taps.shape[1]
    gain_f = gain[...].reshape(1, channels).astype(F32)
    edges = []
    for edge in (near, far):
        _, normed = normed_of(edge[...])
        edges.append(gelu_of(normed * gain_f)[1].astype(BF16).astype(F32))
    before = jnp.where(odd, edges[0], edges[1])
    after = jnp.where(odd, edges[1], edges[0])
    row = iota((tok_rows, channels), 0)
    highs = []
    for j in range(kernel):
        value = taps[j * tok_rows : (j + 1) * tok_rows, :]
        if j < half:
            extra = jnp.sum(before[j:, :], axis=0, keepdims=True)
            value = value + jnp.where(row == 0, extra, 0.0)
        if j > half:
            extra = jnp.sum(after[: j - half, :], axis=0, keepdims=True)
            value = value + jnp.where(row == tok_rows - 1, extra, 0.0)
        high, low = split2(value)
        highs.append(high)
        pairs[j] = jnp.concatenate([high, low], axis=0)
    width = channels // blocks
    for b in range(blocks):
        turn[b ^ me] = jnp.concatenate([h[:, b * width : (b + 1) * width] for h in highs], axis=1)
    for b in range(blocks):
        outs[b][...] = turn[b]


def pool_kernel(pool, pairs, sums, weights, cot, w_a, w_b, rows, v_a, v_b, sems):
    copies = start_copies(((w_a, v_a), (w_b, v_b), (cot, rows.at[1])), sems)
    tok_rows = sums.shape[0]
    total = dot_nn(pairs[0], weights[0])
    for j in range(1, pairs.shape[0]):
        total = total + dot_nn(pairs[j], weights[j])
    conv = total[:tok_rows] + total[tok_rows:]
    rows[0] = ((sums[...] + conv) * (1.0 / pool)).astype(BF16)
    for copy in copies:
        copy.wait()


def pack_kernel(*refs):
    *parts, out = refs
    at = 0
    for part in parts:
        out[at : at + part.shape[0], :] = part[...]
        at += part.shape[0]


def attention_kernel(pool, blocks, near_rels, late, *refs):
    parts, refs = refs[:blocks], refs[blocks:]
    weights, refs = refs[:4], refs[4:]
    g_out, refs = refs[0], refs[1:]
    gts, refs = refs[: len(near_rels)], refs[len(near_rels) :]
    p_buf, c_buf, q_buf, k_buf, v_buf, ga_buf, gq_buf, gk_buf, gv_buf, turn = refs
    size = parts[0].shape[1]
    for at, part in enumerate(parts):
        p_buf[at * size : (at + 1) * size, :] = part[0]
        c_buf[at * size : (at + 1) * size, :] = part[1]
    for i, dst in enumerate((q_buf, k_buf, v_buf)):
        dst[...] = dot_nn(p_buf[...], weights[i][...]).astype(BF16)
    ga_buf[...] = dot_nt(c_buf[...], weights[3][...]).astype(BF16)
    scale = 1.0 / DH**0.5
    for h in range(HEADS):
        cols = slice(h * DH, (h + 1) * DH)
        q, k, v, ga = q_buf[:, cols], k_buf[:, cols], v_buf[:, cols], ga_buf[:, cols]
        scores = dot_nt(q, k) * scale
        expo = jnp.exp(scores - jnp.max(scores, axis=-1, keepdims=True))
        probs = expo / jnp.sum(expo, axis=-1, keepdims=True)
        probs_b = probs.astype(BF16)
        out = dot_nn(probs_b, v).astype(BF16)
        delta = jnp.sum(ga.astype(F32) * out.astype(F32), axis=-1, keepdims=True)
        grad_score = (probs * (dot_nt(ga, v) - delta) * scale).astype(BF16)
        gq_buf[:, cols] = dot_nn(grad_score, k).astype(BF16)
        gk_buf[:, cols] = dot_tn(grad_score, q).astype(BF16)
        gv_buf[:, cols] = dot_tn(probs_b, ga).astype(BF16)
    grad = c_buf[...].astype(F32)
    for i, src in enumerate((gq_buf, gk_buf, gv_buf)):
        grad = grad + dot_nt(src[...], weights[i][...])
    g = (grad * (1.0 / pool)).astype(BF16)
    g_out[...] = g
    tokens = g.shape[0]
    eye = (iota((tokens, tokens), 0) == iota((tokens, tokens), 1)).astype(BF16)
    turned = dot_tn(g, eye).astype(BF16)
    count = turn.shape[0]
    span = turned.shape[0] // count
    me = lax.axis_index("dp")
    for o in range(count):
        turn[o ^ me] = turned[o * span : (o + 1) * span, :]
    for gt, base in zip(gts, near_rels):
        for at, rel in enumerate(late):
            gt[at * span : (at + 1) * span, :] = turn[base ^ rel]


def spread_kernel(kernel, tok_rows, befores, afters, g_ref, weights, highs, lows, near):
    tokens = g_ref.shape[0]
    padded = near.shape[0]
    me = lax.axis_index("ctx")
    row = iota((padded, tokens), 0)
    source = jnp.where(
        row == 0, pick(me, befores), jnp.where(row == tok_rows + 1, pick(me, afters), row - 1)
    )
    source = jnp.where(row > tok_rows + 1, -1, source)
    chosen = (source == iota((padded, tokens), 1)).astype(BF16)
    rows = dot_nn(chosen, g_ref[...]).astype(BF16)
    near[...] = rows
    for j in range(kernel):
        part = slice(j * padded, (j + 1) * padded)
        highs[part, :], lows[part, :] = split2(dot_nt(rows, weights[j]))


def input_grad_kernel(kernel, pool, highs, lows, near, slope, normed, out):
    half = kernel // 2
    rows = out.shape[0]
    padded = near.shape[0]
    start = pl.program_id(0) * rows
    here = pl.ds(pl.multiple_of(start, rows), rows)
    shape = (rows, kernel * padded)
    col = iota(shape, 1)
    tap = sum((col >= padded * j).astype(jnp.int32) for j in range(1, kernel))
    token = col - tap * padded - 1
    offset = iota(shape, 0) + start - tap + half - token * pool
    spread = ((offset >= 0) & (offset < pool)).astype(BF16)
    grad_act = dot_nn(spread, highs[...]) + dot_nn(spread, lows[...])
    plain = spread[:, half * padded : (half + 1) * padded]
    grad_rows = dot_nn(plain, near[...])
    scaled = grad_act * slope[here, :]
    unit = normed[here, :]
    mean = jnp.mean(scaled * unit, axis=-1, keepdims=True)
    out[...] = (grad_rows + scaled - unit * mean).astype(BF16)


def kernel_grad_kernel(factor, *refs):
    count = len(refs) // 2 - 1
    acts, gts, (mine, theirs) = refs[:count], refs[count : 2 * count], refs[2 * count :]
    total = None
    for act, gt in zip(acts, gts):
        term = dot_nn(gt[...], act[...])
        total = term if total is None else total + term
    total = total * factor
    span = mine.shape[0]
    mine[...] = total[:span, :]
    theirs[...] = total[span:, :].astype(BF16)


def fold_kernel(mine, other, kept, sent):
    span = kept.shape[0]
    kept[...] = mine[:span, :] + other[:span, :].astype(F32)
    sent[...] = (mine[span:, :] + other[span:, :].astype(F32)).astype(BF16)


def join_kernel(kernel, mine, other, out):
    width = out.shape[1]
    total = jnp.transpose(mine[...] + other[...].astype(F32))
    for j in range(kernel):
        out[j] = total[j * width : (j + 1) * width, :]


def xor_order(count):
    order = [0]
    bit = count // 2
    while bit:
        order = order + [v ^ bit for v in order]
        bit //= 2
    return order


def swap(value, axis, bit):
    count = lax.axis_size(axis)
    return lax.ppermute(value, axis, [(i, i ^ bit) for i in range(count)])


WHOLE = pl.BlockSpec(memory_space=pltpu.VMEM)


def call(body, args, outs, scratch=(), **options):
    options.setdefault("in_specs", [WHOLE] * len(args))
    options.setdefault("out_specs", [WHOLE] * len(outs))
    return pl.pallas_call(
        body,
        out_shape=list(outs),
        scratch_shapes=list(scratch),
        compiler_params=pltpu.CompilerParams(vmem_limit_bytes=VMEM_LIMIT),
        **options,
    )(*args)


def outside(*values):
    return [pltpu.with_memory_space_constraint(value, pltpu.HBM) for value in values]


def bits_of(count):
    return [1 << at for at in range(count.bit_length() - 1)]


def sums_of(bits):
    out = [0]
    for bit in bits:
        out = out + [bit + value for value in out]
    return out


def per_device(
    features, bases, dna_table, norm_gain, w_conv, w_query, w_key, w_value, w_out, cotangent
):
    feat, cot = features[0], cotangent[0]
    kernel = w_conv.shape[0]
    half = kernel // 2
    length, channels = feat.shape
    tok_rows = cot.shape[0]
    pool = length // tok_rows
    n_ctx, n_dp = lax.axis_size("ctx"), lax.axis_size("dp")
    tokens = n_ctx * tok_rows
    width = channels // n_ctx
    narrow = channels // n_dp
    near_rels = [0, X_BIT, Z_BIT, X_BIT + Z_BIT]
    late = sums_of([bit for bit in bits_of(n_dp) if bit not in (X_BIT, Z_BIT)])

    order = xor_order(n_ctx)
    place = {rel: at for at, rel in enumerate(order)}
    befores = [-1] + [place[c ^ (c - 1)] * tok_rows + tok_rows - 1 for c in range(1, n_ctx)]
    afters = [place[c ^ (c + 1)] * tok_rows for c in range(n_ctx - 1)] + [-1]

    edge = 16
    hbm = pl.BlockSpec(memory_space=pltpu.HBM)
    near, far, feat_v, base_v, table_v, gain_v = call(
        functools.partial(edge_kernel, half),
        outside(feat, bases, dna_table, norm_gain),
        [pltpu.VMEM((half, channels), F32)] * 2
        + [pltpu.VMEM(value.shape, value.dtype) for value in (feat, bases, dna_table, norm_gain)],
        [pltpu.VMEM((2, edge, channels), BF16), pltpu.SemaphoreType.DMA((6,))],
        in_specs=[hbm] * 4,
    )
    near = swap(near, "ctx", 1)
    links = [(i, i + 1) for i in range(1, n_ctx - 1, 2)]
    far = lax.ppermute(far, "ctx", links + [(b, a) for a, b in links])

    block = 128
    taps, sums, slope, normed, w_conv_v, w_query_v, w_key_v = call(
        functools.partial(act_kernel, kernel, pool, tok_rows),
        [feat_v, base_v, table_v, gain_v] + outside(w_conv, w_query, w_key),
        [
            pltpu.VMEM((kernel * tok_rows, channels), F32),
            pltpu.VMEM((tok_rows, channels), F32),
            pltpu.VMEM((length, channels), F32),
            pltpu.VMEM((length, channels), F32),
        ]
        + [pltpu.VMEM(value.shape, BF16) for value in (w_conv, w_query, w_key)],
        [pltpu.VMEM((block, channels), BF16)] * 3 + [pltpu.SemaphoreType.DMA((3,))],
        in_specs=[WHOLE] * 4 + [hbm] * 3,
    )
    pairs, *acts = call(
        functools.partial(taps_kernel, kernel, tok_rows, n_ctx),
        (taps, gain_v, near, far),
        [pltpu.VMEM((kernel, 2 * tok_rows, channels), BF16)]
        + [pltpu.VMEM((tok_rows, kernel * width), BF16)] * n_ctx,
        [pltpu.VMEM((n_ctx, tok_rows, kernel * width), BF16)],
    )
    acts = [acts[0]] + [swap(acts[rel], "ctx", rel) for rel in order[1:]]
    pooled, w_value_v, w_out_v = call(
        functools.partial(pool_kernel, pool),
        [pairs, sums, w_conv_v] + outside(cot, w_value, w_out),
        [pltpu.VMEM((2, tok_rows, channels), BF16)]
        + [pltpu.VMEM(value.shape, BF16) for value in (w_value, w_out)],
        [pltpu.SemaphoreType.DMA((3,))],
        in_specs=[WHOLE] * 3 + [hbm] * 3,
    )
    rows = [pooled]
    bit = n_ctx // 2
    while bit:
        rows = rows + [swap(value, "ctx", bit) for value in rows]
        bit //= 2

    act = call(pack_kernel, acts, [pltpu.VMEM((tokens, kernel * width), BF16)])[0]

    act_z = swap(act, "dp", Z_BIT)
    act_x = swap(act, "dp", X_BIT)

    g_all, *gts = call(
        functools.partial(attention_kernel, pool, n_ctx, near_rels, late),
        (*rows, w_query_v, w_key_v, w_value_v, w_out_v),
        [pltpu.VMEM((tokens, channels), BF16)]
        + [pltpu.VMEM((len(late) * narrow, tokens), BF16)] * len(near_rels),
        [pltpu.VMEM((tokens, channels), BF16)] * 9 + [pltpu.VMEM((n_dp, narrow, tokens), BF16)],
    )

    act_zx = swap(act_z, "dp", X_BIT)
    swapped = [gts[0]]
    for at, rel in enumerate(near_rels[1:], 1):
        swapped.append(swap(gts[at], "dp", rel))

    padded = -(-(tok_rows + 2) // 8) * 8
    highs, lows, near_g = call(
        functools.partial(spread_kernel, kernel, tok_rows, befores, afters),
        (g_all, w_conv_v),
        [pltpu.VMEM((kernel * padded, channels), BF16)] * 2
        + [pltpu.VMEM((padded, channels), BF16)],
    )
    factor = 1.0 / (n_dp * length * n_ctx) ** 0.5
    kept = len(late) // 2
    mine, theirs = call(
        functools.partial(kernel_grad_kernel, factor),
        (act, act_x, act_z, act_zx, *swapped),
        [
            pltpu.VMEM((kept * narrow, kernel * width), F32),
            pltpu.VMEM((kept * narrow, kernel * width), BF16),
        ],
    )
    other = swap(theirs, "dp", late[kept])
    while kept > 1:
        kept //= 2
        mine, theirs = call(
            fold_kernel,
            (mine, other),
            [
                pltpu.VMEM((kept * narrow, kernel * width), F32),
                pltpu.VMEM((kept * narrow, kernel * width), BF16),
            ],
        )
        other = swap(theirs, "dp", late[kept])

    by_rows = pl.BlockSpec((block, channels), lambda i: (i, 0))
    grad_in = call(
        functools.partial(input_grad_kernel, kernel, pool),
        (highs, lows, near_g, slope, normed),
        [jax.ShapeDtypeStruct((length, channels), BF16)],
        grid=(length // block,),
        out_specs=[by_rows],
    )[0]
    grad_conv = call(
        functools.partial(join_kernel, kernel),
        (mine, other),
        [jax.ShapeDtypeStruct((kernel, width, narrow), F32)],
    )[0]
    return grad_in[None], jnp.transpose(grad_conv, (1, 0, 2))


def solution(mesh):
    in_specs = (
        P("dp", "ctx", None),
        P("dp", "ctx"),
        P(),
        P(),
        P(),
        P(),
        P(),
        P(),
        P(),
        P("dp", "ctx", None),
    )
    out_specs = (P("dp", "ctx", None), P("ctx", None, "dp"))
    return jax.shard_map(
        per_device, mesh=mesh, in_specs=in_specs, out_specs=out_specs, check_vma=False
    )
```

```python
import functools

import jax
import jax.numpy as jnp
from jax import lax
from jax.experimental import pallas as pl
from jax.experimental.pallas import tpu as pltpu
from jax.sharding import PartitionSpec as P


HEADS = 6
DH = 128

EPSILON = 1e-06
GELU_SCALE = 0.7978845608028654
CUBIC = 0.044715
F32 = jnp.float32
BF16 = jnp.bfloat16
VMEM_LIMIT = 20 << 20
X_BIT, Z_BIT = 1, 4


def dot_nn(left, right):
    return lax.dot_general(left, right, (((1,), (0,)), ((), ())), preferred_element_type=F32)


def dot_nt(left, right):
    return lax.dot_general(left, right, (((1,), (1,)), ((), ())), preferred_element_type=F32)


def dot_tn(left, right):
    return lax.dot_general(left, right, (((0,), (0,)), ((), ())), preferred_element_type=F32)


def split2(value):
    high = value.astype(BF16)
    return high, (value - high.astype(F32)).astype(BF16)


def iota(shape, dim):
    return lax.broadcasted_iota(jnp.int32, shape, dim)


def normed_of(summed):
    inv_rms = lax.rsqrt(jnp.mean(summed * summed, axis=-1, keepdims=True) + EPSILON)
    return inv_rms, summed * inv_rms


def gelu_of(u):
    tanh_val = jnp.tanh(GELU_SCALE * (u + CUBIC * (u * u * u)))
    return tanh_val, 0.5 * u * (1.0 + tanh_val)


def pick(index, values):
    out = jnp.int32(values[0])
    for at, value in enumerate(values[1:], 1):
        out = jnp.where(index == at, jnp.int32(value), out)
    return out


def start_copies(pairs, sems):
    copies = [pltpu.make_async_copy(src, dst, sems.at[i]) for i, (src, dst) in enumerate(pairs)]
    for copy in copies:
        copy.start()
    return copies


def edge_kernel(
    half, feat, base, table, gain, near, far, feat_buf, base_buf, table_buf, gain_buf, rows_buf, sems
):
    length = feat.shape[0]
    edge = rows_buf.shape[1]
    copies = [
        pltpu.make_async_copy(feat.at[pl.ds(0, edge)], rows_buf.at[0], sems.at[0]),
        pltpu.make_async_copy(feat.at[pl.ds(length - edge, edge)], rows_buf.at[1], sems.at[1]),
        pltpu.make_async_copy(base, base_buf, sems.at[2]),
        pltpu.make_async_copy(table, table_buf, sems.at[3]),
        pltpu.make_async_copy(gain, gain_buf, sems.at[4]),
        pltpu.make_async_copy(feat, feat_buf, sems.at[5]),
    ]
    for copy in copies:
        copy.start()
    for copy in copies[:4]:
        copy.wait()
    odd = lax.axis_index("ctx") % 2 == 1
    table_f = table_buf[...].astype(F32)
    kinds = table_f.shape[0]

    def row(values, at, position):
        code = base_buf[:, position : position + 1]
        out = values[at : at + 1, :]
        for b in range(kinds):
            out = out + jnp.where(code == b, table_f[b : b + 1, :], 0.0)
        return out

    top, bottom = rows_buf[0].astype(F32), rows_buf[1].astype(F32)
    for i in range(half):
        first = row(top, i, i)
        last = row(bottom, edge - half + i, length - half + i)
        near[i : i + 1, :] = jnp.where(odd, first, last)
        far[i : i + 1, :] = jnp.where(odd, last, first)
    for copy in copies[4:]:
        copy.wait()


def act_kernel(
    kernel, pool, tok_rows, feat, base, table, gain, w_hbm,
    taps, sums, tanh_out, normed_out, inv_out, weights, act_buf, high_buf, low_buf, sems,
):
    copies = start_copies(((w_hbm, weights),), sems)
    half = kernel // 2
    rows, channels = feat.shape
    block = act_buf.shape[0]
    gain_f = gain[...].reshape(1, channels).astype(F32)
    taps[...] = jnp.zeros_like(taps)
    sums[...] = jnp.zeros_like(sums)
    chunk = 32

    @pl.loop(0, rows // block)
    def _(step):
        start = pl.multiple_of(step * block, block)
        onehot = (iota((table.shape[0], block), 0) == base[:, pl.ds(start, block)]).astype(BF16)
        embed = dot_tn(onehot, table[...])
        for begin in range(0, block, chunk):
            part = slice(begin, begin + chunk)
            here = pl.ds(start + begin, chunk)
            summed = feat[here, :].astype(F32) + embed[part, :]
            inv_rms, normed = normed_of(summed)
            u = normed * gain_f
            tanh_val, value = gelu_of(u)
            act_buf[part, :] = value.astype(BF16)
            high_buf[part, :], low_buf[part, :] = split2(summed)
            tanh_out[here, :] = tanh_val
            normed_out[here, :] = normed
            inv_out[here, :] = jnp.broadcast_to(inv_rms, (chunk, inv_out.shape[1]))
        shape = (kernel * tok_rows, block)
        row = iota(shape, 0)
        tap = sum((row >= tok_rows * j).astype(jnp.int32) for j in range(1, kernel))
        token = row - tap * tok_rows
        offset = iota(shape, 1) + start - tap + half - token * pool
        spread = ((offset >= 0) & (offset < pool)).astype(BF16)
        taps[...] += dot_nn(spread, act_buf[...])
        plain = spread[half * tok_rows : (half + 1) * tok_rows, :]
        sums[...] += dot_nn(plain, high_buf[...]) + dot_nn(plain, low_buf[...])

    for copy in copies:
        copy.wait()


def slope_kernel(tanh_ref, normed_ref, inv_ref, gain, *refs):
    count = len(refs) // 2 - 1
    sources, slope_out, copied, sems = refs[:count], refs[count], refs[count + 1 : -1], refs[-1]
    copies = start_copies(tuple(zip(sources, copied)), sems)
    rows, channels = normed_ref.shape
    gain_f = gain[...].reshape(1, channels).astype(F32)
    chunk = 32

    @pl.loop(0, rows // chunk)
    def _(step):
        here = pl.ds(pl.multiple_of(step * chunk, chunk), chunk)
        tanh_val = tanh_ref[here, :]
        u = normed_ref[here, :] * gain_f
        slopes = 0.5 * (1.0 + tanh_val) + 0.5 * u * (1.0 - tanh_val * tanh_val) * GELU_SCALE * (
            1.0 + 3.0 * CUBIC * (u * u)
        )
        slope_out[here, :] = inv_ref[here, :1] * (slopes * gain_f)

    for copy in copies:
        copy.wait()


def taps_kernel(kernel, tok_rows, blocks, taps, gain, near, far, pairs, *rest):
    outs, turn = rest[:blocks], rest[blocks]
    half = kernel // 2
    me = lax.axis_index("ctx")
    odd = me % 2 == 1
    channels = taps.shape[1]
    gain_f = gain[...].reshape(1, channels).astype(F32)
    edges = []
    for edge in (near, far):
        _, normed = normed_of(edge[...])
        edges.append(gelu_of(normed * gain_f)[1].astype(BF16).astype(F32))
    before = jnp.where(odd, edges[0], edges[1])
    after = jnp.where(odd, edges[1], edges[0])
    row = iota((tok_rows, channels), 0)
    highs = []
    for j in range(kernel):
        value = taps[j * tok_rows : (j + 1) * tok_rows, :]
        if j < half:
            extra = jnp.sum(before[j:, :], axis=0, keepdims=True)
            value = value + jnp.where(row == 0, extra, 0.0)
        if j > half:
            extra = jnp.sum(after[: j - half, :], axis=0, keepdims=True)
            value = value + jnp.where(row == tok_rows - 1, extra, 0.0)
        high, low = split2(value)
        highs.append(high)
        pairs[j] = jnp.concatenate([high, low], axis=0)
    width = channels // blocks
    for b in range(blocks):
        turn[b ^ me] = jnp.concatenate([h[:, b * width : (b + 1) * width] for h in highs], axis=1)
    for b in range(blocks):
        outs[b][...] = turn[b]


def pool_kernel(pool, pairs, sums, weights, cot, rows, sems):
    copies = start_copies(((cot, rows.at[1]),), sems)
    tok_rows = sums.shape[0]
    total = dot_nn(pairs[0], weights[0])
    for j in range(1, pairs.shape[0]):
        total = total + dot_nn(pairs[j], weights[j])
    conv = total[:tok_rows] + total[tok_rows:]
    rows[0] = ((sums[...] + conv) * (1.0 / pool)).astype(BF16)
    for copy in copies:
        copy.wait()


def pack_kernel(*refs):
    *parts, out, buf = refs
    at = 0
    for part in parts:
        buf[at : at + part.shape[0], :] = part[...]
        at += part.shape[0]
    eye = (iota((at, at), 0) == iota((at, at), 1)).astype(BF16)
    out[...] = dot_tn(buf[...], eye).astype(BF16)


def attention_kernel(pool, blocks, near_rels, late, *refs):
    parts, refs = refs[:blocks], refs[blocks:]
    weights, refs = refs[:4], refs[4:]
    g_out, refs = refs[0], refs[1:]
    gts, refs = refs[: len(near_rels)], refs[len(near_rels) :]
    p_buf, c_buf, q_buf, k_buf, v_buf, ga_buf, gq_buf, gk_buf, gv_buf, turn = refs
    size = parts[0].shape[1]
    for at, part in enumerate(parts):
        p_buf[at * size : (at + 1) * size, :] = part[0]
        c_buf[at * size : (at + 1) * size, :] = part[1]
    for i, dst in enumerate((q_buf, k_buf, v_buf)):
        dst[...] = dot_nn(p_buf[...], weights[i][...]).astype(BF16)
    ga_buf[...] = dot_nt(c_buf[...], weights[3][...]).astype(BF16)
    scale = 1.0 / DH**0.5
    for h in range(HEADS):
        cols = slice(h * DH, (h + 1) * DH)
        q, k, v, ga = q_buf[:, cols], k_buf[:, cols], v_buf[:, cols], ga_buf[:, cols]
        scores = dot_nt(q, k) * scale
        expo = jnp.exp(scores - jnp.max(scores, axis=-1, keepdims=True))
        probs = expo / jnp.sum(expo, axis=-1, keepdims=True)
        probs_b = probs.astype(BF16)
        out = dot_nn(probs_b, v).astype(BF16)
        delta = jnp.sum(ga.astype(F32) * out.astype(F32), axis=-1, keepdims=True)
        grad_score = (probs * (dot_nt(ga, v) - delta) * scale).astype(BF16)
        gq_buf[:, cols] = dot_nn(grad_score, k).astype(BF16)
        gk_buf[:, cols] = dot_tn(grad_score, q).astype(BF16)
        gv_buf[:, cols] = dot_tn(probs_b, ga).astype(BF16)
    grad = c_buf[...].astype(F32)
    for i, src in enumerate((gq_buf, gk_buf, gv_buf)):
        grad = grad + dot_nt(src[...], weights[i][...])
    g = (grad * (1.0 / pool)).astype(BF16)
    g_out[...] = g
    tokens = g.shape[0]
    eye = (iota((tokens, tokens), 0) == iota((tokens, tokens), 1)).astype(BF16)
    turned = dot_tn(g, eye).astype(BF16)
    count = turn.shape[0]
    span = turned.shape[0] // count
    me = lax.axis_index("dp")
    for o in range(count):
        turn[o ^ me] = turned[o * span : (o + 1) * span, :]
    for gt, base in zip(gts, near_rels):
        for at, rel in enumerate(late):
            gt[at * span : (at + 1) * span, :] = turn[base ^ rel]


def spread_kernel(kernel, tok_rows, befores, afters, g_ref, weights, highs, lows, near):
    tokens = g_ref.shape[0]
    padded = near.shape[0]
    me = lax.axis_index("ctx")
    row = iota((padded, tokens), 0)
    source = jnp.where(
        row == 0, pick(me, befores), jnp.where(row == tok_rows + 1, pick(me, afters), row - 1)
    )
    source = jnp.where(row > tok_rows + 1, -1, source)
    chosen = (source == iota((padded, tokens), 1)).astype(BF16)
    rows = dot_nn(chosen, g_ref[...]).astype(BF16)
    near[...] = rows
    for j in range(kernel):
        part = slice(j * padded, (j + 1) * padded)
        highs[part, :], lows[part, :] = split2(dot_nt(rows, weights[j]))


def input_grad_kernel(kernel, pool, highs, lows, near, slope, normed, out):
    half = kernel // 2
    rows = out.shape[0]
    padded = near.shape[0]
    start = pl.program_id(0) * rows
    here = pl.ds(pl.multiple_of(start, rows), rows)
    shape = (rows, kernel * padded)
    col = iota(shape, 1)
    tap = sum((col >= padded * j).astype(jnp.int32) for j in range(1, kernel))
    token = col - tap * padded - 1
    offset = iota(shape, 0) + start - tap + half - token * pool
    spread = ((offset >= 0) & (offset < pool)).astype(BF16)
    grad_act = dot_nn(spread, highs[...]) + dot_nn(spread, lows[...])
    plain = spread[:, half * padded : (half + 1) * padded]
    grad_rows = dot_nn(plain, near[...])
    scaled = grad_act * slope[here, :]
    unit = normed[here, :]
    mean = jnp.mean(scaled * unit, axis=-1, keepdims=True)
    out[...] = (grad_rows + scaled - unit * mean).astype(BF16)


def kernel_grad_kernel(factor, *refs):
    count = len(refs) // 2 - 1
    acts, gts, (mine, theirs) = refs[:count], refs[count : 2 * count], refs[2 * count :]
    total = None
    for act, gt in zip(acts, gts):
        term = dot_nt(gt[...], act[...])
        total = term if total is None else total + term
    total = total * factor
    span = mine.shape[0]
    mine[...] = total[:span, :]
    theirs[...] = total[span:, :].astype(BF16)


def fold_kernel(mine, other, kept, sent):
    span = kept.shape[0]
    kept[...] = mine[:span, :] + other[:span, :].astype(F32)
    sent[...] = (mine[span:, :] + other[span:, :].astype(F32)).astype(BF16)


def join_kernel(kernel, mine, other, out):
    width = out.shape[1]
    total = jnp.transpose(mine[...] + other[...].astype(F32))
    for j in range(kernel):
        out[j] = total[j * width : (j + 1) * width, :]


def xor_order(count):
    order = [0]
    bit = count // 2
    while bit:
        order = order + [v ^ bit for v in order]
        bit //= 2
    return order


def swap(value, axis, bit):
    count = lax.axis_size(axis)
    return lax.ppermute(value, axis, [(i, i ^ bit) for i in range(count)])


WHOLE = pl.BlockSpec(memory_space=pltpu.VMEM)


def call(body, args, outs, scratch=(), **options):
    options.setdefault("in_specs", [WHOLE] * len(args))
    options.setdefault("out_specs", [WHOLE] * len(outs))
    return pl.pallas_call(
        body,
        out_shape=list(outs),
        scratch_shapes=list(scratch),
        compiler_params=pltpu.CompilerParams(vmem_limit_bytes=VMEM_LIMIT),
        **options,
    )(*args)


def outside(*values):
    return [pltpu.with_memory_space_constraint(value, pltpu.HBM) for value in values]


def bits_of(count):
    return [1 << at for at in range(count.bit_length() - 1)]


def sums_of(bits):
    out = [0]
    for bit in bits:
        out = out + [bit + value for value in out]
    return out


def per_device(
    features, bases, dna_table, norm_gain, w_conv, w_query, w_key, w_value, w_out, cotangent
):
    feat, cot = features[0], cotangent[0]
    kernel = w_conv.shape[0]
    half = kernel // 2
    length, channels = feat.shape
    tok_rows = cot.shape[0]
    pool = length // tok_rows
    n_ctx, n_dp = lax.axis_size("ctx"), lax.axis_size("dp")
    tokens = n_ctx * tok_rows
    width = channels // n_ctx
    narrow = channels // n_dp
    near_rels = [0, X_BIT, Z_BIT, X_BIT + Z_BIT]
    late = sums_of([bit for bit in bits_of(n_dp) if bit not in (X_BIT, Z_BIT)])

    order = xor_order(n_ctx)
    place = {rel: at for at, rel in enumerate(order)}
    befores = [-1] + [place[c ^ (c - 1)] * tok_rows + tok_rows - 1 for c in range(1, n_ctx)]
    afters = [place[c ^ (c + 1)] * tok_rows for c in range(n_ctx - 1)] + [-1]

    edge = 16
    hbm = pl.BlockSpec(memory_space=pltpu.HBM)
    near, far, feat_v, base_v, table_v, gain_v = call(
        functools.partial(edge_kernel, half),
        outside(feat, bases, dna_table, norm_gain),
        [pltpu.VMEM((half, channels), F32)] * 2
        + [pltpu.VMEM(value.shape, value.dtype) for value in (feat, bases, dna_table, norm_gain)],
        [pltpu.VMEM((2, edge, channels), BF16), pltpu.SemaphoreType.DMA((6,))],
        in_specs=[hbm] * 4,
    )
    near = swap(near, "ctx", 1)
    links = [(i, i + 1) for i in range(1, n_ctx - 1, 2)]
    far = lax.ppermute(far, "ctx", links + [(b, a) for a, b in links])

    block = 128
    taps, sums, tanh_val, normed, inv_rms, w_conv_v = call(
        functools.partial(act_kernel, kernel, pool, tok_rows),
        [feat_v, base_v, table_v, gain_v] + outside(w_conv),
        [
            pltpu.VMEM((kernel * tok_rows, channels), F32),
            pltpu.VMEM((tok_rows, channels), F32),
            pltpu.VMEM((length, channels), F32),
            pltpu.VMEM((length, channels), F32),
            pltpu.VMEM((length, 128), F32),
            pltpu.VMEM(w_conv.shape, BF16),
        ],
        [pltpu.VMEM((block, channels), BF16)] * 3 + [pltpu.SemaphoreType.DMA((1,))],
        in_specs=[WHOLE] * 4 + [hbm],
    )
    pairs, *acts = call(
        functools.partial(taps_kernel, kernel, tok_rows, n_ctx),
        (taps, gain_v, near, far),
        [pltpu.VMEM((kernel, 2 * tok_rows, channels), BF16)]
        + [pltpu.VMEM((tok_rows, kernel * width), BF16)] * n_ctx,
        [pltpu.VMEM((n_ctx, tok_rows, kernel * width), BF16)],
    )
    acts = [acts[0]] + [swap(acts[rel], "ctx", rel) for rel in order[1:]]
    pooled = call(
        functools.partial(pool_kernel, pool),
        [pairs, sums, w_conv_v] + outside(cot),
        [pltpu.VMEM((2, tok_rows, channels), BF16)],
        [pltpu.SemaphoreType.DMA((1,))],
        in_specs=[WHOLE] * 3 + [hbm],
    )[0]
    squares = (w_query, w_key, w_value, w_out)
    slope, *squares_v = call(
        slope_kernel,
        [tanh_val, normed, inv_rms, gain_v] + outside(*squares),
        [pltpu.VMEM((length, channels), F32)] + [pltpu.VMEM(w.shape, BF16) for w in squares],
        [pltpu.SemaphoreType.DMA((4,))],
        in_specs=[WHOLE] * 4 + [hbm] * 4,
    )
    rows = [pooled]
    bit = n_ctx // 2
    while bit:
        rows = rows + [swap(value, "ctx", bit) for value in rows]
        bit //= 2

    act = call(
        pack_kernel,
        acts,
        [pltpu.VMEM((kernel * width, tokens), BF16)],
        [pltpu.VMEM((tokens, kernel * width), BF16)],
    )[0]

    act_z = swap(act, "dp", Z_BIT)
    act_x = swap(act, "dp", X_BIT)

    g_all, *gts = call(
        functools.partial(attention_kernel, pool, n_ctx, near_rels, late),
        (*rows, *squares_v),
        [pltpu.VMEM((tokens, channels), BF16)]
        + [pltpu.VMEM((len(late) * narrow, tokens), BF16)] * len(near_rels),
        [pltpu.VMEM((tokens, channels), BF16)] * 9 + [pltpu.VMEM((n_dp, narrow, tokens), BF16)],
    )

    act_zx = swap(act_z, "dp", X_BIT)
    swapped = [gts[0]]
    for at, rel in enumerate(near_rels[1:], 1):
        swapped.append(swap(gts[at], "dp", rel))

    padded = -(-(tok_rows + 2) // 8) * 8
    highs, lows, near_g = call(
        functools.partial(spread_kernel, kernel, tok_rows, befores, afters),
        (g_all, w_conv_v),
        [pltpu.VMEM((kernel * padded, channels), BF16)] * 2
        + [pltpu.VMEM((padded, channels), BF16)],
    )
    factor = 1.0 / (n_dp * length * n_ctx) ** 0.5
    kept = len(late) // 2
    mine, theirs = call(
        functools.partial(kernel_grad_kernel, factor),
        (act, act_x, act_z, act_zx, *swapped),
        [
            pltpu.VMEM((kept * narrow, kernel * width), F32),
            pltpu.VMEM((kept * narrow, kernel * width), BF16),
        ],
    )
    other = swap(theirs, "dp", late[kept])
    while kept > 1:
        kept //= 2
        mine, theirs = call(
            fold_kernel,
            (mine, other),
            [
                pltpu.VMEM((kept * narrow, kernel * width), F32),
                pltpu.VMEM((kept * narrow, kernel * width), BF16),
            ],
        )
        other = swap(theirs, "dp", late[kept])

    by_rows = pl.BlockSpec((block, channels), lambda i: (i, 0))
    grad_in = call(
        functools.partial(input_grad_kernel, kernel, pool),
        (highs, lows, near_g, slope, normed),
        [jax.ShapeDtypeStruct((length, channels), BF16)],
        grid=(length // block,),
        out_specs=[by_rows],
    )[0]
    grad_conv = call(
        functools.partial(join_kernel, kernel),
        (mine, other),
        [jax.ShapeDtypeStruct((kernel, width, narrow), F32)],
    )[0]
    return grad_in[None], jnp.transpose(grad_conv, (1, 0, 2))


def solution(mesh):
    in_specs = (
        P("dp", "ctx", None),
        P("dp", "ctx"),
        P(),
        P(),
        P(),
        P(),
        P(),
        P(),
        P(),
        P("dp", "ctx", None),
    )
    out_specs = (P("dp", "ctx", None), P("ctx", None, "dp"))
    return jax.shard_map(
        per_device, mesh=mesh, in_specs=in_specs, out_specs=out_specs, check_vma=False
    )
```

```python
import functools

import jax
import jax.numpy as jnp
from jax import lax
from jax.experimental import pallas as pl
from jax.experimental.pallas import tpu as pltpu
from jax.sharding import PartitionSpec as P


HEADS = 6
DH = 128

EPSILON = 1e-06
GELU_SCALE = 0.7978845608028654
CUBIC = 0.044715
F32 = jnp.float32
BF16 = jnp.bfloat16
VMEM_LIMIT = 28 << 20
X_BIT, Z_BIT = 1, 4


def dot_nn(left, right):
    return lax.dot_general(left, right, (((1,), (0,)), ((), ())), preferred_element_type=F32)


def dot_nt(left, right):
    return lax.dot_general(left, right, (((1,), (1,)), ((), ())), preferred_element_type=F32)


def dot_tn(left, right):
    return lax.dot_general(left, right, (((0,), (0,)), ((), ())), preferred_element_type=F32)


def split2(value):
    high = value.astype(BF16)
    return high, (value - high.astype(F32)).astype(BF16)


def iota(shape, dim):
    return lax.broadcasted_iota(jnp.int32, shape, dim)


def normed_of(summed):
    inv_rms = lax.rsqrt(jnp.mean(summed * summed, axis=-1, keepdims=True) + EPSILON)
    return inv_rms, summed * inv_rms


def gelu_of(u):
    tanh_val = jnp.tanh(GELU_SCALE * (u + CUBIC * (u * u * u)))
    return tanh_val, 0.5 * u * (1.0 + tanh_val)


def pick(index, values):
    out = jnp.int32(values[0])
    for at, value in enumerate(values[1:], 1):
        out = jnp.where(index == at, jnp.int32(value), out)
    return out


def start_copies(pairs, sems):
    copies = [pltpu.make_async_copy(src, dst, sems.at[i]) for i, (src, dst) in enumerate(pairs)]
    for copy in copies:
        copy.start()
    return copies


def act_kernel(
    kernel, pool, tok_rows, feat_hbm, base_hbm, table_hbm, gain_hbm, cot_hbm, w_hbm,
    taps, sums, tanh_out, normed_out, inv_out, gain, cot, weights,
    feat, base, table, act_buf, high_buf, low_buf, sems,
):
    half = kernel // 2
    rows, channels = feat.shape
    block = act_buf.shape[0]
    count = rows // block
    small = ((base_hbm, base), (table_hbm, table), (gain_hbm, gain))
    parts = tuple(
        (feat_hbm.at[pl.ds(i * block, block)], feat.at[pl.ds(i * block, block)]) for i in range(count)
    )
    copies = start_copies(small + parts + ((cot_hbm, cot), (w_hbm, weights)), sems)
    padded = taps.shape[0] // kernel
    taps[...] = jnp.zeros_like(taps)
    sums[...] = jnp.zeros_like(sums)
    for copy in copies[: len(small)]:
        copy.wait()
    gain_f = gain[...].reshape(1, channels).astype(F32)
    chunk = 32

    @pl.loop(0, count)
    def _(step):
        start = pl.multiple_of(step * block, block)
        here = pl.ds(start, block)
        pltpu.make_async_copy(feat_hbm.at[here], feat.at[here], sems.at[len(small) + step]).wait()
        onehot = (iota((table.shape[0], block), 0) == base[:, here]).astype(BF16)
        embed = dot_tn(onehot, table[...])
        for begin in range(0, block, chunk):
            part = slice(begin, begin + chunk)
            here = pl.ds(start + begin, chunk)
            summed = feat[here, :].astype(F32) + embed[part, :]
            inv_rms, normed = normed_of(summed)
            u = normed * gain_f
            tanh_val, value = gelu_of(u)
            act_buf[part, :] = value.astype(BF16)
            high_buf[part, :], low_buf[part, :] = split2(summed)
            tanh_out[here, :] = tanh_val
            normed_out[here, :] = normed
            inv_out[here, :] = jnp.broadcast_to(inv_rms, (chunk, inv_out.shape[1]))
        shape = (kernel * padded, block)
        row = iota(shape, 0)
        tap = sum((row >= padded * j).astype(jnp.int32) for j in range(1, kernel))
        token = row - tap * padded
        token = jnp.where(token == tok_rows, -1, jnp.where(token == tok_rows + 1, tok_rows, token))
        known = row - tap * padded < tok_rows + 2
        offset = iota(shape, 1) + start - tap + half - token * pool
        spread = ((offset >= 0) & (offset < pool) & known).astype(BF16)
        taps[...] += dot_nn(spread, act_buf[...])
        plain = spread[half * padded : (half + 1) * padded, :]
        sums[...] += dot_nn(plain, high_buf[...]) + dot_nn(plain, low_buf[...])

    for copy in copies[len(small) + count :]:
        copy.wait()


def taps_kernel(kernel, blocks, taps, pairs, *rest):
    outs, turn = rest[:blocks], rest[blocks]
    me = lax.axis_index("ctx")
    padded = taps.shape[0] // kernel
    highs = []
    for j in range(kernel):
        high, low = split2(taps[j * padded : (j + 1) * padded, :])
        highs.append(high)
        pairs[j] = jnp.concatenate([high, low], axis=0)
    width = taps.shape[1] // blocks
    for b in range(blocks):
        turn[b ^ me] = jnp.concatenate([h[:, b * width : (b + 1) * width] for h in highs], axis=1)
    for b in range(blocks):
        outs[b][...] = turn[b]


def pool_kernel(pool, tok_rows, pairs, sums, weights, cot, rows):
    padded = sums.shape[0]
    total = dot_nn(pairs[0], weights[0])
    for j in range(1, pairs.shape[0]):
        total = total + dot_nn(pairs[j], weights[j])
    conv = total[:padded] + total[padded:]
    value = (sums[...] + conv) * (1.0 / pool)
    high, low = split2(value)
    rows[:padded, :] = high
    rows[padded : padded + tok_rows, :] = cot[...]
    low_f = low.astype(F32)
    ends = [low_f[:1], low_f[tok_rows - 1 : tok_rows + 2]]
    ends = jnp.concatenate(ends + [jnp.zeros((4, low.shape[1]), F32)], axis=0)
    rows[padded + tok_rows :, :] = ends.astype(BF16)


def neighbours(me, order, count, befores, afters, ends):
    zero = jnp.zeros(ends.shape[1:], F32)
    ends[0] = zero
    ends[count + 1] = zero
    for rel, before, after in zip(order, befores, afters):
        owner = me ^ rel
        ends[owner + 1, 0:1, :] = before
        ends[owner + 1, 1:2, :] = after
    return [(ends[me ^ rel, 1:2, :], ends[(me ^ rel) + 2, 0:1, :]) for rel in order]


def pack_kernel(order, tok_rows, *refs):
    *parts, out, buf, ends = refs
    me = lax.axis_index("ctx")
    tails = [part[tok_rows : tok_rows + 8, :].astype(F32) for part in parts]
    extra = neighbours(
        me, order, len(parts), [tail[0:1] for tail in tails], [tail[1:2] for tail in tails], ends
    )
    for at, (part, (first, last)) in enumerate(zip(parts, extra)):
        value = part[:tok_rows, :].astype(F32)
        row = iota(value.shape, 0)
        value = value + jnp.where(row == 0, first, 0.0) + jnp.where(row == tok_rows - 1, last, 0.0)
        buf[at * tok_rows : (at + 1) * tok_rows, :] = value.astype(BF16)
    total = buf.shape[0]
    eye = (iota((total, total), 0) == iota((total, total), 1)).astype(BF16)
    out[...] = dot_tn(buf[...], eye).astype(BF16)


def attention_kernel(pool, order, tok_rows, near_rels, late, *refs):
    blocks = len(order)
    parts, refs = refs[:blocks], refs[blocks:]
    (wq, wk, wv_hbm, wo_hbm), refs = refs[:4], refs[4:]
    g_out, refs = refs[0], refs[1:]
    gts, refs = refs[: len(near_rels)], refs[len(near_rels) :]
    p_buf, c_buf, q_buf, k_buf, v_buf, ga_buf, gq_buf, gk_buf, gv_buf = refs[:9]
    probs_buf, turn, ends, wv, wo, sems = refs[9:]
    copies = start_copies(((wv_hbm, wv), (wo_hbm, wo)), sems)
    padded = parts[0].shape[0] - tok_rows - 8
    befores, afters, firsts, lasts = [], [], [], []
    for part in parts:
        tail = part[tok_rows : tok_rows + 8, :].astype(F32)
        lows = part[padded + tok_rows :, :].astype(F32)
        firsts.append(part[:8, :].astype(F32)[0:1] + lows[0:1])
        lasts.append(part[tok_rows - 8 : tok_rows, :].astype(F32)[7:8] + lows[1:2])
        befores.append(tail[0:1] + lows[2:3])
        afters.append(tail[1:2] + lows[3:4])
    extra = neighbours(lax.axis_index("ctx"), order, blocks, befores, afters, ends)
    for at, (part, first, last, (to_first, to_last)) in enumerate(zip(parts, firsts, lasts, extra)):
        value = part[:tok_rows, :].astype(F32)
        row = iota(value.shape, 0)
        value = jnp.where(row == 0, first + to_first, value)
        value = jnp.where(row == tok_rows - 1, last + to_last, value)
        here = slice(at * tok_rows, (at + 1) * tok_rows)
        p_buf[here, :] = value.astype(BF16)
        c_buf[here, :] = part[padded : padded + tok_rows, :]
    q_buf[...] = dot_nn(p_buf[...], wq[...]).astype(BF16)
    k_buf[...] = dot_nn(p_buf[...], wk[...]).astype(BF16)
    scale = 1.0 / DH**0.5
    for h in range(HEADS):
        cols = slice(h * DH, (h + 1) * DH)
        scores = dot_nt(q_buf[:, cols], k_buf[:, cols]) * scale
        expo = jnp.exp(scores - jnp.max(scores, axis=-1, keepdims=True))
        probs_buf[h] = expo / jnp.sum(expo, axis=-1, keepdims=True)
    copies[0].wait()
    v_buf[...] = dot_nn(p_buf[...], wv[...]).astype(BF16)
    copies[1].wait()
    ga_buf[...] = dot_nt(c_buf[...], wo[...]).astype(BF16)
    for h in range(HEADS):
        cols = slice(h * DH, (h + 1) * DH)
        q, k, v, ga = q_buf[:, cols], k_buf[:, cols], v_buf[:, cols], ga_buf[:, cols]
        probs = probs_buf[h]
        probs_b = probs.astype(BF16)
        out = dot_nn(probs_b, v).astype(BF16)
        delta = jnp.sum(ga.astype(F32) * out.astype(F32), axis=-1, keepdims=True)
        grad_score = (probs * (dot_nt(ga, v) - delta) * scale).astype(BF16)
        gq_buf[:, cols] = dot_nn(grad_score, k).astype(BF16)
        gk_buf[:, cols] = dot_tn(grad_score, q).astype(BF16)
        gv_buf[:, cols] = dot_tn(probs_b, ga).astype(BF16)
    grad = c_buf[...].astype(F32)
    for src, weight in ((gq_buf, wq), (gk_buf, wk), (gv_buf, wv)):
        grad = grad + dot_nt(src[...], weight[...])
    g = (grad * (1.0 / pool)).astype(BF16)
    g_out[...] = g
    tokens = g.shape[0]
    eye = (iota((tokens, tokens), 0) == iota((tokens, tokens), 1)).astype(BF16)
    turned = dot_tn(g, eye).astype(BF16)
    count = turn.shape[0]
    span = turned.shape[0] // count
    me = lax.axis_index("dp")
    for o in range(count):
        turn[o ^ me] = turned[o * span : (o + 1) * span, :]
    for gt, base in zip(gts, near_rels):
        for at, rel in enumerate(late):
            gt[at * span : (at + 1) * span, :] = turn[base ^ rel]


def spread_kernel(kernel, tok_rows, befores, afters, g_ref, weights, highs, lows, near):
    tokens = g_ref.shape[0]
    padded = near.shape[0]
    me = lax.axis_index("ctx")
    row = iota((padded, tokens), 0)
    source = jnp.where(
        row == 0, pick(me, befores), jnp.where(row == tok_rows + 1, pick(me, afters), row - 1)
    )
    source = jnp.where(row > tok_rows + 1, -1, source)
    chosen = (source == iota((padded, tokens), 1)).astype(BF16)
    rows = dot_nn(chosen, g_ref[...]).astype(BF16)
    near[...] = rows
    for j in range(kernel):
        part = slice(j * padded, (j + 1) * padded)
        highs[part, :], lows[part, :] = split2(dot_nt(rows, weights[j]))


def input_grad_kernel(
    kernel, pool, highs, lows, near, tanh_ref, normed_ref, inv_ref, gain, out
):
    half = kernel // 2
    rows, channels = out.shape
    padded = near.shape[0]
    start = pl.program_id(0) * rows
    here = pl.ds(pl.multiple_of(start, rows), rows)
    shape = (rows, kernel * padded)
    col = iota(shape, 1)
    tap = sum((col >= padded * j).astype(jnp.int32) for j in range(1, kernel))
    token = col - tap * padded - 1
    offset = iota(shape, 0) + start - tap + half - token * pool
    spread = ((offset >= 0) & (offset < pool)).astype(BF16)
    grad_act = dot_nn(spread, highs[...]) + dot_nn(spread, lows[...])
    plain = spread[:, half * padded : (half + 1) * padded]
    grad_rows = dot_nn(plain, near[...])
    gain_f = gain[...].reshape(1, channels).astype(F32)
    tanh_val, unit = tanh_ref[here, :], normed_ref[here, :]
    u = unit * gain_f
    slopes = 0.5 * (1.0 + tanh_val) + 0.5 * u * (1.0 - tanh_val * tanh_val) * GELU_SCALE * (
        1.0 + 3.0 * CUBIC * (u * u)
    )
    grad_norm = grad_act * slopes * gain_f
    mean = jnp.mean(grad_norm * unit, axis=-1, keepdims=True)
    out[...] = (grad_rows + inv_ref[here, :1] * (grad_norm - unit * mean)).astype(BF16)


def kernel_grad_kernel(factor, *refs):
    count = len(refs) // 2 - 1
    acts, gts, (mine, theirs) = refs[:count], refs[count : 2 * count], refs[2 * count :]
    total = None
    for act, gt in zip(acts, gts):
        term = dot_nt(gt[...], act[...])
        total = term if total is None else total + term
    total = total * factor
    span = mine.shape[0]
    mine[...] = total[:span, :]
    theirs[...] = total[span:, :].astype(BF16)


def fold_kernel(mine, other, kept, sent):
    span = kept.shape[0]
    kept[...] = mine[:span, :] + other[:span, :].astype(F32)
    sent[...] = (mine[span:, :] + other[span:, :].astype(F32)).astype(BF16)


def join_kernel(kernel, mine, other, out):
    width = out.shape[1]
    total = jnp.transpose(mine[...] + other[...].astype(F32))
    for j in range(kernel):
        out[j] = total[j * width : (j + 1) * width, :]


def xor_order(count):
    order = [0]
    bit = count // 2
    while bit:
        order = order + [v ^ bit for v in order]
        bit //= 2
    return order


def swap(value, axis, bit):
    count = lax.axis_size(axis)
    return lax.ppermute(value, axis, [(i, i ^ bit) for i in range(count)])


WHOLE = pl.BlockSpec(memory_space=pltpu.VMEM)


def call(body, args, outs, scratch=(), **options):
    options.setdefault("in_specs", [WHOLE] * len(args))
    options.setdefault("out_specs", [WHOLE] * len(outs))
    return pl.pallas_call(
        body,
        out_shape=list(outs),
        scratch_shapes=list(scratch),
        compiler_params=pltpu.CompilerParams(vmem_limit_bytes=VMEM_LIMIT),
        **options,
    )(*args)


def outside(*values):
    return [pltpu.with_memory_space_constraint(value, pltpu.HBM) for value in values]


def bits_of(count):
    return [1 << at for at in range(count.bit_length() - 1)]


def sums_of(bits):
    out = [0]
    for bit in bits:
        out = out + [bit + value for value in out]
    return out


def per_device(
    features, bases, dna_table, norm_gain, w_conv, w_query, w_key, w_value, w_out, cotangent
):
    feat, cot = features[0], cotangent[0]
    kernel = w_conv.shape[0]
    length, channels = feat.shape
    tok_rows = cot.shape[0]
    pool = length // tok_rows
    n_ctx, n_dp = lax.axis_size("ctx"), lax.axis_size("dp")
    tokens = n_ctx * tok_rows
    width = channels // n_ctx
    narrow = channels // n_dp
    near_rels = [0, X_BIT, Z_BIT, X_BIT + Z_BIT]
    late = sums_of([bit for bit in bits_of(n_dp) if bit not in (X_BIT, Z_BIT)])

    order = xor_order(n_ctx)
    place = {rel: at for at, rel in enumerate(order)}
    befores = [-1] + [place[c ^ (c - 1)] * tok_rows + tok_rows - 1 for c in range(1, n_ctx)]
    afters = [place[c ^ (c + 1)] * tok_rows for c in range(n_ctx - 1)] + [-1]

    hbm = pl.BlockSpec(memory_space=pltpu.HBM)
    block = 128
    wide = -(-(tok_rows + 2) // 8) * 8
    taps, sums, tanh_val, normed, inv_rms, gain_v, cot_v, w_conv_v = call(
        functools.partial(act_kernel, kernel, pool, tok_rows),
        outside(feat, bases, dna_table, norm_gain, cot, w_conv),
        [
            pltpu.VMEM((kernel * wide, channels), F32),
            pltpu.VMEM((wide, channels), F32),
            pltpu.VMEM((length, channels), F32),
            pltpu.VMEM((length, channels), F32),
            pltpu.VMEM((length, 128), F32),
            pltpu.VMEM(norm_gain.shape, BF16),
            pltpu.VMEM(cot.shape, BF16),
            pltpu.VMEM(w_conv.shape, BF16),
        ],
        [
            pltpu.VMEM(feat.shape, BF16),
            pltpu.VMEM(bases.shape, jnp.int32),
            pltpu.VMEM(dna_table.shape, BF16),
        ]
        + [pltpu.VMEM((block, channels), BF16)] * 3
        + [pltpu.SemaphoreType.DMA((5 + length // block,))],
        in_specs=[hbm] * 6,
    )
    pairs, *acts = call(
        functools.partial(taps_kernel, kernel, n_ctx),
        (taps,),
        [pltpu.VMEM((kernel, 2 * wide, channels), BF16)]
        + [pltpu.VMEM((wide, kernel * width), BF16)] * n_ctx,
        [pltpu.VMEM((n_ctx, wide, kernel * width), BF16)],
    )
    acts = [acts[0]] + [swap(acts[rel], "ctx", rel) for rel in order[1:]]
    pooled = call(
        functools.partial(pool_kernel, pool, tok_rows),
        (pairs, sums, w_conv_v, cot_v),
        [pltpu.VMEM((wide + tok_rows + 8, channels), BF16)],
    )[0]
    rows = [pooled]
    bit = n_ctx // 2
    while bit:
        rows = rows + [swap(value, "ctx", bit) for value in rows]
        bit //= 2

    act = call(
        functools.partial(pack_kernel, order, tok_rows),
        acts,
        [pltpu.VMEM((kernel * width, tokens), BF16)],
        [
            pltpu.VMEM((tokens, kernel * width), BF16),
            pltpu.VMEM((n_ctx + 2, 8, kernel * width), F32),
        ],
    )[0]

    act_z = swap(act, "dp", Z_BIT)
    act_x = swap(act, "dp", X_BIT)

    g_all, *gts = call(
        functools.partial(attention_kernel, pool, order, tok_rows, near_rels, late),
        [*rows, w_query, w_key] + outside(w_value, w_out),
        [pltpu.VMEM((tokens, channels), BF16)]
        + [pltpu.VMEM((len(late) * narrow, tokens), BF16)] * len(near_rels),
        [pltpu.VMEM((tokens, channels), BF16)] * 9
        + [
            pltpu.VMEM((HEADS, tokens, tokens), F32),
            pltpu.VMEM((n_dp, narrow, tokens), BF16),
            pltpu.VMEM((n_ctx + 2, 8, channels), F32),
            pltpu.VMEM(w_value.shape, BF16),
            pltpu.VMEM(w_out.shape, BF16),
            pltpu.SemaphoreType.DMA((2,)),
        ],
        in_specs=[WHOLE] * (n_ctx + 2) + [hbm] * 2,
    )

    act_zx = swap(act_z, "dp", X_BIT)
    swapped = [gts[0]]
    for at, rel in enumerate(near_rels[1:], 1):
        swapped.append(swap(gts[at], "dp", rel))

    padded = -(-(tok_rows + 2) // 8) * 8
    highs, lows, near_g = call(
        functools.partial(spread_kernel, kernel, tok_rows, befores, afters),
        (g_all, w_conv_v),
        [pltpu.VMEM((kernel * padded, channels), BF16)] * 2
        + [pltpu.VMEM((padded, channels), BF16)],
    )
    factor = 1.0 / (n_dp * length * n_ctx) ** 0.5
    kept = len(late) // 2
    mine, theirs = call(
        functools.partial(kernel_grad_kernel, factor),
        (act, act_x, act_z, act_zx, *swapped),
        [
            pltpu.VMEM((kept * narrow, kernel * width), F32),
            pltpu.VMEM((kept * narrow, kernel * width), BF16),
        ],
    )
    other = swap(theirs, "dp", late[kept])
    while kept > 1:
        kept //= 2
        mine, theirs = call(
            fold_kernel,
            (mine, other),
            [
                pltpu.VMEM((kept * narrow, kernel * width), F32),
                pltpu.VMEM((kept * narrow, kernel * width), BF16),
            ],
        )
        other = swap(theirs, "dp", late[kept])

    by_rows = pl.BlockSpec((block, channels), lambda i: (i, 0))
    grad_in = call(
        functools.partial(input_grad_kernel, kernel, pool),
        (highs, lows, near_g, tanh_val, normed, inv_rms, gain_v),
        [jax.ShapeDtypeStruct((length, channels), BF16)],
        grid=(length // block,),
        out_specs=[by_rows],
    )[0]
    grad_conv = call(
        functools.partial(join_kernel, kernel),
        (mine, other),
        [jax.ShapeDtypeStruct((kernel, width, narrow), F32)],
    )[0]
    return grad_in[None], jnp.transpose(grad_conv, (1, 0, 2))


def solution(mesh):
    in_specs = (
        P("dp", "ctx", None),
        P("dp", "ctx"),
        P(),
        P(),
        P(),
        P(),
        P(),
        P(),
        P(),
        P("dp", "ctx", None),
    )
    out_specs = (P("dp", "ctx", None), P("ctx", None, "dp"))
    return jax.shard_map(
        per_device, mesh=mesh, in_specs=in_specs, out_specs=out_specs, check_vma=False
    )
```

```python
import functools

import jax
import jax.numpy as jnp
from jax import lax
from jax.experimental import pallas as pl
from jax.experimental.pallas import tpu as pltpu
from jax.sharding import PartitionSpec as P


HEADS = 6
DH = 128

EPSILON = 1e-06
GELU_SCALE = 0.7978845608028654
CUBIC = 0.044715
F32 = jnp.float32
BF16 = jnp.bfloat16
VMEM_LIMIT = 28 << 20
X_BIT, Z_BIT = 1, 4


def dot_nn(left, right):
    return lax.dot_general(left, right, (((1,), (0,)), ((), ())), preferred_element_type=F32)


def dot_nt(left, right):
    return lax.dot_general(left, right, (((1,), (1,)), ((), ())), preferred_element_type=F32)


def dot_tn(left, right):
    return lax.dot_general(left, right, (((0,), (0,)), ((), ())), preferred_element_type=F32)


def split2(value):
    high = value.astype(BF16)
    return high, (value - high.astype(F32)).astype(BF16)


def iota(shape, dim):
    return lax.broadcasted_iota(jnp.int32, shape, dim)


def normed_of(summed):
    inv_rms = lax.rsqrt(jnp.mean(summed * summed, axis=-1, keepdims=True) + EPSILON)
    return inv_rms, summed * inv_rms


def gelu_of(u):
    tanh_val = jnp.tanh(GELU_SCALE * (u + CUBIC * (u * u * u)))
    return tanh_val, 0.5 * u * (1.0 + tanh_val)


def pick(index, values):
    out = jnp.int32(values[0])
    for at, value in enumerate(values[1:], 1):
        out = jnp.where(index == at, jnp.int32(value), out)
    return out


def start_copies(pairs, sems):
    copies = [pltpu.make_async_copy(src, dst, sems.at[i]) for i, (src, dst) in enumerate(pairs)]
    for copy in copies:
        copy.start()
    return copies


def act_kernel(
    kernel, pool, tok_rows, feat_hbm, base_hbm, table_hbm, gain_hbm, cot_hbm, w_hbm,
    taps, sums, normed_out, inv_out, gain, cot, weights, feat, base, table, act_buf, sems,
):
    half = kernel // 2
    _, channels = feat.shape
    count, block = act_buf.shape[:2]
    small = ((base_hbm, base), (table_hbm, table), (gain_hbm, gain))
    parts = tuple(
        (feat_hbm.at[pl.ds(i * block, block)], feat.at[pl.ds(i * block, block)]) for i in range(count)
    )
    copies = start_copies(small + parts + ((cot_hbm, cot), (w_hbm, weights)), sems)
    padded = taps.shape[0] // kernel
    for copy in copies[: len(small)]:
        copy.wait()
    gain_f = gain[...].reshape(1, channels).astype(F32)
    chunk = 32
    for step in range(count):
        start = step * block
        here = slice(start, start + block)
        copies[len(small) + step].wait()
        onehot = (iota((table.shape[0], block), 0) == base[:, here]).astype(BF16)
        embed = dot_tn(onehot, table[...])
        for begin in range(0, block, chunk):
            part = slice(begin, begin + chunk)
            some = slice(start + begin, start + begin + chunk)
            summed = feat[some, :].astype(F32) + embed[part, :]
            inv_rms, normed = normed_of(summed)
            act_buf[step, part, :] = gelu_of(normed * gain_f)[1].astype(BF16)
            normed_out[some, :] = normed
            inv_out[some, :] = jnp.broadcast_to(inv_rms, (chunk, inv_out.shape[1]))
        shape = (kernel * padded, block)
        row = iota(shape, 0)
        tap = sum((row >= padded * j).astype(jnp.int32) for j in range(1, kernel))
        token = row - tap * padded
        token = jnp.where(token == tok_rows, -1, jnp.where(token == tok_rows + 1, tok_rows, token))
        known = row - tap * padded < tok_rows + 2
        offset = iota(shape, 1) + start - tap + half - token * pool
        spread = ((offset >= 0) & (offset < pool) & known).astype(BF16)
        term = dot_nn(spread, act_buf[step])
        taps[...] = term if step == 0 else taps[...] + term
        plain = spread[half * padded : (half + 1) * padded, :]
        counts = dot_nt(plain, onehot).astype(BF16)
        term = dot_nn(plain, feat[here, :]) + dot_nn(counts, table[...])
        sums[...] = term if step == 0 else sums[...] + term

    for copy in copies[len(small) + count :]:
        copy.wait()


def taps_kernel(kernel, blocks, taps, pairs, *rest):
    outs, turn = rest[:blocks], rest[blocks]
    me = lax.axis_index("ctx")
    padded = taps.shape[0] // kernel
    highs = []
    for j in range(kernel):
        high, low = split2(taps[j * padded : (j + 1) * padded, :])
        highs.append(high)
        pairs[j] = jnp.concatenate([high, low], axis=0)
    width = taps.shape[1] // blocks
    for b in range(blocks):
        turn[b ^ me] = jnp.concatenate([h[:, b * width : (b + 1) * width] for h in highs], axis=1)
    for b in range(blocks):
        outs[b][...] = turn[b]


def pool_kernel(pool, tok_rows, pairs, sums, weights, cot, rows):
    padded = sums.shape[0]
    total = dot_nn(pairs[0], weights[0])
    for j in range(1, pairs.shape[0]):
        total = total + dot_nn(pairs[j], weights[j])
    conv = total[:padded] + total[padded:]
    value = (sums[...] + conv) * (1.0 / pool)
    high, low = split2(value)
    rows[:padded, :] = high
    rows[padded : padded + tok_rows, :] = cot[...]
    low_f = low.astype(F32)
    ends = [low_f[:1], low_f[tok_rows - 1 : tok_rows + 2]]
    ends = jnp.concatenate(ends + [jnp.zeros((4, low.shape[1]), F32)], axis=0)
    rows[padded + tok_rows :, :] = ends.astype(BF16)


def neighbours(me, order, count, befores, afters, ends):
    zero = jnp.zeros(ends.shape[1:], F32)
    ends[0] = zero
    ends[count + 1] = zero
    for rel, before, after in zip(order, befores, afters):
        owner = me ^ rel
        ends[owner + 1, 0:1, :] = before
        ends[owner + 1, 1:2, :] = after
    return [(ends[me ^ rel, 1:2, :], ends[(me ^ rel) + 2, 0:1, :]) for rel in order]


def pack_kernel(order, tok_rows, *refs):
    *parts, out, buf, ends = refs
    me = lax.axis_index("ctx")
    tails = [part[tok_rows : tok_rows + 8, :].astype(F32) for part in parts]
    extra = neighbours(
        me, order, len(parts), [tail[0:1] for tail in tails], [tail[1:2] for tail in tails], ends
    )
    for at, (part, (first, last)) in enumerate(zip(parts, extra)):
        value = part[:tok_rows, :].astype(F32)
        row = iota(value.shape, 0)
        value = value + jnp.where(row == 0, first, 0.0) + jnp.where(row == tok_rows - 1, last, 0.0)
        buf[at * tok_rows : (at + 1) * tok_rows, :] = value.astype(BF16)
    total = buf.shape[0]
    eye = (iota((total, total), 0) == iota((total, total), 1)).astype(BF16)
    out[...] = dot_tn(buf[...], eye).astype(BF16)


def attention_kernel(pool, order, tok_rows, near_rels, late, *refs):
    blocks = len(order)
    parts, refs = refs[:blocks], refs[blocks:]
    (wq, wk, wv_hbm, wo_hbm), refs = refs[:4], refs[4:]
    g_out, refs = refs[0], refs[1:]
    gts, refs = refs[: len(near_rels)], refs[len(near_rels) :]
    p_buf, c_buf, q_buf, k_buf, v_buf, ga_buf, gq_buf, gk_buf, gv_buf = refs[:9]
    probs_buf, turn, ends, wv, wo, sems = refs[9:]
    copies = start_copies(((wv_hbm, wv), (wo_hbm, wo)), sems)
    padded = parts[0].shape[0] - tok_rows - 8
    befores, afters, firsts, lasts = [], [], [], []
    for part in parts:
        tail = part[tok_rows : tok_rows + 8, :].astype(F32)
        lows = part[padded + tok_rows :, :].astype(F32)
        firsts.append(part[:8, :].astype(F32)[0:1] + lows[0:1])
        lasts.append(part[tok_rows - 8 : tok_rows, :].astype(F32)[7:8] + lows[1:2])
        befores.append(tail[0:1] + lows[2:3])
        afters.append(tail[1:2] + lows[3:4])
    extra = neighbours(lax.axis_index("ctx"), order, blocks, befores, afters, ends)
    for at, (part, first, last, (to_first, to_last)) in enumerate(zip(parts, firsts, lasts, extra)):
        value = part[:tok_rows, :].astype(F32)
        row = iota(value.shape, 0)
        value = jnp.where(row == 0, first + to_first, value)
        value = jnp.where(row == tok_rows - 1, last + to_last, value)
        here = slice(at * tok_rows, (at + 1) * tok_rows)
        p_buf[here, :] = value.astype(BF16)
        c_buf[here, :] = part[padded : padded + tok_rows, :]
    q_buf[...] = dot_nn(p_buf[...], wq[...]).astype(BF16)
    k_buf[...] = dot_nn(p_buf[...], wk[...]).astype(BF16)
    scale = 1.0 / DH**0.5
    for h in range(HEADS):
        cols = slice(h * DH, (h + 1) * DH)
        scores = dot_nt(q_buf[:, cols], k_buf[:, cols]) * scale
        expo = jnp.exp(scores - jnp.max(scores, axis=-1, keepdims=True))
        probs_buf[h] = expo / jnp.sum(expo, axis=-1, keepdims=True)
    copies[0].wait()
    v_buf[...] = dot_nn(p_buf[...], wv[...]).astype(BF16)
    copies[1].wait()
    ga_buf[...] = dot_nt(c_buf[...], wo[...]).astype(BF16)
    for h in range(HEADS):
        cols = slice(h * DH, (h + 1) * DH)
        q, k, v, ga = q_buf[:, cols], k_buf[:, cols], v_buf[:, cols], ga_buf[:, cols]
        probs = probs_buf[h]
        probs_b = probs.astype(BF16)
        out = dot_nn(probs_b, v).astype(BF16)
        delta = jnp.sum(ga.astype(F32) * out.astype(F32), axis=-1, keepdims=True)
        grad_score = (probs * (dot_nt(ga, v) - delta) * scale).astype(BF16)
        gq_buf[:, cols] = dot_nn(grad_score, k).astype(BF16)
        gk_buf[:, cols] = dot_tn(grad_score, q).astype(BF16)
        gv_buf[:, cols] = dot_tn(probs_b, ga).astype(BF16)
    grad = c_buf[...].astype(F32)
    for src, weight in ((gq_buf, wq), (gk_buf, wk), (gv_buf, wv)):
        grad = grad + dot_nt(src[...], weight[...])
    g = (grad * (1.0 / pool)).astype(BF16)
    g_out[...] = g
    tokens = g.shape[0]
    eye = (iota((tokens, tokens), 0) == iota((tokens, tokens), 1)).astype(BF16)
    turned = dot_tn(g, eye).astype(BF16)
    count = turn.shape[0]
    span = turned.shape[0] // count
    me = lax.axis_index("dp")
    for o in range(count):
        turn[o ^ me] = turned[o * span : (o + 1) * span, :]
    for gt, base in zip(gts, near_rels):
        for at, rel in enumerate(late):
            gt[at * span : (at + 1) * span, :] = turn[base ^ rel]


def spread_kernel(kernel, tok_rows, befores, afters, g_ref, weights, highs, lows, near):
    tokens = g_ref.shape[0]
    padded = near.shape[0]
    me = lax.axis_index("ctx")
    row = iota((padded, tokens), 0)
    source = jnp.where(
        row == 0, pick(me, befores), jnp.where(row == tok_rows + 1, pick(me, afters), row - 1)
    )
    source = jnp.where(row > tok_rows + 1, -1, source)
    chosen = (source == iota((padded, tokens), 1)).astype(BF16)
    rows = dot_nn(chosen, g_ref[...]).astype(BF16)
    near[...] = rows
    for j in range(kernel):
        part = slice(j * padded, (j + 1) * padded)
        highs[part, :], lows[part, :] = split2(dot_nt(rows, weights[j]))


def input_grad_kernel(
    kernel, pool, highs, lows, near, normed_ref, inv_ref, gain, out
):
    half = kernel // 2
    rows, channels = out.shape
    padded = near.shape[0]
    start = pl.program_id(0) * rows
    here = pl.ds(pl.multiple_of(start, rows), rows)
    shape = (rows, kernel * padded)
    col = iota(shape, 1)
    tap = sum((col >= padded * j).astype(jnp.int32) for j in range(1, kernel))
    token = col - tap * padded - 1
    offset = iota(shape, 0) + start - tap + half - token * pool
    spread = ((offset >= 0) & (offset < pool)).astype(BF16)
    grad_act = dot_nn(spread, highs[...]) + dot_nn(spread, lows[...])
    plain = spread[:, half * padded : (half + 1) * padded]
    grad_rows = dot_nn(plain, near[...])
    gain_f = gain[...].reshape(1, channels).astype(F32)
    unit = normed_ref[here, :]
    u = unit * gain_f
    tanh_val = gelu_of(u)[0]
    slopes = 0.5 * (1.0 + tanh_val) + 0.5 * u * (1.0 - tanh_val * tanh_val) * GELU_SCALE * (
        1.0 + 3.0 * CUBIC * (u * u)
    )
    grad_norm = grad_act * slopes * gain_f
    mean = jnp.mean(grad_norm * unit, axis=-1, keepdims=True)
    out[...] = (grad_rows + inv_ref[here, :1] * (grad_norm - unit * mean)).astype(BF16)


def cut_kernel(value, *outs):
    at = 0
    for out in outs:
        out[...] = value[at : at + out.shape[0], :]
        at += out.shape[0]


def kernel_grad_kernel(factor, begin, *refs):
    count = len(refs) // 2 - 1
    acts, gts, (mine, theirs) = refs[:count], refs[count : 2 * count], refs[2 * count :]
    span, size = mine.shape
    total = None
    for act, gt in zip(acts, gts):
        at = begin if act.shape[0] > size else 0
        term = dot_nt(gt[...], act[at : at + size, :])
        total = term if total is None else total + term
    total = total * factor
    mine[...] = total[:span, :]
    theirs[...] = total[span:, :].astype(BF16)


def fold_kernel(mine, other, kept, sent):
    span = kept.shape[0]
    kept[...] = mine[:span, :] + other[:span, :].astype(F32)
    sent[...] = (mine[span:, :] + other[span:, :].astype(F32)).astype(BF16)


def join_kernel(kernel, *refs):
    *parts, out = refs
    width = out.shape[1]
    half = len(parts) // 2
    sums = [a[...] + b[...].astype(F32) for a, b in zip(parts[:half], parts[half:])]
    total = jnp.transpose(jnp.concatenate(sums, axis=1))
    for j in range(kernel):
        out[j] = total[j * width : (j + 1) * width, :]


def xor_order(count):
    order = [0]
    bit = count // 2
    while bit:
        order = order + [v ^ bit for v in order]
        bit //= 2
    return order


def swap(value, axis, bit):
    count = lax.axis_size(axis)
    return lax.ppermute(value, axis, [(i, i ^ bit) for i in range(count)])


WHOLE = pl.BlockSpec(memory_space=pltpu.VMEM)


def call(body, args, outs, scratch=(), **options):
    options.setdefault("in_specs", [WHOLE] * len(args))
    options.setdefault("out_specs", [WHOLE] * len(outs))
    return pl.pallas_call(
        body,
        out_shape=list(outs),
        scratch_shapes=list(scratch),
        compiler_params=pltpu.CompilerParams(vmem_limit_bytes=VMEM_LIMIT),
        **options,
    )(*args)


def outside(*values):
    return [pltpu.with_memory_space_constraint(value, pltpu.HBM) for value in values]


def bits_of(count):
    return [1 << at for at in range(count.bit_length() - 1)]


def sums_of(bits):
    out = [0]
    for bit in bits:
        out = out + [bit + value for value in out]
    return out


def per_device(
    features, bases, dna_table, norm_gain, w_conv, w_query, w_key, w_value, w_out, cotangent
):
    feat, cot = features[0], cotangent[0]
    kernel = w_conv.shape[0]
    length, channels = feat.shape
    tok_rows = cot.shape[0]
    pool = length // tok_rows
    n_ctx, n_dp = lax.axis_size("ctx"), lax.axis_size("dp")
    tokens = n_ctx * tok_rows
    width = channels // n_ctx
    narrow = channels // n_dp
    near_rels = [0, X_BIT, Z_BIT, X_BIT + Z_BIT]
    late = sums_of([bit for bit in bits_of(n_dp) if bit not in (X_BIT, Z_BIT)])

    order = xor_order(n_ctx)
    place = {rel: at for at, rel in enumerate(order)}
    befores = [-1] + [place[c ^ (c - 1)] * tok_rows + tok_rows - 1 for c in range(1, n_ctx)]
    afters = [place[c ^ (c + 1)] * tok_rows for c in range(n_ctx - 1)] + [-1]

    hbm = pl.BlockSpec(memory_space=pltpu.HBM)
    block = 128
    wide = -(-(tok_rows + 2) // 8) * 8
    taps, sums, normed, inv_rms, gain_v, cot_v, w_conv_v = call(
        functools.partial(act_kernel, kernel, pool, tok_rows),
        outside(feat, bases, dna_table, norm_gain, cot, w_conv),
        [
            pltpu.VMEM((kernel * wide, channels), F32),
            pltpu.VMEM((wide, channels), F32),
            pltpu.VMEM((length, channels), F32),
            pltpu.VMEM((length, 128), F32),
            pltpu.VMEM(norm_gain.shape, BF16),
            pltpu.VMEM(cot.shape, BF16),
            pltpu.VMEM(w_conv.shape, BF16),
        ],
        [
            pltpu.VMEM(feat.shape, BF16),
            pltpu.VMEM(bases.shape, jnp.int32),
            pltpu.VMEM(dna_table.shape, BF16),
            pltpu.VMEM((length // block, block, channels), BF16),
        ]
        + [pltpu.SemaphoreType.DMA((5 + length // block,))],
        in_specs=[hbm] * 6,
    )
    pairs, *acts = call(
        functools.partial(taps_kernel, kernel, n_ctx),
        (taps,),
        [pltpu.VMEM((kernel, 2 * wide, channels), BF16)]
        + [pltpu.VMEM((wide, kernel * width), BF16)] * n_ctx,
        [pltpu.VMEM((n_ctx, wide, kernel * width), BF16)],
    )
    acts = [acts[0]] + [swap(acts[rel], "ctx", rel) for rel in order[1:]]
    pooled = call(
        functools.partial(pool_kernel, pool, tok_rows),
        (pairs, sums, w_conv_v, cot_v),
        [pltpu.VMEM((wide + tok_rows + 8, channels), BF16)],
    )[0]
    rows = [pooled]
    bit = n_ctx // 2
    while bit:
        rows = rows + [swap(value, "ctx", bit) for value in rows]
        bit //= 2

    act = call(
        functools.partial(pack_kernel, order, tok_rows),
        acts,
        [pltpu.VMEM((kernel * width, tokens), BF16)],
        [
            pltpu.VMEM((tokens, kernel * width), BF16),
            pltpu.VMEM((n_ctx + 2, 8, kernel * width), F32),
        ],
    )[0]

    act_z = swap(act, "dp", Z_BIT)
    act_x = swap(act, "dp", X_BIT)

    g_all, *gts = call(
        functools.partial(attention_kernel, pool, order, tok_rows, near_rels, late),
        [*rows, w_query, w_key] + outside(w_value, w_out),
        [pltpu.VMEM((tokens, channels), BF16)]
        + [pltpu.VMEM((len(late) * narrow, tokens), BF16)] * len(near_rels),
        [pltpu.VMEM((tokens, channels), BF16)] * 9
        + [
            pltpu.VMEM((HEADS, tokens, tokens), F32),
            pltpu.VMEM((n_dp, narrow, tokens), BF16),
            pltpu.VMEM((n_ctx + 2, 8, channels), F32),
            pltpu.VMEM(w_value.shape, BF16),
            pltpu.VMEM(w_out.shape, BF16),
            pltpu.SemaphoreType.DMA((2,)),
        ],
        in_specs=[WHOLE] * (n_ctx + 2) + [hbm] * 2,
    )

    depth = kernel * width
    cuts = [0, -(-depth // 32) * 16, depth]
    sizes = [end - begin for begin, end in zip(cuts, cuts[1:])]
    act_zx = call(cut_kernel, (act_z,), [pltpu.VMEM((size, tokens), BF16) for size in sizes])
    act_zx = list(act_zx)
    for at, value in enumerate(act_zx):
        act_zx[at] = swap(value, "dp", X_BIT)
    swapped = [gts[0]]
    for at, rel in enumerate(near_rels[1:], 1):
        swapped.append(swap(gts[at], "dp", rel))

    padded = -(-(tok_rows + 2) // 8) * 8
    highs, lows, near_g = call(
        functools.partial(spread_kernel, kernel, tok_rows, befores, afters),
        (g_all, w_conv_v),
        [pltpu.VMEM((kernel * padded, channels), BF16)] * 2
        + [pltpu.VMEM((padded, channels), BF16)],
    )
    factor = 1.0 / (n_dp * length * n_ctx) ** 0.5
    mines, others = [], []
    for at, size in enumerate(sizes):
        kept = len(late) // 2
        mine, theirs = call(
            functools.partial(kernel_grad_kernel, factor, cuts[at]),
            (act, act_x, act_z, act_zx[at], *swapped),
            [pltpu.VMEM((kept * narrow, size), F32), pltpu.VMEM((kept * narrow, size), BF16)],
        )
        other = swap(theirs, "dp", late[kept])
        while kept > 1:
            kept //= 2
            mine, theirs = call(
                fold_kernel,
                (mine, other),
                [pltpu.VMEM((kept * narrow, size), F32), pltpu.VMEM((kept * narrow, size), BF16)],
            )
            other = swap(theirs, "dp", late[kept])
        mines.append(mine)
        others.append(other)

    by_rows = pl.BlockSpec((block, channels), lambda i: (i, 0))
    grad_in = call(
        functools.partial(input_grad_kernel, kernel, pool),
        (highs, lows, near_g, normed, inv_rms, gain_v),
        [jax.ShapeDtypeStruct((length, channels), BF16)],
        grid=(length // block,),
        out_specs=[by_rows],
    )[0]
    grad_conv = call(
        functools.partial(join_kernel, kernel),
        (*mines, *others),
        [jax.ShapeDtypeStruct((kernel, width, narrow), F32)],
    )[0]
    return grad_in[None], jnp.transpose(grad_conv, (1, 0, 2))


def solution(mesh):
    in_specs = (
        P("dp", "ctx", None),
        P("dp", "ctx"),
        P(),
        P(),
        P(),
        P(),
        P(),
        P(),
        P(),
        P("dp", "ctx", None),
    )
    out_specs = (P("dp", "ctx", None), P("ctx", None, "dp"))
    return jax.shard_map(
        per_device, mesh=mesh, in_specs=in_specs, out_specs=out_specs, check_vma=False
    )
```

```python
import functools

import jax
import jax.numpy as jnp
from jax import lax
from jax.experimental import pallas as pl
from jax.experimental.pallas import tpu as pltpu
from jax.sharding import PartitionSpec as P


HEADS = 6
DH = 128

EPSILON = 1e-06
GELU_SCALE = 0.7978845608028654
CUBIC = 0.044715
F32 = jnp.float32
BF16 = jnp.bfloat16
VMEM_LIMIT = 28 << 20
FLOPS_PER_MICRO = 1.15e9
X_BIT, Z_BIT = 1, 4


def dot_nn(left, right):
    return lax.dot_general(left, right, (((1,), (0,)), ((), ())), preferred_element_type=F32)


def dot_nt(left, right):
    return lax.dot_general(left, right, (((1,), (1,)), ((), ())), preferred_element_type=F32)


def dot_tn(left, right):
    return lax.dot_general(left, right, (((0,), (0,)), ((), ())), preferred_element_type=F32)


def split2(value):
    high = value.astype(BF16)
    return high, (value - high.astype(F32)).astype(BF16)


def iota(shape, dim):
    return lax.broadcasted_iota(jnp.int32, shape, dim)


def normed_of(summed):
    inv_rms = lax.rsqrt(jnp.mean(summed * summed, axis=-1, keepdims=True) + EPSILON)
    return inv_rms, summed * inv_rms


def gelu_of(u):
    tanh_val = jnp.tanh(GELU_SCALE * (u + CUBIC * (u * u * u)))
    return tanh_val, 0.5 * u * (1.0 + tanh_val)


def pick(index, values):
    out = jnp.int32(values[0])
    for at, value in enumerate(values[1:], 1):
        out = jnp.where(index == at, jnp.int32(value), out)
    return out


def start_copies(pairs, sems):
    copies = [pltpu.make_async_copy(src, dst, sems.at[i]) for i, (src, dst) in enumerate(pairs)]
    for copy in copies:
        copy.start()
    return copies


def act_kernel(
    kernel, pool, tok_rows, feat_hbm, base_hbm, table_hbm, gain_hbm, cot_hbm,
    taps, sums, normed_out, inv_out, gain, cot, feat, base, table, act_buf, sems,
):
    half = kernel // 2
    _, channels = feat.shape
    count, block = act_buf.shape[:2]
    small = ((base_hbm, base), (table_hbm, table), (gain_hbm, gain))
    parts = tuple(
        (feat_hbm.at[pl.ds(i * block, block)], feat.at[pl.ds(i * block, block)]) for i in range(count)
    )
    copies = start_copies(small + parts + ((cot_hbm, cot),), sems)
    padded = taps.shape[0] // kernel
    for copy in copies[: len(small)]:
        copy.wait()
    gain_f = gain[...].reshape(1, channels).astype(F32)
    chunk = 32
    for step in range(count):
        start = step * block
        here = slice(start, start + block)
        copies[len(small) + step].wait()
        onehot = (iota((table.shape[0], block), 0) == base[:, here]).astype(BF16)
        embed = dot_tn(onehot, table[...])
        for begin in range(0, block, chunk):
            part = slice(begin, begin + chunk)
            some = slice(start + begin, start + begin + chunk)
            summed = feat[some, :].astype(F32) + embed[part, :]
            inv_rms, normed = normed_of(summed)
            act_buf[step, part, :] = gelu_of(normed * gain_f)[1].astype(BF16)
            normed_out[some, :] = normed
            inv_out[some, :] = jnp.broadcast_to(inv_rms, (chunk, inv_out.shape[1]))
        shape = (kernel * padded, block)
        row = iota(shape, 0)
        tap = sum((row >= padded * j).astype(jnp.int32) for j in range(1, kernel))
        token = row - tap * padded
        token = jnp.where(token == tok_rows, -1, jnp.where(token == tok_rows + 1, tok_rows, token))
        known = row - tap * padded < tok_rows + 2
        offset = iota(shape, 1) + start - tap + half - token * pool
        spread = ((offset >= 0) & (offset < pool) & known).astype(BF16)
        term = dot_nn(spread, act_buf[step])
        taps[...] = term if step == 0 else taps[...] + term
        plain = spread[half * padded : (half + 1) * padded, :]
        counts = dot_nt(plain, onehot).astype(BF16)
        term = dot_nn(plain, feat[here, :]) + dot_nn(counts, table[...])
        sums[...] = term if step == 0 else sums[...] + term

    for copy in copies[len(small) + count :]:
        copy.wait()


def taps_kernel(kernel, blocks, taps, pairs, *rest):
    outs, turn = rest[:blocks], rest[blocks]
    me = lax.axis_index("ctx")
    padded = taps.shape[0] // kernel
    highs = []
    for j in range(kernel):
        high, low = split2(taps[j * padded : (j + 1) * padded, :])
        highs.append(high)
        pairs[j] = jnp.concatenate([high, low], axis=0)
    width = taps.shape[1] // blocks
    for b in range(blocks):
        turn[b ^ me] = jnp.concatenate([h[:, b * width : (b + 1) * width] for h in highs], axis=1)
    for b in range(blocks):
        outs[b][...] = turn[b]


def pool_kernel(pool, tok_rows, pairs, sums, weights, cot, rows):
    padded = sums.shape[0]
    total = dot_nn(pairs[0], weights[0])
    for j in range(1, pairs.shape[0]):
        total = total + dot_nn(pairs[j], weights[j])
    conv = total[:padded] + total[padded:]
    value = (sums[...] + conv) * (1.0 / pool)
    high, low = split2(value)
    rows[:padded, :] = high
    rows[padded : padded + tok_rows, :] = cot[...]
    low_f = low.astype(F32)
    ends = [low_f[:1], low_f[tok_rows - 1 : tok_rows + 2]]
    ends = jnp.concatenate(ends + [jnp.zeros((4, low.shape[1]), F32)], axis=0)
    rows[padded + tok_rows :, :] = ends.astype(BF16)


def neighbours(me, order, count, befores, afters, ends):
    zero = jnp.zeros(ends.shape[1:], F32)
    ends[0] = zero
    ends[count + 1] = zero
    for rel, before, after in zip(order, befores, afters):
        owner = me ^ rel
        ends[owner + 1, 0:1, :] = before
        ends[owner + 1, 1:2, :] = after
    return [(ends[me ^ rel, 1:2, :], ends[(me ^ rel) + 2, 0:1, :]) for rel in order]


def pack_kernel(order, tok_rows, *refs):
    *parts, out, buf, ends = refs
    me = lax.axis_index("ctx")
    tails = [part[tok_rows : tok_rows + 8, :].astype(F32) for part in parts]
    extra = neighbours(
        me, order, len(parts), [tail[0:1] for tail in tails], [tail[1:2] for tail in tails], ends
    )
    for at, (part, (first, last)) in enumerate(zip(parts, extra)):
        value = part[:tok_rows, :].astype(F32)
        row = iota(value.shape, 0)
        value = value + jnp.where(row == 0, first, 0.0) + jnp.where(row == tok_rows - 1, last, 0.0)
        buf[at * tok_rows : (at + 1) * tok_rows, :] = value.astype(BF16)
    total = buf.shape[0]
    eye = (iota((total, total), 0) == iota((total, total), 1)).astype(BF16)
    out[...] = dot_tn(buf[...], eye).astype(BF16)


def attention_kernel(pool, order, tok_rows, near_rels, late, *refs):
    blocks = len(order)
    parts, refs = refs[:blocks], refs[blocks:]
    (wq, wk, wv_hbm, wo_hbm), refs = refs[:4], refs[4:]
    g_out, refs = refs[0], refs[1:]
    gts, refs = refs[: len(near_rels)], refs[len(near_rels) :]
    p_buf, c_buf, q_buf, k_buf, v_buf, ga_buf, gq_buf, gk_buf, gv_buf = refs[:9]
    probs_buf, turn, ends, wv, wo, sems = refs[9:]
    copies = start_copies(((wv_hbm, wv), (wo_hbm, wo)), sems)
    padded = parts[0].shape[0] - tok_rows - 8
    befores, afters, firsts, lasts = [], [], [], []
    for part in parts:
        tail = part[tok_rows : tok_rows + 8, :].astype(F32)
        lows = part[padded + tok_rows :, :].astype(F32)
        firsts.append(part[:8, :].astype(F32)[0:1] + lows[0:1])
        lasts.append(part[tok_rows - 8 : tok_rows, :].astype(F32)[7:8] + lows[1:2])
        befores.append(tail[0:1] + lows[2:3])
        afters.append(tail[1:2] + lows[3:4])
    extra = neighbours(lax.axis_index("ctx"), order, blocks, befores, afters, ends)
    for at, (part, first, last, (to_first, to_last)) in enumerate(zip(parts, firsts, lasts, extra)):
        value = part[:tok_rows, :].astype(F32)
        row = iota(value.shape, 0)
        value = jnp.where(row == 0, first + to_first, value)
        value = jnp.where(row == tok_rows - 1, last + to_last, value)
        here = slice(at * tok_rows, (at + 1) * tok_rows)
        p_buf[here, :] = value.astype(BF16)
        c_buf[here, :] = part[padded : padded + tok_rows, :]
    q_buf[...] = dot_nn(p_buf[...], wq[...]).astype(BF16)
    k_buf[...] = dot_nn(p_buf[...], wk[...]).astype(BF16)
    scale = 1.0 / DH**0.5
    for h in range(HEADS):
        cols = slice(h * DH, (h + 1) * DH)
        scores = dot_nt(q_buf[:, cols], k_buf[:, cols]) * scale
        expo = jnp.exp(scores - jnp.max(scores, axis=-1, keepdims=True))
        probs_buf[h] = expo / jnp.sum(expo, axis=-1, keepdims=True)
    copies[0].wait()
    v_buf[...] = dot_nn(p_buf[...], wv[...]).astype(BF16)
    copies[1].wait()
    ga_buf[...] = dot_nt(c_buf[...], wo[...]).astype(BF16)
    for h in range(HEADS):
        cols = slice(h * DH, (h + 1) * DH)
        q, k, v, ga = q_buf[:, cols], k_buf[:, cols], v_buf[:, cols], ga_buf[:, cols]
        probs = probs_buf[h]
        probs_b = probs.astype(BF16)
        out = dot_nn(probs_b, v).astype(BF16)
        delta = jnp.sum(ga.astype(F32) * out.astype(F32), axis=-1, keepdims=True)
        grad_score = (probs * (dot_nt(ga, v) - delta) * scale).astype(BF16)
        gq_buf[:, cols] = dot_nn(grad_score, k).astype(BF16)
        gk_buf[:, cols] = dot_tn(grad_score, q).astype(BF16)
        gv_buf[:, cols] = dot_tn(probs_b, ga).astype(BF16)
    grad = c_buf[...].astype(F32)
    for src, weight in ((gq_buf, wq), (gk_buf, wk), (gv_buf, wv)):
        grad = grad + dot_nt(src[...], weight[...])
    g = (grad * (1.0 / pool)).astype(BF16)
    g_out[...] = g
    tokens = g.shape[0]
    eye = (iota((tokens, tokens), 0) == iota((tokens, tokens), 1)).astype(BF16)
    turned = dot_tn(g, eye).astype(BF16)
    count = turn.shape[0]
    span = turned.shape[0] // count
    me = lax.axis_index("dp")
    for o in range(count):
        turn[o ^ me] = turned[o * span : (o + 1) * span, :]
    for gt, base in zip(gts, near_rels):
        for at, rel in enumerate(late):
            gt[at * span : (at + 1) * span, :] = turn[base ^ rel]


def spread_kernel(kernel, tok_rows, befores, afters, g_ref, weights, highs, lows, near):
    tokens = g_ref.shape[0]
    padded = near.shape[0]
    me = lax.axis_index("ctx")
    row = iota((padded, tokens), 0)
    source = jnp.where(
        row == 0, pick(me, befores), jnp.where(row == tok_rows + 1, pick(me, afters), row - 1)
    )
    source = jnp.where(row > tok_rows + 1, -1, source)
    chosen = (source == iota((padded, tokens), 1)).astype(BF16)
    rows = dot_nn(chosen, g_ref[...]).astype(BF16)
    near[...] = rows
    for j in range(kernel):
        part = slice(j * padded, (j + 1) * padded)
        highs[part, :], lows[part, :] = split2(dot_nt(rows, weights[j]))


def input_grad_kernel(
    kernel, pool, highs, lows, near, normed_ref, inv_ref, gain, out
):
    half = kernel // 2
    rows, channels = out.shape
    padded = near.shape[0]
    start = pl.program_id(0) * rows
    here = pl.ds(pl.multiple_of(start, rows), rows)
    shape = (rows, kernel * padded)
    col = iota(shape, 1)
    tap = sum((col >= padded * j).astype(jnp.int32) for j in range(1, kernel))
    token = col - tap * padded - 1
    offset = iota(shape, 0) + start - tap + half - token * pool
    spread = ((offset >= 0) & (offset < pool)).astype(BF16)
    grad_act = dot_nn(spread, highs[...]) + dot_nn(spread, lows[...])
    plain = spread[:, half * padded : (half + 1) * padded]
    grad_rows = dot_nn(plain, near[...])
    gain_f = gain[...].reshape(1, channels).astype(F32)
    unit = normed_ref[here, :]
    u = unit * gain_f
    tanh_val = gelu_of(u)[0]
    slopes = 0.5 * (1.0 + tanh_val) + 0.5 * u * (1.0 - tanh_val * tanh_val) * GELU_SCALE * (
        1.0 + 3.0 * CUBIC * (u * u)
    )
    grad_norm = grad_act * slopes * gain_f
    mean = jnp.mean(grad_norm * unit, axis=-1, keepdims=True)
    out[...] = (grad_rows + inv_ref[here, :1] * (grad_norm - unit * mean)).astype(BF16)


def cut_kernel(value, *outs):
    at = 0
    for out in outs:
        out[...] = value[at : at + out.shape[0], :]
        at += out.shape[0]


def kernel_grad_kernel(factor, begin, *refs):
    count = len(refs) // 2 - 1
    acts, gts, (mine, theirs) = refs[:count], refs[count : 2 * count], refs[2 * count :]
    span, size = mine.shape
    total = None
    for act, gt in zip(acts, gts):
        at = begin if act.shape[0] > size else 0
        term = dot_nt(gt[...], act[at : at + size, :])
        total = term if total is None else total + term
    total = total * factor
    mine[...] = total[:span, :]
    theirs[...] = total[span:, :].astype(BF16)


def fold_kernel(mine, other, kept, sent):
    span = kept.shape[0]
    kept[...] = mine[:span, :] + other[:span, :].astype(F32)
    sent[...] = (mine[span:, :] + other[span:, :].astype(F32)).astype(BF16)


def join_kernel(kernel, *refs):
    *parts, out = refs
    width = out.shape[1]
    half = len(parts) // 2
    sums = [a[...] + b[...].astype(F32) for a, b in zip(parts[:half], parts[half:])]
    total = jnp.transpose(jnp.concatenate(sums, axis=1))
    for j in range(kernel):
        out[j] = total[j * width : (j + 1) * width, :]


def xor_order(count):
    order = [0]
    bit = count // 2
    while bit:
        order = order + [v ^ bit for v in order]
        bit //= 2
    return order


def swap(value, axis, bit):
    count = lax.axis_size(axis)
    return lax.ppermute(value, axis, [(i, i ^ bit) for i in range(count)])


WHOLE = pl.BlockSpec(memory_space=pltpu.VMEM)


def call(body, args, outs, scratch=(), micros=1, **options):
    options.setdefault("in_specs", [WHOLE] * len(args))
    options.setdefault("out_specs", [WHOLE] * len(outs))
    return pl.pallas_call(
        body,
        out_shape=list(outs),
        scratch_shapes=list(scratch),
        compiler_params=pltpu.CompilerParams(vmem_limit_bytes=VMEM_LIMIT),
        cost_estimate=pl.CostEstimate(
            flops=int(micros * FLOPS_PER_MICRO), bytes_accessed=0, transcendentals=0
        ),
        **options,
    )(*args)


def outside(*values):
    return [pltpu.with_memory_space_constraint(value, pltpu.HBM) for value in values]


def bits_of(count):
    return [1 << at for at in range(count.bit_length() - 1)]


def sums_of(bits):
    out = [0]
    for bit in bits:
        out = out + [bit + value for value in out]
    return out


def per_device(
    features, bases, dna_table, norm_gain, w_conv, w_query, w_key, w_value, w_out, cotangent
):
    feat, cot = features[0], cotangent[0]
    kernel = w_conv.shape[0]
    length, channels = feat.shape
    tok_rows = cot.shape[0]
    pool = length // tok_rows
    n_ctx, n_dp = lax.axis_size("ctx"), lax.axis_size("dp")
    tokens = n_ctx * tok_rows
    width = channels // n_ctx
    narrow = channels // n_dp
    near_rels = [0, X_BIT, Z_BIT, X_BIT + Z_BIT]
    late = sums_of([bit for bit in bits_of(n_dp) if bit not in (X_BIT, Z_BIT)])

    order = xor_order(n_ctx)
    place = {rel: at for at, rel in enumerate(order)}
    befores = [-1] + [place[c ^ (c - 1)] * tok_rows + tok_rows - 1 for c in range(1, n_ctx)]
    afters = [place[c ^ (c + 1)] * tok_rows for c in range(n_ctx - 1)] + [-1]

    hbm = pl.BlockSpec(memory_space=pltpu.HBM)
    block = 128
    wide = -(-(tok_rows + 2) // 8) * 8
    taps, sums, normed, inv_rms, gain_v, cot_v = call(
        functools.partial(act_kernel, kernel, pool, tok_rows),
        outside(feat, bases, dna_table, norm_gain, cot),
        [
            pltpu.VMEM((kernel * wide, channels), F32),
            pltpu.VMEM((wide, channels), F32),
            pltpu.VMEM((length, channels), F32),
            pltpu.VMEM((length, 128), F32),
            pltpu.VMEM(norm_gain.shape, BF16),
            pltpu.VMEM(cot.shape, BF16),
        ],
        [
            pltpu.VMEM(feat.shape, BF16),
            pltpu.VMEM(bases.shape, jnp.int32),
            pltpu.VMEM(dna_table.shape, BF16),
            pltpu.VMEM((length // block, block, channels), BF16),
        ]
        + [pltpu.SemaphoreType.DMA((4 + length // block,))],
        in_specs=[hbm] * 5,
        micros=3,
    )
    pairs, *acts = call(
        functools.partial(taps_kernel, kernel, n_ctx),
        (taps,),
        [pltpu.VMEM((kernel, 2 * wide, channels), BF16)]
        + [pltpu.VMEM((wide, kernel * width), BF16)] * n_ctx,
        [pltpu.VMEM((n_ctx, wide, kernel * width), BF16)],
    )
    swapped = [acts[0]]
    for rel in order[1:]:
        swapped.append(swap(acts[rel], "ctx", rel))
    acts = swapped
    pooled = call(
        functools.partial(pool_kernel, pool, tok_rows),
        (pairs, sums, w_conv, cot_v),
        [pltpu.VMEM((wide + tok_rows + 8, channels), BF16)],
    )[0]
    rows = [pooled]
    bit = n_ctx // 2
    while bit:
        rows = rows + [swap(value, "ctx", bit) for value in rows]
        bit //= 2

    act = call(
        functools.partial(pack_kernel, order, tok_rows),
        acts,
        [pltpu.VMEM((kernel * width, tokens), BF16)],
        [
            pltpu.VMEM((tokens, kernel * width), BF16),
            pltpu.VMEM((n_ctx + 2, 8, kernel * width), F32),
        ],
    )[0]

    act_z = swap(act, "dp", Z_BIT)
    act_x = swap(act, "dp", X_BIT)

    g_all, *gts = call(
        functools.partial(attention_kernel, pool, order, tok_rows, near_rels, late),
        [*rows, w_query, w_key] + outside(w_value, w_out),
        [pltpu.VMEM((tokens, channels), BF16)]
        + [pltpu.VMEM((len(late) * narrow, tokens), BF16)] * len(near_rels),
        [pltpu.VMEM((tokens, channels), BF16)] * 9
        + [
            pltpu.VMEM((HEADS, tokens, tokens), F32),
            pltpu.VMEM((n_dp, narrow, tokens), BF16),
            pltpu.VMEM((n_ctx + 2, 8, channels), F32),
            pltpu.VMEM(w_value.shape, BF16),
            pltpu.VMEM(w_out.shape, BF16),
            pltpu.SemaphoreType.DMA((2,)),
        ],
        in_specs=[WHOLE] * (n_ctx + 2) + [hbm] * 2,
        micros=5,
    )

    depth = kernel * width
    cuts = [0, -(-depth // 32) * 16, depth]
    sizes = [end - begin for begin, end in zip(cuts, cuts[1:])]
    act_zx = call(cut_kernel, (act_z,), [pltpu.VMEM((size, tokens), BF16) for size in sizes])
    act_zx = list(act_zx)
    for at, value in enumerate(act_zx):
        act_zx[at] = swap(value, "dp", X_BIT)
    swapped = [gts[0]]
    for at, rel in enumerate(near_rels[1:], 1):
        swapped.append(swap(gts[at], "dp", rel))

    padded = -(-(tok_rows + 2) // 8) * 8
    highs, lows, near_g = call(
        functools.partial(spread_kernel, kernel, tok_rows, befores, afters),
        (g_all, w_conv),
        [pltpu.VMEM((kernel * padded, channels), BF16)] * 2
        + [pltpu.VMEM((padded, channels), BF16)],
    )
    factor = 1.0 / (n_dp * length * n_ctx) ** 0.5
    mines, others = [], []
    for at, size in enumerate(sizes):
        kept = len(late) // 2
        mine, theirs = call(
            functools.partial(kernel_grad_kernel, factor, cuts[at]),
            (act, act_x, act_z, act_zx[at], *swapped),
            [pltpu.VMEM((kept * narrow, size), F32), pltpu.VMEM((kept * narrow, size), BF16)],
        )
        other = swap(theirs, "dp", late[kept])
        while kept > 1:
            kept //= 2
            mine, theirs = call(
                fold_kernel,
                (mine, other),
                [pltpu.VMEM((kept * narrow, size), F32), pltpu.VMEM((kept * narrow, size), BF16)],
            )
            other = swap(theirs, "dp", late[kept])
        mines.append(mine)
        others.append(other)

    by_rows = pl.BlockSpec((block, channels), lambda i: (i, 0))
    grad_in = call(
        functools.partial(input_grad_kernel, kernel, pool),
        (highs, lows, near_g, normed, inv_rms, gain_v),
        [jax.ShapeDtypeStruct((length, channels), BF16)],
        grid=(length // block,),
        out_specs=[by_rows],
    )[0]
    grad_conv = call(
        functools.partial(join_kernel, kernel),
        (*mines, *others),
        [jax.ShapeDtypeStruct((kernel, width, narrow), F32)],
    )[0]
    return grad_in[None], jnp.transpose(grad_conv, (1, 0, 2))


def solution(mesh):
    in_specs = (
        P("dp", "ctx", None),
        P("dp", "ctx"),
        P(),
        P(),
        P(),
        P(),
        P(),
        P(),
        P(),
        P("dp", "ctx", None),
    )
    out_specs = (P("dp", "ctx", None), P("ctx", None, "dp"))
    return jax.shard_map(
        per_device, mesh=mesh, in_specs=in_specs, out_specs=out_specs, check_vma=False
    )
```

```python
import functools

import jax
import jax.numpy as jnp
from jax import lax
from jax.experimental import pallas as pl
from jax.experimental.pallas import tpu as pltpu
from jax.sharding import PartitionSpec as P


HEADS = 6
DH = 128

EPSILON = 1e-06
GELU_SCALE = 0.7978845608028654
CUBIC = 0.044715
F32 = jnp.float32
BF16 = jnp.bfloat16
VMEM_LIMIT = 28 << 20
FLOPS_PER_MICRO = 1.15e9
X_BIT, Z_BIT = 1, 4
BLOCK = 128


def dot_nn(left, right):
    return lax.dot_general(left, right, (((1,), (0,)), ((), ())), preferred_element_type=F32)


def dot_nt(left, right):
    return lax.dot_general(left, right, (((1,), (1,)), ((), ())), preferred_element_type=F32)


def dot_tn(left, right):
    return lax.dot_general(left, right, (((0,), (0,)), ((), ())), preferred_element_type=F32)


def split2(value):
    high = value.astype(BF16)
    return high, (value - high.astype(F32)).astype(BF16)


def iota(shape, dim):
    return lax.broadcasted_iota(jnp.int32, shape, dim)


def normed_of(summed):
    inv_rms = lax.rsqrt(jnp.mean(summed * summed, axis=-1, keepdims=True) + EPSILON)
    return inv_rms, summed * inv_rms


def gelu_of(u):
    tanh_val = jnp.tanh(GELU_SCALE * (u + CUBIC * (u * u * u)))
    return tanh_val, 0.5 * u * (1.0 + tanh_val)


def pick(index, values):
    out = jnp.int32(values[0])
    for at, value in enumerate(values[1:], 1):
        out = jnp.where(index == at, jnp.int32(value), out)
    return out


def start_copies(pairs, sems):
    copies = [pltpu.make_async_copy(src, dst, sems.at[i]) for i, (src, dst) in enumerate(pairs)]
    for copy in copies:
        copy.start()
    return copies


def act_kernel(
    kernel, pool, tok_rows, feat_hbm, base_hbm, table_hbm, gain_hbm, cot_hbm,
    taps, sums, normed_out, inv_out, gain, cot, feat, base, table, act_buf, spread, embed, sems,
):
    half = kernel // 2
    rows, channels = feat.shape
    block = BLOCK
    count = rows // block
    small = ((base_hbm, base), (table_hbm, table), (gain_hbm, gain))
    parts = tuple(
        (feat_hbm.at[pl.ds(i * block, block)], feat.at[pl.ds(i * block, block)]) for i in range(count)
    )
    copies = start_copies(small + parts + ((cot_hbm, cot),), sems)
    padded = taps.shape[0] // kernel
    shape = (kernel * padded, rows)
    row = iota(shape, 0)
    tap = sum((row >= padded * j).astype(jnp.int32) for j in range(1, kernel))
    token = row - tap * padded
    known = token < tok_rows + 2
    token = jnp.where(token == tok_rows, -1, jnp.where(token == tok_rows + 1, tok_rows, token))
    offset = iota(shape, 1) - tap + half - token * pool
    spread[...] = ((offset >= 0) & (offset < pool) & known).astype(BF16)
    for copy in copies[: len(small)]:
        copy.wait()
    gain_f = gain[...].reshape(1, channels).astype(F32)
    onehot = (iota((table.shape[0], rows), 0) == base[...]).astype(BF16)
    embed[...] = dot_tn(onehot, table[...])
    for copy in copies[len(small) : len(small) + count]:
        copy.wait()

    summed = feat[...].astype(F32) + embed[...]
    inv_rms, normed = normed_of(summed)
    act_buf[...] = gelu_of(normed * gain_f)[1].astype(BF16)
    normed_out[...] = normed
    inv_out[...] = jnp.broadcast_to(inv_rms, inv_out.shape)
    taps[...] = dot_nn(spread[...], act_buf[...])
    plain = spread[half * padded : (half + 1) * padded, :]
    counts = dot_nt(plain, onehot).astype(BF16)
    sums[...] = dot_nn(plain, feat[...]) + dot_nn(counts, table[...])

    for copy in copies[len(small) + count :]:
        copy.wait()


def taps_kernel(kernel, blocks, taps, pairs, *rest):
    outs, turn = rest[:blocks], rest[blocks]
    me = lax.axis_index("ctx")
    padded = taps.shape[0] // kernel
    highs = []
    for j in range(kernel):
        high, low = split2(taps[j * padded : (j + 1) * padded, :])
        highs.append(high)
        pairs[j] = jnp.concatenate([high, low], axis=0)
    width = taps.shape[1] // blocks
    for b in range(blocks):
        turn[b ^ me] = jnp.concatenate([h[:, b * width : (b + 1) * width] for h in highs], axis=1)
    for b in range(blocks):
        outs[b][...] = turn[b]


def pool_kernel(pool, tok_rows, pairs, sums, weights, cot, rows):
    padded = sums.shape[0]
    total = dot_nn(pairs[0], weights[0])
    for j in range(1, pairs.shape[0]):
        total = total + dot_nn(pairs[j], weights[j])
    conv = total[:padded] + total[padded:]
    value = (sums[...] + conv) * (1.0 / pool)
    high, low = split2(value)
    rows[:padded, :] = high
    rows[padded : padded + tok_rows, :] = cot[...]
    low_f = low.astype(F32)
    ends = [low_f[:1], low_f[tok_rows - 1 : tok_rows + 2]]
    ends = jnp.concatenate(ends + [jnp.zeros((4, low.shape[1]), F32)], axis=0)
    rows[padded + tok_rows :, :] = ends.astype(BF16)


def neighbours(me, order, count, befores, afters, ends):
    zero = jnp.zeros(ends.shape[1:], F32)
    ends[0] = zero
    ends[count + 1] = zero
    for rel, before, after in zip(order, befores, afters):
        owner = me ^ rel
        ends[owner + 1, 0:1, :] = before
        ends[owner + 1, 1:2, :] = after
    return [(ends[me ^ rel, 1:2, :], ends[(me ^ rel) + 2, 0:1, :]) for rel in order]


def pack_kernel(order, tok_rows, *refs):
    *parts, out, buf, ends = refs
    me = lax.axis_index("ctx")
    tails = [part[tok_rows : tok_rows + 8, :].astype(F32) for part in parts]
    extra = neighbours(
        me, order, len(parts), [tail[0:1] for tail in tails], [tail[1:2] for tail in tails], ends
    )
    for at, (part, (first, last)) in enumerate(zip(parts, extra)):
        value = part[:tok_rows, :].astype(F32)
        row = iota(value.shape, 0)
        value = value + jnp.where(row == 0, first, 0.0) + jnp.where(row == tok_rows - 1, last, 0.0)
        buf[at * tok_rows : (at + 1) * tok_rows, :] = value.astype(BF16)
    total = buf.shape[0]
    eye = (iota((total, total), 0) == iota((total, total), 1)).astype(BF16)
    out[...] = dot_tn(buf[...], eye).astype(BF16)


def attention_kernel(pool, order, tok_rows, near_rels, late, *refs):
    blocks = len(order)
    parts, refs = refs[:blocks], refs[blocks:]
    (wq, wk, wv_hbm, wo_hbm), refs = refs[:4], refs[4:]
    g_out, refs = refs[0], refs[1:]
    gts, refs = refs[: len(near_rels)], refs[len(near_rels) :]
    p_buf, c_buf, q_buf, k_buf, v_buf, ga_buf, gq_buf, gk_buf, gv_buf = refs[:9]
    probs_buf, turn, ends, wv, wo, sems = refs[9:]
    copies = start_copies(((wv_hbm, wv), (wo_hbm, wo)), sems)
    padded = parts[0].shape[0] - tok_rows - 8
    befores, afters, firsts, lasts = [], [], [], []
    for part in parts:
        tail = part[tok_rows : tok_rows + 8, :].astype(F32)
        lows = part[padded + tok_rows :, :].astype(F32)
        firsts.append(part[:8, :].astype(F32)[0:1] + lows[0:1])
        lasts.append(part[tok_rows - 8 : tok_rows, :].astype(F32)[7:8] + lows[1:2])
        befores.append(tail[0:1] + lows[2:3])
        afters.append(tail[1:2] + lows[3:4])
    extra = neighbours(lax.axis_index("ctx"), order, blocks, befores, afters, ends)
    for at, (part, first, last, (to_first, to_last)) in enumerate(zip(parts, firsts, lasts, extra)):
        value = part[:tok_rows, :].astype(F32)
        row = iota(value.shape, 0)
        value = jnp.where(row == 0, first + to_first, value)
        value = jnp.where(row == tok_rows - 1, last + to_last, value)
        here = slice(at * tok_rows, (at + 1) * tok_rows)
        p_buf[here, :] = value.astype(BF16)
        c_buf[here, :] = part[padded : padded + tok_rows, :]
    q_buf[...] = dot_nn(p_buf[...], wq[...]).astype(BF16)
    k_buf[...] = dot_nn(p_buf[...], wk[...]).astype(BF16)
    scale = 1.0 / DH**0.5
    for h in range(HEADS):
        cols = slice(h * DH, (h + 1) * DH)
        scores = dot_nt(k_buf[:, cols], q_buf[:, cols]) * scale
        expo = jnp.exp(scores - jnp.max(scores, axis=0, keepdims=True))
        probs_buf[h] = expo / jnp.sum(expo, axis=0, keepdims=True)
    copies[0].wait()
    v_buf[...] = dot_nn(p_buf[...], wv[...]).astype(BF16)
    copies[1].wait()
    ga_buf[...] = dot_nt(wo[...], c_buf[...]).astype(BF16)
    for h in range(HEADS):
        cols = slice(h * DH, (h + 1) * DH)
        q, k, v, ga = q_buf[:, cols], k_buf[:, cols], v_buf[:, cols], ga_buf[cols, :]
        probs = probs_buf[h]
        probs_b = probs.astype(BF16)
        out = dot_tn(v, probs_b).astype(BF16)
        delta = jnp.sum(ga.astype(F32) * out.astype(F32), axis=0, keepdims=True)
        grad_score = (probs * (dot_nn(v, ga) - delta) * scale).astype(BF16)
        gq_buf[:, cols] = dot_tn(grad_score, k).astype(BF16)
        gk_buf[:, cols] = dot_nn(grad_score, q).astype(BF16)
        gv_buf[:, cols] = dot_nt(probs_b, ga).astype(BF16)
    grad = jnp.transpose(c_buf[...].astype(F32))
    for src, weight in ((gq_buf, wq), (gk_buf, wk), (gv_buf, wv)):
        grad = grad + dot_nt(weight[...], src[...])
    turned = (grad * (1.0 / pool)).astype(BF16)
    g_out[...] = turned
    count = turn.shape[0]
    span = turned.shape[0] // count
    me = lax.axis_index("dp")
    for o in range(count):
        turn[o ^ me] = turned[o * span : (o + 1) * span, :]
    for gt, base in zip(gts, near_rels):
        for at, rel in enumerate(late):
            gt[at * span : (at + 1) * span, :] = turn[base ^ rel]


def spread_kernel(kernel, tok_rows, befores, afters, g_ref, weights, highs, lows, near):
    tokens = g_ref.shape[1]
    padded = near.shape[0]
    me = lax.axis_index("ctx")
    row = iota((padded, tokens), 0)
    source = jnp.where(
        row == 0, pick(me, befores), jnp.where(row == tok_rows + 1, pick(me, afters), row - 1)
    )
    source = jnp.where(row > tok_rows + 1, -1, source)
    chosen = (source == iota((padded, tokens), 1)).astype(BF16)
    rows = dot_nt(chosen, g_ref[...]).astype(BF16)
    near[...] = rows
    for j in range(kernel):
        part = slice(j * padded, (j + 1) * padded)
        highs[part, :], lows[part, :] = split2(dot_nt(rows, weights[j]))


def input_grad_kernel(
    kernel, pool, highs, lows, near, normed_ref, inv_ref, gain, out
):
    half = kernel // 2
    rows, channels = out.shape
    padded = near.shape[0]
    start = pl.program_id(0) * rows
    here = pl.ds(pl.multiple_of(start, rows), rows)
    shape = (rows, kernel * padded)
    col = iota(shape, 1)
    tap = sum((col >= padded * j).astype(jnp.int32) for j in range(1, kernel))
    token = col - tap * padded - 1
    offset = iota(shape, 0) + start - tap + half - token * pool
    spread = ((offset >= 0) & (offset < pool)).astype(BF16)
    grad_act = dot_nn(spread, highs[...]) + dot_nn(spread, lows[...])
    plain = spread[:, half * padded : (half + 1) * padded]
    grad_rows = dot_nn(plain, near[...])
    gain_f = gain[...].reshape(1, channels).astype(F32)
    unit = normed_ref[here, :]
    u = unit * gain_f
    tanh_val = gelu_of(u)[0]
    slopes = 0.5 * (1.0 + tanh_val) + 0.5 * u * (1.0 - tanh_val * tanh_val) * GELU_SCALE * (
        1.0 + 3.0 * CUBIC * (u * u)
    )
    grad_norm = grad_act * slopes * gain_f
    mean = jnp.mean(grad_norm * unit, axis=-1, keepdims=True)
    out[...] = (grad_rows + inv_ref[here, :1] * (grad_norm - unit * mean)).astype(BF16)


def cut_kernel(value, *outs):
    at = 0
    for out in outs:
        out[...] = value[at : at + out.shape[0], :]
        at += out.shape[0]


def kernel_grad_kernel(factor, begin, *refs):
    count = len(refs) // 2 - 1
    acts, gts, (mine, theirs) = refs[:count], refs[count : 2 * count], refs[2 * count :]
    span, size = mine.shape
    total = None
    for act, gt in zip(acts, gts):
        at = begin if act.shape[0] > size else 0
        term = dot_nt(gt[...], act[at : at + size, :])
        total = term if total is None else total + term
    total = total * factor
    mine[...] = total[:span, :]
    theirs[...] = total[span:, :].astype(BF16)


def fold_kernel(mine, other, kept, sent):
    span = kept.shape[0]
    kept[...] = mine[:span, :] + other[:span, :].astype(F32)
    sent[...] = (mine[span:, :] + other[span:, :].astype(F32)).astype(BF16)


def join_kernel(kernel, *refs):
    *parts, out = refs
    width = out.shape[1]
    half = len(parts) // 2
    sums = [a[...] + b[...].astype(F32) for a, b in zip(parts[:half], parts[half:])]
    total = jnp.transpose(jnp.concatenate(sums, axis=1))
    for j in range(kernel):
        out[j] = total[j * width : (j + 1) * width, :]


def xor_order(count):
    order = [0]
    bit = count // 2
    while bit:
        order = order + [v ^ bit for v in order]
        bit //= 2
    return order


def swap(value, axis, bit):
    count = lax.axis_size(axis)
    return lax.ppermute(value, axis, [(i, i ^ bit) for i in range(count)])


WHOLE = pl.BlockSpec(memory_space=pltpu.VMEM)


def call(body, args, outs, scratch=(), micros=1, **options):
    options.setdefault("in_specs", [WHOLE] * len(args))
    options.setdefault("out_specs", [WHOLE] * len(outs))
    return pl.pallas_call(
        body,
        out_shape=list(outs),
        scratch_shapes=list(scratch),
        compiler_params=pltpu.CompilerParams(vmem_limit_bytes=VMEM_LIMIT),
        cost_estimate=pl.CostEstimate(
            flops=int(micros * FLOPS_PER_MICRO), bytes_accessed=0, transcendentals=0
        ),
        **options,
    )(*args)


def outside(*values):
    return [pltpu.with_memory_space_constraint(value, pltpu.HBM) for value in values]


def bits_of(count):
    return [1 << at for at in range(count.bit_length() - 1)]


def sums_of(bits):
    out = [0]
    for bit in bits:
        out = out + [bit + value for value in out]
    return out


def per_device(
    features, bases, dna_table, norm_gain, w_conv, w_query, w_key, w_value, w_out, cotangent
):
    feat, cot = features[0], cotangent[0]
    kernel = w_conv.shape[0]
    length, channels = feat.shape
    tok_rows = cot.shape[0]
    pool = length // tok_rows
    n_ctx, n_dp = lax.axis_size("ctx"), lax.axis_size("dp")
    tokens = n_ctx * tok_rows
    width = channels // n_ctx
    narrow = channels // n_dp
    near_rels = [0, X_BIT, Z_BIT, X_BIT + Z_BIT]
    late = sums_of([bit for bit in bits_of(n_dp) if bit not in (X_BIT, Z_BIT)])

    order = xor_order(n_ctx)
    place = {rel: at for at, rel in enumerate(order)}
    befores = [-1] + [place[c ^ (c - 1)] * tok_rows + tok_rows - 1 for c in range(1, n_ctx)]
    afters = [place[c ^ (c + 1)] * tok_rows for c in range(n_ctx - 1)] + [-1]

    hbm = pl.BlockSpec(memory_space=pltpu.HBM)
    block = BLOCK
    wide = -(-(tok_rows + 2) // 8) * 8
    taps, sums, normed, inv_rms, gain_v, cot_v = call(
        functools.partial(act_kernel, kernel, pool, tok_rows),
        outside(feat, bases, dna_table, norm_gain, cot),
        [
            pltpu.VMEM((kernel * wide, channels), F32),
            pltpu.VMEM((wide, channels), F32),
            pltpu.VMEM((length, channels), F32),
            pltpu.VMEM((length, 128), F32),
            pltpu.VMEM(norm_gain.shape, BF16),
            pltpu.VMEM(cot.shape, BF16),
        ],
        [
            pltpu.VMEM(feat.shape, BF16),
            pltpu.VMEM(bases.shape, jnp.int32),
            pltpu.VMEM(dna_table.shape, BF16),
            pltpu.VMEM(feat.shape, BF16),
            pltpu.VMEM((kernel * wide, length), BF16),
            pltpu.VMEM((length, channels), F32),
        ]
        + [pltpu.SemaphoreType.DMA((4 + length // block,))],
        in_specs=[hbm] * 5,
        micros=3,
    )
    pairs, *acts = call(
        functools.partial(taps_kernel, kernel, n_ctx),
        (taps,),
        [pltpu.VMEM((kernel, 2 * wide, channels), BF16)]
        + [pltpu.VMEM((wide, kernel * width), BF16)] * n_ctx,
        [pltpu.VMEM((n_ctx, wide, kernel * width), BF16)],
    )
    swapped = [acts[0]]
    for rel in order[1:]:
        swapped.append(swap(acts[rel], "ctx", rel))
    acts = swapped
    pooled = call(
        functools.partial(pool_kernel, pool, tok_rows),
        (pairs, sums, w_conv, cot_v),
        [pltpu.VMEM((wide + tok_rows + 8, channels), BF16)],
    )[0]
    rows = [pooled]
    bit = n_ctx // 2
    while bit:
        rows = rows + [swap(value, "ctx", bit) for value in rows]
        bit //= 2

    act = call(
        functools.partial(pack_kernel, order, tok_rows),
        acts,
        [pltpu.VMEM((kernel * width, tokens), BF16)],
        [
            pltpu.VMEM((tokens, kernel * width), BF16),
            pltpu.VMEM((n_ctx + 2, 8, kernel * width), F32),
        ],
    )[0]

    act_z = swap(act, "dp", Z_BIT)
    act_x = swap(act, "dp", X_BIT)

    g_all, *gts = call(
        functools.partial(attention_kernel, pool, order, tok_rows, near_rels, late),
        [*rows, w_query, w_key] + outside(w_value, w_out),
        [pltpu.VMEM((channels, tokens), BF16)]
        + [pltpu.VMEM((len(late) * narrow, tokens), BF16)] * len(near_rels),
        [pltpu.VMEM((tokens, channels), BF16)] * 5
        + [pltpu.VMEM((channels, tokens), BF16)]
        + [pltpu.VMEM((tokens, channels), BF16)] * 3
        + [
            pltpu.VMEM((HEADS, tokens, tokens), F32),
            pltpu.VMEM((n_dp, narrow, tokens), BF16),
            pltpu.VMEM((n_ctx + 2, 8, channels), F32),
            pltpu.VMEM(w_value.shape, BF16),
            pltpu.VMEM(w_out.shape, BF16),
            pltpu.SemaphoreType.DMA((2,)),
        ],
        in_specs=[WHOLE] * (n_ctx + 2) + [hbm] * 2,
        micros=5,
    )

    depth = kernel * width
    cuts = [0, -(-depth // 32) * 16, depth]
    sizes = [end - begin for begin, end in zip(cuts, cuts[1:])]
    act_zx = call(cut_kernel, (act_z,), [pltpu.VMEM((size, tokens), BF16) for size in sizes])
    act_zx = list(act_zx)
    for at, value in enumerate(act_zx):
        act_zx[at] = swap(value, "dp", X_BIT)
    swapped = [gts[0]]
    for at, rel in enumerate(near_rels[1:], 1):
        swapped.append(swap(gts[at], "dp", rel))

    padded = -(-(tok_rows + 2) // 8) * 8
    highs, lows, near_g = call(
        functools.partial(spread_kernel, kernel, tok_rows, befores, afters),
        (g_all, w_conv),
        [pltpu.VMEM((kernel * padded, channels), BF16)] * 2
        + [pltpu.VMEM((padded, channels), BF16)],
    )
    factor = 1.0 / (n_dp * length * n_ctx) ** 0.5
    mines, others = [], []
    for at, size in enumerate(sizes):
        kept = len(late) // 2
        mine, theirs = call(
            functools.partial(kernel_grad_kernel, factor, cuts[at]),
            (act, act_x, act_z, act_zx[at], *swapped),
            [pltpu.VMEM((kept * narrow, size), F32), pltpu.VMEM((kept * narrow, size), BF16)],
        )
        other = swap(theirs, "dp", late[kept])
        while kept > 1:
            kept //= 2
            mine, theirs = call(
                fold_kernel,
                (mine, other),
                [pltpu.VMEM((kept * narrow, size), F32), pltpu.VMEM((kept * narrow, size), BF16)],
            )
            other = swap(theirs, "dp", late[kept])
        mines.append(mine)
        others.append(other)

    by_rows = pl.BlockSpec((block, channels), lambda i: (i, 0))
    grad_in = call(
        functools.partial(input_grad_kernel, kernel, pool),
        (highs, lows, near_g, normed, inv_rms, gain_v),
        [jax.ShapeDtypeStruct((length, channels), BF16)],
        grid=(length // block,),
        out_specs=[by_rows],
    )[0]
    grad_conv = call(
        functools.partial(join_kernel, kernel),
        (*mines, *others),
        [jax.ShapeDtypeStruct((kernel, width, narrow), F32)],
    )[0]
    return grad_in[None], jnp.transpose(grad_conv, (1, 0, 2))


def solution(mesh):
    in_specs = (
        P("dp", "ctx", None),
        P("dp", "ctx"),
        P(),
        P(),
        P(),
        P(),
        P(),
        P(),
        P(),
        P("dp", "ctx", None),
    )
    out_specs = (P("dp", "ctx", None), P("ctx", None, "dp"))
    return jax.shard_map(
        per_device, mesh=mesh, in_specs=in_specs, out_specs=out_specs, check_vma=False
    )
```

```python
import functools

import jax
import jax.numpy as jnp
from jax import lax
from jax.experimental import pallas as pl
from jax.experimental.pallas import tpu as pltpu
from jax.sharding import PartitionSpec as P


HEADS = 6
DH = 128

EPSILON = 1e-06
GELU_SCALE = 0.7978845608028654
CUBIC = 0.044715
F32 = jnp.float32
BF16 = jnp.bfloat16
VMEM_LIMIT = 28 << 20
FLOPS_PER_MICRO = 1.15e9
X_BIT, Z_BIT = 1, 4
BLOCK = 128


def dot_nn(left, right):
    return lax.dot_general(left, right, (((1,), (0,)), ((), ())), preferred_element_type=F32)


def dot_nt(left, right):
    return lax.dot_general(left, right, (((1,), (1,)), ((), ())), preferred_element_type=F32)


def dot_tn(left, right):
    return lax.dot_general(left, right, (((0,), (0,)), ((), ())), preferred_element_type=F32)


def split2(value):
    high = value.astype(BF16)
    return high, (value - high.astype(F32)).astype(BF16)


def iota(shape, dim):
    return lax.broadcasted_iota(jnp.int32, shape, dim)


def normed_of(summed):
    inv_rms = lax.rsqrt(jnp.mean(summed * summed, axis=-1, keepdims=True) + EPSILON)
    return inv_rms, summed * inv_rms


def gelu_of(u):
    tanh_val = jnp.tanh(GELU_SCALE * (u + CUBIC * (u * u * u)))
    return tanh_val, 0.5 * u * (1.0 + tanh_val)


def pick(index, values):
    out = jnp.int32(values[0])
    for at, value in enumerate(values[1:], 1):
        out = jnp.where(index == at, jnp.int32(value), out)
    return out


def start_copies(pairs, sems):
    copies = [pltpu.make_async_copy(src, dst, sems.at[i]) for i, (src, dst) in enumerate(pairs)]
    for copy in copies:
        copy.start()
    return copies


def act_kernel(
    kernel, pool, tok_rows, feat_hbm, base_hbm, table_hbm, gain_hbm, cot_hbm,
    taps, sums, normed_out, inv_out, gain, cot, feat, base, table, act_buf, spread, embed, sems,
):
    half = kernel // 2
    rows, channels = feat.shape
    block = BLOCK
    count = rows // block
    small = ((base_hbm, base), (table_hbm, table), (gain_hbm, gain))
    parts = tuple(
        (feat_hbm.at[pl.ds(i * block, block)], feat.at[pl.ds(i * block, block)]) for i in range(count)
    )
    copies = start_copies(small + parts + ((cot_hbm, cot),), sems)
    padded = taps.shape[0] // kernel
    shape = (kernel * padded, rows)
    row = iota(shape, 0)
    tap = sum((row >= padded * j).astype(jnp.int32) for j in range(1, kernel))
    token = row - tap * padded
    known = token < tok_rows + 2
    token = jnp.where(token == tok_rows, -1, jnp.where(token == tok_rows + 1, tok_rows, token))
    offset = iota(shape, 1) - tap + half - token * pool
    spread[...] = ((offset >= 0) & (offset < pool) & known).astype(BF16)
    for copy in copies[: len(small)]:
        copy.wait()
    gain_f = gain[...].reshape(1, channels).astype(F32)
    onehot = (iota((table.shape[0], rows), 0) == base[...]).astype(BF16)
    embed[...] = dot_tn(onehot, table[...])
    for copy in copies[len(small) : len(small) + count]:
        copy.wait()

    summed = feat[...].astype(F32) + embed[...]
    inv_rms, normed = normed_of(summed)
    act_buf[...] = gelu_of(normed * gain_f)[1].astype(BF16)
    normed_out[...] = normed
    inv_out[...] = jnp.broadcast_to(inv_rms, inv_out.shape)
    taps[...] = dot_nn(spread[...], act_buf[...])
    plain = spread[half * padded : (half + 1) * padded, :]
    counts = dot_nt(plain, onehot).astype(BF16)
    sums[...] = dot_nn(plain, feat[...]) + dot_nn(counts, table[...])

    for copy in copies[len(small) + count :]:
        copy.wait()


def taps_kernel(kernel, blocks, taps, pairs, *rest):
    outs, turn = rest[:blocks], rest[blocks]
    me = lax.axis_index("ctx")
    padded = taps.shape[0] // kernel
    highs = []
    for j in range(kernel):
        high, low = split2(taps[j * padded : (j + 1) * padded, :])
        highs.append(high)
        pairs[j] = jnp.concatenate([high, low], axis=0)
    width = taps.shape[1] // blocks
    for b in range(blocks):
        turn[b ^ me] = jnp.concatenate([h[:, b * width : (b + 1) * width] for h in highs], axis=1)
    for b in range(blocks):
        outs[b][...] = turn[b]


def pool_kernel(pool, tok_rows, pairs, sums, weights, cot, rows):
    padded = sums.shape[0]
    total = dot_nn(pairs[0], weights[0])
    for j in range(1, pairs.shape[0]):
        total = total + dot_nn(pairs[j], weights[j])
    conv = total[:padded] + total[padded:]
    value = (sums[...] + conv) * (1.0 / pool)
    high, low = split2(value)
    rows[:padded, :] = high
    rows[padded : padded + tok_rows, :] = cot[...]
    low_f = low.astype(F32)
    ends = [low_f[:1], low_f[tok_rows - 1 : tok_rows + 2]]
    ends = jnp.concatenate(ends + [jnp.zeros((4, low.shape[1]), F32)], axis=0)
    rows[padded + tok_rows :, :] = ends.astype(BF16)


def neighbours(me, order, count, befores, afters, ends):
    zero = jnp.zeros(ends.shape[1:], F32)
    ends[0] = zero
    ends[count + 1] = zero
    for rel, before, after in zip(order, befores, afters):
        owner = me ^ rel
        ends[owner + 1, 0:1, :] = before
        ends[owner + 1, 1:2, :] = after
    return [(ends[me ^ rel, 1:2, :], ends[(me ^ rel) + 2, 0:1, :]) for rel in order]


def pack_kernel(order, tok_rows, *refs):
    *parts, out, buf, ends = refs
    me = lax.axis_index("ctx")
    tails = [part[tok_rows : tok_rows + 8, :].astype(F32) for part in parts]
    extra = neighbours(
        me, order, len(parts), [tail[0:1] for tail in tails], [tail[1:2] for tail in tails], ends
    )
    for at, (part, (first, last)) in enumerate(zip(parts, extra)):
        value = part[:tok_rows, :].astype(F32)
        row = iota(value.shape, 0)
        value = value + jnp.where(row == 0, first, 0.0) + jnp.where(row == tok_rows - 1, last, 0.0)
        buf[at * tok_rows : (at + 1) * tok_rows, :] = value.astype(BF16)
    total = buf.shape[0]
    eye = (iota((total, total), 0) == iota((total, total), 1)).astype(BF16)
    out[...] = dot_tn(buf[...], eye).astype(BF16)


def attention_kernel(pool, order, tok_rows, near_rels, late, *refs):
    blocks = len(order)
    parts, refs = refs[:blocks], refs[blocks:]
    (wq, wk, wv_hbm, wo_hbm), refs = refs[:4], refs[4:]
    g_out, refs = refs[0], refs[1:]
    gts, refs = refs[: len(near_rels)], refs[len(near_rels) :]
    p_buf, c_buf, q_buf, k_buf, v_buf, ga_buf, gq_buf, gk_buf, gv_buf = refs[:9]
    probs_buf, turn, ends, wv, wo, sems = refs[9:]
    copies = start_copies(((wv_hbm, wv), (wo_hbm, wo)), sems)
    padded = parts[0].shape[0] - tok_rows - 8
    befores, afters, firsts, lasts = [], [], [], []
    for part in parts:
        tail = part[tok_rows : tok_rows + 8, :].astype(F32)
        lows = part[padded + tok_rows :, :].astype(F32)
        firsts.append(part[:8, :].astype(F32)[0:1] + lows[0:1])
        lasts.append(part[tok_rows - 8 : tok_rows, :].astype(F32)[7:8] + lows[1:2])
        befores.append(tail[0:1] + lows[2:3])
        afters.append(tail[1:2] + lows[3:4])
    extra = neighbours(lax.axis_index("ctx"), order, blocks, befores, afters, ends)
    for at, (part, first, last, (to_first, to_last)) in enumerate(zip(parts, firsts, lasts, extra)):
        value = part[:tok_rows, :].astype(F32)
        row = iota(value.shape, 0)
        value = jnp.where(row == 0, first + to_first, value)
        value = jnp.where(row == tok_rows - 1, last + to_last, value)
        here = slice(at * tok_rows, (at + 1) * tok_rows)
        p_buf[here, :] = value.astype(BF16)
        c_buf[here, :] = part[padded : padded + tok_rows, :]
    q_buf[...] = dot_nn(p_buf[...], wq[...]).astype(BF16)
    k_buf[...] = dot_nn(p_buf[...], wk[...]).astype(BF16)
    scale = 1.0 / DH**0.5
    heads = [slice(h * DH, (h + 1) * DH) for h in range(HEADS)]
    scores = [dot_nt(k_buf[:, cols], q_buf[:, cols]) * scale for cols in heads]
    for h, score in enumerate(scores):
        expo = jnp.exp(score - jnp.max(score, axis=0, keepdims=True))
        probs_buf[h] = expo / jnp.sum(expo, axis=0, keepdims=True)
    copies[0].wait()
    v_buf[...] = dot_nn(p_buf[...], wv[...]).astype(BF16)
    copies[1].wait()
    ga_buf[...] = dot_nt(wo[...], c_buf[...]).astype(BF16)
    probs_b = [probs_buf[h].astype(BF16) for h in range(HEADS)]
    outs = [dot_tn(v_buf[:, cols], p).astype(BF16) for cols, p in zip(heads, probs_b)]
    terms = [dot_nn(v_buf[:, cols], ga_buf[cols, :]) for cols in heads]
    for cols, p in zip(heads, probs_b):
        gv_buf[:, cols] = dot_nt(p, ga_buf[cols, :]).astype(BF16)
    slopes = []
    for h, cols in enumerate(heads):
        delta = jnp.sum(ga_buf[cols, :].astype(F32) * outs[h].astype(F32), axis=0, keepdims=True)
        slopes.append((probs_buf[h] * (terms[h] - delta) * scale).astype(BF16))
    for cols, slope in zip(heads, slopes):
        gk_buf[:, cols] = dot_nn(slope, q_buf[:, cols]).astype(BF16)
        gq_buf[:, cols] = dot_tn(slope, k_buf[:, cols]).astype(BF16)
    grad = jnp.transpose(c_buf[...].astype(F32))
    for src, weight in ((gq_buf, wq), (gk_buf, wk), (gv_buf, wv)):
        grad = grad + dot_nt(weight[...], src[...])
    turned = (grad * (1.0 / pool)).astype(BF16)
    g_out[...] = turned
    count = turn.shape[0]
    span = turned.shape[0] // count
    me = lax.axis_index("dp")
    for o in range(count):
        turn[o ^ me] = turned[o * span : (o + 1) * span, :]
    for gt, base in zip(gts, near_rels):
        for at, rel in enumerate(late):
            gt[at * span : (at + 1) * span, :] = turn[base ^ rel]


def spread_kernel(kernel, tok_rows, befores, afters, g_ref, weights, highs, lows, near):
    tokens = g_ref.shape[1]
    padded = near.shape[0]
    me = lax.axis_index("ctx")
    row = iota((padded, tokens), 0)
    source = jnp.where(
        row == 0, pick(me, befores), jnp.where(row == tok_rows + 1, pick(me, afters), row - 1)
    )
    source = jnp.where(row > tok_rows + 1, -1, source)
    chosen = (source == iota((padded, tokens), 1)).astype(BF16)
    rows = dot_nt(chosen, g_ref[...]).astype(BF16)
    near[...] = rows
    for j in range(kernel):
        part = slice(j * padded, (j + 1) * padded)
        highs[part, :], lows[part, :] = split2(dot_nt(rows, weights[j]))


def input_grad_kernel(
    kernel, pool, highs, lows, near, normed_ref, inv_ref, gain, out
):
    half = kernel // 2
    rows, channels = out.shape
    padded = near.shape[0]
    start = pl.program_id(0) * rows
    here = pl.ds(pl.multiple_of(start, rows), rows)
    shape = (rows, kernel * padded)
    col = iota(shape, 1)
    tap = sum((col >= padded * j).astype(jnp.int32) for j in range(1, kernel))
    token = col - tap * padded - 1
    offset = iota(shape, 0) + start - tap + half - token * pool
    spread = ((offset >= 0) & (offset < pool)).astype(BF16)
    grad_act = dot_nn(spread, highs[...]) + dot_nn(spread, lows[...])
    plain = spread[:, half * padded : (half + 1) * padded]
    grad_rows = dot_nn(plain, near[...])
    gain_f = gain[...].reshape(1, channels).astype(F32)
    unit = normed_ref[here, :]
    u = unit * gain_f
    tanh_val = gelu_of(u)[0]
    slopes = 0.5 * (1.0 + tanh_val) + 0.5 * u * (1.0 - tanh_val * tanh_val) * GELU_SCALE * (
        1.0 + 3.0 * CUBIC * (u * u)
    )
    grad_norm = grad_act * slopes * gain_f
    mean = jnp.mean(grad_norm * unit, axis=-1, keepdims=True)
    out[...] = (grad_rows + inv_ref[here, :1] * (grad_norm - unit * mean)).astype(BF16)


def cut_kernel(value, *outs):
    at = 0
    for out in outs:
        out[...] = value[at : at + out.shape[0], :]
        at += out.shape[0]


def kernel_grad_kernel(factor, begin, *refs):
    count = len(refs) // 2 - 1
    acts, gts, (mine, theirs) = refs[:count], refs[count : 2 * count], refs[2 * count :]
    span, size = mine.shape
    total = None
    for act, gt in zip(acts, gts):
        at = begin if act.shape[0] > size else 0
        term = dot_nt(gt[...], act[at : at + size, :])
        total = term if total is None else total + term
    total = total * factor
    mine[...] = total[:span, :]
    theirs[...] = total[span:, :].astype(BF16)


def fold_kernel(mine, other, kept, sent):
    span = kept.shape[0]
    kept[...] = mine[:span, :] + other[:span, :].astype(F32)
    sent[...] = (mine[span:, :] + other[span:, :].astype(F32)).astype(BF16)


def join_kernel(kernel, *refs):
    *parts, out = refs
    width = out.shape[1]
    half = len(parts) // 2
    sums = [a[...] + b[...].astype(F32) for a, b in zip(parts[:half], parts[half:])]
    total = jnp.transpose(jnp.concatenate(sums, axis=1))
    for j in range(kernel):
        out[j] = total[j * width : (j + 1) * width, :]


def xor_order(count):
    order = [0]
    bit = count // 2
    while bit:
        order = order + [v ^ bit for v in order]
        bit //= 2
    return order


def swap(value, axis, bit):
    count = lax.axis_size(axis)
    return lax.ppermute(value, axis, [(i, i ^ bit) for i in range(count)])


WHOLE = pl.BlockSpec(memory_space=pltpu.VMEM)


def call(body, args, outs, scratch=(), micros=1, **options):
    options.setdefault("in_specs", [WHOLE] * len(args))
    options.setdefault("out_specs", [WHOLE] * len(outs))
    return pl.pallas_call(
        body,
        out_shape=list(outs),
        scratch_shapes=list(scratch),
        compiler_params=pltpu.CompilerParams(vmem_limit_bytes=VMEM_LIMIT),
        cost_estimate=pl.CostEstimate(
            flops=int(micros * FLOPS_PER_MICRO), bytes_accessed=0, transcendentals=0
        ),
        **options,
    )(*args)


def outside(*values):
    return [pltpu.with_memory_space_constraint(value, pltpu.HBM) for value in values]


def bits_of(count):
    return [1 << at for at in range(count.bit_length() - 1)]


def sums_of(bits):
    out = [0]
    for bit in bits:
        out = out + [bit + value for value in out]
    return out


def per_device(
    features, bases, dna_table, norm_gain, w_conv, w_query, w_key, w_value, w_out, cotangent
):
    feat, cot = features[0], cotangent[0]
    kernel = w_conv.shape[0]
    length, channels = feat.shape
    tok_rows = cot.shape[0]
    pool = length // tok_rows
    n_ctx, n_dp = lax.axis_size("ctx"), lax.axis_size("dp")
    tokens = n_ctx * tok_rows
    width = channels // n_ctx
    narrow = channels // n_dp
    near_rels = [0, X_BIT, Z_BIT, X_BIT + Z_BIT]
    late = sums_of([bit for bit in bits_of(n_dp) if bit not in (X_BIT, Z_BIT)])

    order = xor_order(n_ctx)
    place = {rel: at for at, rel in enumerate(order)}
    befores = [-1] + [place[c ^ (c - 1)] * tok_rows + tok_rows - 1 for c in range(1, n_ctx)]
    afters = [place[c ^ (c + 1)] * tok_rows for c in range(n_ctx - 1)] + [-1]

    hbm = pl.BlockSpec(memory_space=pltpu.HBM)
    block = BLOCK
    wide = -(-(tok_rows + 2) // 8) * 8
    taps, sums, normed, inv_rms, gain_v, cot_v = call(
        functools.partial(act_kernel, kernel, pool, tok_rows),
        outside(feat, bases, dna_table, norm_gain, cot),
        [
            pltpu.VMEM((kernel * wide, channels), F32),
            pltpu.VMEM((wide, channels), F32),
            pltpu.VMEM((length, channels), F32),
            pltpu.VMEM((length, 128), F32),
            pltpu.VMEM(norm_gain.shape, BF16),
            pltpu.VMEM(cot.shape, BF16),
        ],
        [
            pltpu.VMEM(feat.shape, BF16),
            pltpu.VMEM(bases.shape, jnp.int32),
            pltpu.VMEM(dna_table.shape, BF16),
            pltpu.VMEM(feat.shape, BF16),
            pltpu.VMEM((kernel * wide, length), BF16),
            pltpu.VMEM((length, channels), F32),
        ]
        + [pltpu.SemaphoreType.DMA((4 + length // block,))],
        in_specs=[hbm] * 5,
        micros=3,
    )
    pairs, *acts = call(
        functools.partial(taps_kernel, kernel, n_ctx),
        (taps,),
        [pltpu.VMEM((kernel, 2 * wide, channels), BF16)]
        + [pltpu.VMEM((wide, kernel * width), BF16)] * n_ctx,
        [pltpu.VMEM((n_ctx, wide, kernel * width), BF16)],
    )
    swapped = [acts[0]]
    for rel in order[1:]:
        swapped.append(swap(acts[rel], "ctx", rel))
    acts = swapped
    pooled = call(
        functools.partial(pool_kernel, pool, tok_rows),
        (pairs, sums, w_conv, cot_v),
        [pltpu.VMEM((wide + tok_rows + 8, channels), BF16)],
    )[0]
    rows = [pooled]
    bit = n_ctx // 2
    while bit:
        rows = rows + [swap(value, "ctx", bit) for value in rows]
        bit //= 2

    act = call(
        functools.partial(pack_kernel, order, tok_rows),
        acts,
        [pltpu.VMEM((kernel * width, tokens), BF16)],
        [
            pltpu.VMEM((tokens, kernel * width), BF16),
            pltpu.VMEM((n_ctx + 2, 8, kernel * width), F32),
        ],
    )[0]

    act_z = swap(act, "dp", Z_BIT)
    act_x = swap(act, "dp", X_BIT)

    g_all, *gts = call(
        functools.partial(attention_kernel, pool, order, tok_rows, near_rels, late),
        [*rows, w_query, w_key] + outside(w_value, w_out),
        [pltpu.VMEM((channels, tokens), BF16)]
        + [pltpu.VMEM((len(late) * narrow, tokens), BF16)] * len(near_rels),
        [pltpu.VMEM((tokens, channels), BF16)] * 5
        + [pltpu.VMEM((channels, tokens), BF16)]
        + [pltpu.VMEM((tokens, channels), BF16)] * 3
        + [
            pltpu.VMEM((HEADS, tokens, tokens), F32),
            pltpu.VMEM((n_dp, narrow, tokens), BF16),
            pltpu.VMEM((n_ctx + 2, 8, channels), F32),
            pltpu.VMEM(w_value.shape, BF16),
            pltpu.VMEM(w_out.shape, BF16),
            pltpu.SemaphoreType.DMA((2,)),
        ],
        in_specs=[WHOLE] * (n_ctx + 2) + [hbm] * 2,
        micros=5,
    )

    depth = kernel * width
    cuts = [0, -(-depth // 32) * 16, depth]
    sizes = [end - begin for begin, end in zip(cuts, cuts[1:])]
    act_zx = call(cut_kernel, (act_z,), [pltpu.VMEM((size, tokens), BF16) for size in sizes])
    act_zx = list(act_zx)
    for at, value in enumerate(act_zx):
        act_zx[at] = swap(value, "dp", X_BIT)
    swapped = [gts[0]]
    for at, rel in enumerate(near_rels[1:], 1):
        swapped.append(swap(gts[at], "dp", rel))

    padded = -(-(tok_rows + 2) // 8) * 8
    highs, lows, near_g = call(
        functools.partial(spread_kernel, kernel, tok_rows, befores, afters),
        (g_all, w_conv),
        [pltpu.VMEM((kernel * padded, channels), BF16)] * 2
        + [pltpu.VMEM((padded, channels), BF16)],
    )
    factor = 1.0 / (n_dp * length * n_ctx) ** 0.5
    mines, others = [], []
    for at, size in enumerate(sizes):
        kept = len(late) // 2
        mine, theirs = call(
            functools.partial(kernel_grad_kernel, factor, cuts[at]),
            (act, act_x, act_z, act_zx[at], *swapped),
            [pltpu.VMEM((kept * narrow, size), F32), pltpu.VMEM((kept * narrow, size), BF16)],
        )
        other = swap(theirs, "dp", late[kept])
        while kept > 1:
            kept //= 2
            mine, theirs = call(
                fold_kernel,
                (mine, other),
                [pltpu.VMEM((kept * narrow, size), F32), pltpu.VMEM((kept * narrow, size), BF16)],
            )
            other = swap(theirs, "dp", late[kept])
        mines.append(mine)
        others.append(other)

    by_rows = pl.BlockSpec((block, channels), lambda i: (i, 0))
    grad_in = call(
        functools.partial(input_grad_kernel, kernel, pool),
        (highs, lows, near_g, normed, inv_rms, gain_v),
        [jax.ShapeDtypeStruct((length, channels), BF16)],
        grid=(length // block,),
        out_specs=[by_rows],
    )[0]
    grad_conv = call(
        functools.partial(join_kernel, kernel),
        (*mines, *others),
        [jax.ShapeDtypeStruct((kernel, width, narrow), F32)],
    )[0]
    return grad_in[None], jnp.transpose(grad_conv, (1, 0, 2))


def solution(mesh):
    in_specs = (
        P("dp", "ctx", None),
        P("dp", "ctx"),
        P(),
        P(),
        P(),
        P(),
        P(),
        P(),
        P(),
        P("dp", "ctx", None),
    )
    out_specs = (P("dp", "ctx", None), P("ctx", None, "dp"))
    return jax.shard_map(
        per_device, mesh=mesh, in_specs=in_specs, out_specs=out_specs, check_vma=False
    )
```

```python
import functools

import jax
import jax.numpy as jnp
from jax import lax
from jax.experimental import pallas as pl
from jax.experimental.pallas import tpu as pltpu
from jax.sharding import PartitionSpec as P


HEADS = 6
DH = 128

EPSILON = 1e-06
GELU_SCALE = 0.7978845608028654
CUBIC = 0.044715
F32 = jnp.float32
BF16 = jnp.bfloat16
VMEM_LIMIT = 28 << 20
FLOPS_PER_MICRO = 1.15e9
X_BIT, Z_BIT = 1, 4
BLOCK = 128


def dot_nn(left, right):
    return lax.dot_general(left, right, (((1,), (0,)), ((), ())), preferred_element_type=F32)


def dot_nt(left, right):
    return lax.dot_general(left, right, (((1,), (1,)), ((), ())), preferred_element_type=F32)


def dot_tn(left, right):
    return lax.dot_general(left, right, (((0,), (0,)), ((), ())), preferred_element_type=F32)


def split2(value):
    high = value.astype(BF16)
    return high, (value - high.astype(F32)).astype(BF16)


def iota(shape, dim):
    return lax.broadcasted_iota(jnp.int32, shape, dim)


def normed_of(summed):
    inv_rms = lax.rsqrt(jnp.mean(summed * summed, axis=-1, keepdims=True) + EPSILON)
    return inv_rms, summed * inv_rms


def gelu_of(u):
    tanh_val = jnp.tanh(GELU_SCALE * (u + CUBIC * (u * u * u)))
    return tanh_val, 0.5 * u * (1.0 + tanh_val)


def pick(index, values):
    out = jnp.int32(values[0])
    for at, value in enumerate(values[1:], 1):
        out = jnp.where(index == at, jnp.int32(value), out)
    return out


def start_copies(pairs, sems):
    copies = [pltpu.make_async_copy(src, dst, sems.at[i]) for i, (src, dst) in enumerate(pairs)]
    for copy in copies:
        copy.start()
    return copies


def act_kernel(
    kernel, pool, tok_rows, feat_hbm, base_hbm, table_hbm, gain_hbm, cot_hbm,
    taps, sums, normed_out, inv_out, gain, cot, feat, base, table, act_buf, spread, embed, sems,
):
    half = kernel // 2
    rows, channels = feat.shape
    block = BLOCK
    count = rows // block
    small = ((base_hbm, base), (table_hbm, table), (gain_hbm, gain))
    parts = tuple(
        (feat_hbm.at[pl.ds(i * block, block)], feat.at[pl.ds(i * block, block)]) for i in range(count)
    )
    copies = start_copies(small + parts + ((cot_hbm, cot),), sems)
    padded = taps.shape[0] // kernel
    shape = (kernel * padded, rows)
    row = iota(shape, 0)
    tap = sum((row >= padded * j).astype(jnp.int32) for j in range(1, kernel))
    token = row - tap * padded
    known = token < tok_rows + 2
    token = jnp.where(token == tok_rows, -1, jnp.where(token == tok_rows + 1, tok_rows, token))
    offset = iota(shape, 1) - tap + half - token * pool
    spread[...] = ((offset >= 0) & (offset < pool) & known).astype(BF16)
    for copy in copies[: len(small)]:
        copy.wait()
    gain_f = gain[...].reshape(1, channels).astype(F32)
    onehot = (iota((table.shape[0], rows), 0) == base[...]).astype(BF16)
    embed[...] = dot_tn(onehot, table[...])
    for copy in copies[len(small) : len(small) + count]:
        copy.wait()

    summed = feat[...].astype(F32) + embed[...]
    inv_rms, normed = normed_of(summed)
    act_buf[...] = gelu_of(normed * gain_f)[1].astype(BF16)
    normed_out[...] = normed
    inv_out[...] = jnp.broadcast_to(inv_rms, inv_out.shape)
    taps[...] = dot_nn(spread[...], act_buf[...])
    plain = spread[half * padded : (half + 1) * padded, :]
    counts = dot_nt(plain, onehot).astype(BF16)
    sums[...] = dot_nn(plain, feat[...]) + dot_nn(counts, table[...])

    for copy in copies[len(small) + count :]:
        copy.wait()


def taps_kernel(kernel, blocks, taps, pairs, *rest):
    outs, turn = rest[:blocks], rest[blocks]
    me = lax.axis_index("ctx")
    padded = taps.shape[0] // kernel
    highs = []
    for j in range(kernel):
        high, low = split2(taps[j * padded : (j + 1) * padded, :])
        highs.append(high)
        pairs[j] = jnp.concatenate([high, low], axis=0)
    width = taps.shape[1] // blocks
    for b in range(blocks):
        turn[b ^ me] = jnp.concatenate([h[:, b * width : (b + 1) * width] for h in highs], axis=1)
    for b in range(blocks):
        outs[b][...] = turn[b]


def pool_kernel(pool, tok_rows, pairs, sums, weights, cot, rows):
    padded = sums.shape[0]
    total = dot_nn(pairs[0], weights[0])
    for j in range(1, pairs.shape[0]):
        total = total + dot_nn(pairs[j], weights[j])
    conv = total[:padded] + total[padded:]
    value = (sums[...] + conv) * (1.0 / pool)
    high, low = split2(value)
    rows[:padded, :] = high
    rows[padded : padded + tok_rows, :] = cot[...]
    low_f = low.astype(F32)
    ends = [low_f[:1], low_f[tok_rows - 1 : tok_rows + 2]]
    ends = jnp.concatenate(ends + [jnp.zeros((4, low.shape[1]), F32)], axis=0)
    rows[padded + tok_rows :, :] = ends.astype(BF16)


def neighbours(me, order, count, befores, afters, ends):
    zero = jnp.zeros(ends.shape[1:], F32)
    ends[0] = zero
    ends[count + 1] = zero
    for rel, before, after in zip(order, befores, afters):
        owner = me ^ rel
        ends[owner + 1, 0:1, :] = before
        ends[owner + 1, 1:2, :] = after
    return [(ends[me ^ rel, 1:2, :], ends[(me ^ rel) + 2, 0:1, :]) for rel in order]


def pack_kernel(order, tok_rows, *refs):
    *parts, out, buf, ends = refs
    me = lax.axis_index("ctx")
    tails = [part[tok_rows : tok_rows + 8, :].astype(F32) for part in parts]
    extra = neighbours(
        me, order, len(parts), [tail[0:1] for tail in tails], [tail[1:2] for tail in tails], ends
    )
    for at, (part, (first, last)) in enumerate(zip(parts, extra)):
        value = part[:tok_rows, :].astype(F32)
        row = iota(value.shape, 0)
        value = value + jnp.where(row == 0, first, 0.0) + jnp.where(row == tok_rows - 1, last, 0.0)
        buf[at * tok_rows : (at + 1) * tok_rows, :] = value.astype(BF16)
    total = buf.shape[0]
    eye = (iota((total, total), 0) == iota((total, total), 1)).astype(BF16)
    out[...] = dot_tn(buf[...], eye).astype(BF16)


def attention_kernel(pool, order, tok_rows, near_rels, late, *refs):
    blocks = len(order)
    parts, refs = refs[:blocks], refs[blocks:]
    (wq, wk, wv_hbm, wo_hbm), refs = refs[:4], refs[4:]
    g_out, refs = refs[0], refs[1:]
    gts, refs = refs[: len(near_rels)], refs[len(near_rels) :]
    p_buf, c_buf, q_buf, k_buf, v_buf, ga_buf, gq_buf, gk_buf, gv_buf = refs[:9]
    probs_buf, turn, ends, wv, wo, sems = refs[9:]
    copies = start_copies(((wv_hbm, wv), (wo_hbm, wo)), sems)
    padded = parts[0].shape[0] - tok_rows - 8
    befores, afters, firsts, lasts = [], [], [], []
    for part in parts:
        tail = part[tok_rows : tok_rows + 8, :].astype(F32)
        lows = part[padded + tok_rows :, :].astype(F32)
        firsts.append(part[:8, :].astype(F32)[0:1] + lows[0:1])
        lasts.append(part[tok_rows - 8 : tok_rows, :].astype(F32)[7:8] + lows[1:2])
        befores.append(tail[0:1] + lows[2:3])
        afters.append(tail[1:2] + lows[3:4])
    extra = neighbours(lax.axis_index("ctx"), order, blocks, befores, afters, ends)
    for at, (part, first, last, (to_first, to_last)) in enumerate(zip(parts, firsts, lasts, extra)):
        value = part[:tok_rows, :].astype(F32)
        row = iota(value.shape, 0)
        value = jnp.where(row == 0, first + to_first, value)
        value = jnp.where(row == tok_rows - 1, last + to_last, value)
        here = slice(at * tok_rows, (at + 1) * tok_rows)
        p_buf[here, :] = value.astype(BF16)
        c_buf[here, :] = part[padded : padded + tok_rows, :]
    q_buf[...] = dot_nn(p_buf[...], wq[...]).astype(BF16)
    k_buf[...] = dot_nn(p_buf[...], wk[...]).astype(BF16)
    scale = 1.0 / DH**0.5
    heads = [slice(h * DH, (h + 1) * DH) for h in range(HEADS)]
    scores = [dot_nt(k_buf[:, cols], q_buf[:, cols]) * scale for cols in heads]
    for h, score in enumerate(scores):
        expo = jnp.exp(score - jnp.max(score, axis=0, keepdims=True))
        probs_buf[h] = expo / jnp.sum(expo, axis=0, keepdims=True)
    copies[0].wait()
    v_buf[...] = dot_nn(p_buf[...], wv[...]).astype(BF16)
    copies[1].wait()
    ga_buf[...] = dot_nt(wo[...], c_buf[...]).astype(BF16)
    probs_b = [probs_buf[h].astype(BF16) for h in range(HEADS)]
    outs = [dot_tn(v_buf[:, cols], p).astype(BF16) for cols, p in zip(heads, probs_b)]
    terms = [dot_nn(v_buf[:, cols], ga_buf[cols, :]) for cols in heads]
    for cols, p in zip(heads, probs_b):
        gv_buf[:, cols] = dot_nt(p, ga_buf[cols, :]).astype(BF16)
    slopes = []
    for h, cols in enumerate(heads):
        delta = jnp.sum(ga_buf[cols, :].astype(F32) * outs[h].astype(F32), axis=0, keepdims=True)
        slopes.append((probs_buf[h] * (terms[h] - delta) * scale).astype(BF16))
    for cols, slope in zip(heads, slopes):
        gk_buf[:, cols] = dot_nn(slope, q_buf[:, cols]).astype(BF16)
        gq_buf[:, cols] = dot_tn(slope, k_buf[:, cols]).astype(BF16)
    grad = jnp.transpose(c_buf[...].astype(F32))
    for src, weight in ((gq_buf, wq), (gk_buf, wk), (gv_buf, wv)):
        grad = grad + dot_nt(weight[...], src[...])
    turned = (grad * (1.0 / pool)).astype(BF16)
    g_out[...] = turned
    count = turn.shape[0]
    span = turned.shape[0] // count
    me = lax.axis_index("dp")
    for o in range(count):
        turn[o ^ me] = turned[o * span : (o + 1) * span, :]
    for at, rel in enumerate(late):
        gts[0][at * span : (at + 1) * span, :] = turn[rel]
    half = len(late) // 2
    core = lax.axis_index("ctx") % 2
    for gt, base in zip(gts[1:], near_rels[1:]):
        for at in range(half):
            rel = pick(core, [late[at], late[half + at]])
            gt[at * span : (at + 1) * span, :] = turn[base ^ rel]


def spread_kernel(kernel, tok_rows, befores, afters, g_ref, weights, highs, lows, near):
    tokens = g_ref.shape[1]
    padded = near.shape[0]
    me = lax.axis_index("ctx")
    row = iota((padded, tokens), 0)
    source = jnp.where(
        row == 0, pick(me, befores), jnp.where(row == tok_rows + 1, pick(me, afters), row - 1)
    )
    source = jnp.where(row > tok_rows + 1, -1, source)
    chosen = (source == iota((padded, tokens), 1)).astype(BF16)
    rows = dot_nt(chosen, g_ref[...]).astype(BF16)
    near[...] = rows
    for j in range(kernel):
        part = slice(j * padded, (j + 1) * padded)
        highs[part, :], lows[part, :] = split2(dot_nt(rows, weights[j]))


def input_grad_kernel(
    kernel, pool, highs, lows, near, normed_ref, inv_ref, gain, out
):
    half = kernel // 2
    rows, channels = out.shape
    padded = near.shape[0]
    start = pl.program_id(0) * rows
    here = pl.ds(pl.multiple_of(start, rows), rows)
    shape = (rows, kernel * padded)
    col = iota(shape, 1)
    tap = sum((col >= padded * j).astype(jnp.int32) for j in range(1, kernel))
    token = col - tap * padded - 1
    offset = iota(shape, 0) + start - tap + half - token * pool
    spread = ((offset >= 0) & (offset < pool)).astype(BF16)
    grad_act = dot_nn(spread, highs[...]) + dot_nn(spread, lows[...])
    plain = spread[:, half * padded : (half + 1) * padded]
    grad_rows = dot_nn(plain, near[...])
    gain_f = gain[...].reshape(1, channels).astype(F32)
    unit = normed_ref[here, :]
    u = unit * gain_f
    tanh_val = gelu_of(u)[0]
    slopes = 0.5 * (1.0 + tanh_val) + 0.5 * u * (1.0 - tanh_val * tanh_val) * GELU_SCALE * (
        1.0 + 3.0 * CUBIC * (u * u)
    )
    grad_norm = grad_act * slopes * gain_f
    mean = jnp.mean(grad_norm * unit, axis=-1, keepdims=True)
    out[...] = (grad_rows + inv_ref[here, :1] * (grad_norm - unit * mean)).astype(BF16)


def cut_kernel(value, *outs):
    at = 0
    for out in outs:
        out[...] = value[at : at + out.shape[0], :]
        at += out.shape[0]


def kernel_grad_kernel(factor, begin, *refs):
    *refs, mine, theirs = refs
    count = (len(refs) + 1) // 3
    acts, own, refs = refs[:count], refs[count], refs[count + 1 :]
    first = lax.axis_index("ctx") % 2 == 0
    gts = [own[...]]
    for here, other in zip(refs[: count - 1], refs[count - 1 :]):
        turned = pltpu.roll(other[...].astype(F32), other.shape[1] // 2, axis=1)
        a, b = here[...], turned.astype(BF16)
        gts.append(jnp.concatenate([jnp.where(first, a, b), jnp.where(first, b, a)], axis=0))
    span, size = mine.shape
    total = None
    for act, gt in zip(acts, gts):
        at = begin if act.shape[0] > size else 0
        term = dot_nt(gt, act[at : at + size, :])
        total = term if total is None else total + term
    total = total * factor
    mine[...] = total[:span, :]
    theirs[...] = total[span:, :].astype(BF16)


def fold_kernel(mine, other, kept, sent):
    span = kept.shape[0]
    kept[...] = mine[:span, :] + other[:span, :].astype(F32)
    sent[...] = (mine[span:, :] + other[span:, :].astype(F32)).astype(BF16)


def join_kernel(kernel, *refs):
    *parts, out = refs
    width = out.shape[1]
    half = len(parts) // 2
    sums = [a[...] + b[...].astype(F32) for a, b in zip(parts[:half], parts[half:])]
    total = jnp.transpose(jnp.concatenate(sums, axis=1))
    for j in range(kernel):
        out[j] = total[j * width : (j + 1) * width, :]


def xor_order(count):
    order = [0]
    bit = count // 2
    while bit:
        order = order + [v ^ bit for v in order]
        bit //= 2
    return order


def swap(value, axis, bit):
    count = lax.axis_size(axis)
    return lax.ppermute(value, axis, [(i, i ^ bit) for i in range(count)])


WHOLE = pl.BlockSpec(memory_space=pltpu.VMEM)


def call(body, args, outs, scratch=(), micros=1, **options):
    options.setdefault("in_specs", [WHOLE] * len(args))
    options.setdefault("out_specs", [WHOLE] * len(outs))
    return pl.pallas_call(
        body,
        out_shape=list(outs),
        scratch_shapes=list(scratch),
        compiler_params=pltpu.CompilerParams(vmem_limit_bytes=VMEM_LIMIT),
        cost_estimate=pl.CostEstimate(
            flops=int(micros * FLOPS_PER_MICRO), bytes_accessed=0, transcendentals=0
        ),
        **options,
    )(*args)


def outside(*values):
    return [pltpu.with_memory_space_constraint(value, pltpu.HBM) for value in values]


def bits_of(count):
    return [1 << at for at in range(count.bit_length() - 1)]


def sums_of(bits):
    out = [0]
    for bit in bits:
        out = out + [bit + value for value in out]
    return out


def per_device(
    features, bases, dna_table, norm_gain, w_conv, w_query, w_key, w_value, w_out, cotangent
):
    feat, cot = features[0], cotangent[0]
    kernel = w_conv.shape[0]
    length, channels = feat.shape
    tok_rows = cot.shape[0]
    pool = length // tok_rows
    n_ctx, n_dp = lax.axis_size("ctx"), lax.axis_size("dp")
    tokens = n_ctx * tok_rows
    width = channels // n_ctx
    narrow = channels // n_dp
    near_rels = [0, X_BIT, Z_BIT, X_BIT + Z_BIT]
    late = sums_of([bit for bit in bits_of(n_dp) if bit not in (X_BIT, Z_BIT)])

    order = xor_order(n_ctx)
    place = {rel: at for at, rel in enumerate(order)}
    befores = [-1] + [place[c ^ (c - 1)] * tok_rows + tok_rows - 1 for c in range(1, n_ctx)]
    afters = [place[c ^ (c + 1)] * tok_rows for c in range(n_ctx - 1)] + [-1]

    hbm = pl.BlockSpec(memory_space=pltpu.HBM)
    block = BLOCK
    wide = -(-(tok_rows + 2) // 8) * 8
    taps, sums, normed, inv_rms, gain_v, cot_v = call(
        functools.partial(act_kernel, kernel, pool, tok_rows),
        outside(feat, bases, dna_table, norm_gain, cot),
        [
            pltpu.VMEM((kernel * wide, channels), F32),
            pltpu.VMEM((wide, channels), F32),
            pltpu.VMEM((length, channels), F32),
            pltpu.VMEM((length, 128), F32),
            pltpu.VMEM(norm_gain.shape, BF16),
            pltpu.VMEM(cot.shape, BF16),
        ],
        [
            pltpu.VMEM(feat.shape, BF16),
            pltpu.VMEM(bases.shape, jnp.int32),
            pltpu.VMEM(dna_table.shape, BF16),
            pltpu.VMEM(feat.shape, BF16),
            pltpu.VMEM((kernel * wide, length), BF16),
            pltpu.VMEM((length, channels), F32),
        ]
        + [pltpu.SemaphoreType.DMA((4 + length // block,))],
        in_specs=[hbm] * 5,
        micros=3,
    )
    pairs, *acts = call(
        functools.partial(taps_kernel, kernel, n_ctx),
        (taps,),
        [pltpu.VMEM((kernel, 2 * wide, channels), BF16)]
        + [pltpu.VMEM((wide, kernel * width), BF16)] * n_ctx,
        [pltpu.VMEM((n_ctx, wide, kernel * width), BF16)],
    )
    swapped = [acts[0]]
    for rel in order[1:]:
        swapped.append(swap(acts[rel], "ctx", rel))
    acts = swapped
    pooled = call(
        functools.partial(pool_kernel, pool, tok_rows),
        (pairs, sums, w_conv, cot_v),
        [pltpu.VMEM((wide + tok_rows + 8, channels), BF16)],
    )[0]
    rows = [pooled]
    bit = n_ctx // 2
    while bit:
        rows = rows + [swap(value, "ctx", bit) for value in rows]
        bit //= 2

    act = call(
        functools.partial(pack_kernel, order, tok_rows),
        acts,
        [pltpu.VMEM((kernel * width, tokens), BF16)],
        [
            pltpu.VMEM((tokens, kernel * width), BF16),
            pltpu.VMEM((n_ctx + 2, 8, kernel * width), F32),
        ],
    )[0]

    act_z = swap(act, "dp", Z_BIT)
    act_x = swap(act, "dp", X_BIT)

    g_all, *gts = call(
        functools.partial(attention_kernel, pool, order, tok_rows, near_rels, late),
        [*rows, w_query, w_key] + outside(w_value, w_out),
        [pltpu.VMEM((channels, tokens), BF16), pltpu.VMEM((len(late) * narrow, tokens), BF16)]
        + [pltpu.VMEM((len(late) // 2 * narrow, tokens), BF16)] * (len(near_rels) - 1),
        [pltpu.VMEM((tokens, channels), BF16)] * 5
        + [pltpu.VMEM((channels, tokens), BF16)]
        + [pltpu.VMEM((tokens, channels), BF16)] * 3
        + [
            pltpu.VMEM((HEADS, tokens, tokens), F32),
            pltpu.VMEM((n_dp, narrow, tokens), BF16),
            pltpu.VMEM((n_ctx + 2, 8, channels), F32),
            pltpu.VMEM(w_value.shape, BF16),
            pltpu.VMEM(w_out.shape, BF16),
            pltpu.SemaphoreType.DMA((2,)),
        ],
        in_specs=[WHOLE] * (n_ctx + 2) + [hbm] * 2,
        micros=5,
    )

    depth = kernel * width
    cuts = [0, -(-depth // 32) * 16, depth]
    sizes = [end - begin for begin, end in zip(cuts, cuts[1:])]
    act_zx = call(cut_kernel, (act_z,), [pltpu.VMEM((size, tokens), BF16) for size in sizes])
    act_zx = list(act_zx)
    for at, value in enumerate(act_zx):
        act_zx[at] = swap(value, "dp", X_BIT)
    swapped, shared = [], []
    for at, rel in enumerate(near_rels[1:], 1):
        swapped.append(swap(gts[at], "dp", rel))
        shared.append(swap(swapped[-1], "ctx", 1))

    padded = -(-(tok_rows + 2) // 8) * 8
    highs, lows, near_g = call(
        functools.partial(spread_kernel, kernel, tok_rows, befores, afters),
        (g_all, w_conv),
        [pltpu.VMEM((kernel * padded, channels), BF16)] * 2
        + [pltpu.VMEM((padded, channels), BF16)],
    )
    factor = 1.0 / (n_dp * length * n_ctx) ** 0.5
    mines, others = [], []
    for at, size in enumerate(sizes):
        kept = len(late) // 2
        mine, theirs = call(
            functools.partial(kernel_grad_kernel, factor, cuts[at]),
            (act, act_x, act_z, act_zx[at], gts[0], *swapped, *shared),
            [pltpu.VMEM((kept * narrow, size), F32), pltpu.VMEM((kept * narrow, size), BF16)],
        )
        other = swap(theirs, "dp", late[kept])
        while kept > 1:
            kept //= 2
            mine, theirs = call(
                fold_kernel,
                (mine, other),
                [pltpu.VMEM((kept * narrow, size), F32), pltpu.VMEM((kept * narrow, size), BF16)],
            )
            other = swap(theirs, "dp", late[kept])
        mines.append(mine)
        others.append(other)

    by_rows = pl.BlockSpec((block, channels), lambda i: (i, 0))
    grad_in = call(
        functools.partial(input_grad_kernel, kernel, pool),
        (highs, lows, near_g, normed, inv_rms, gain_v),
        [jax.ShapeDtypeStruct((length, channels), BF16)],
        grid=(length // block,),
        out_specs=[by_rows],
    )[0]
    grad_conv = call(
        functools.partial(join_kernel, kernel),
        (*mines, *others),
        [jax.ShapeDtypeStruct((kernel, width, narrow), F32)],
    )[0]
    return grad_in[None], jnp.transpose(grad_conv, (1, 0, 2))


def solution(mesh):
    in_specs = (
        P("dp", "ctx", None),
        P("dp", "ctx"),
        P(),
        P(),
        P(),
        P(),
        P(),
        P(),
        P(),
        P("dp", "ctx", None),
    )
    out_specs = (P("dp", "ctx", None), P("ctx", None, "dp"))
    return jax.shard_map(
        per_device, mesh=mesh, in_specs=in_specs, out_specs=out_specs, check_vma=False
    )
```

```python
import functools

import jax
import jax.numpy as jnp
from jax import lax
from jax.experimental import pallas as pl
from jax.experimental.pallas import tpu as pltpu
from jax.sharding import PartitionSpec as P


HEADS = 6
DH = 128

EPSILON = 1e-06
GELU_SCALE = 0.7978845608028654
CUBIC = 0.044715
F32 = jnp.float32
BF16 = jnp.bfloat16
VMEM_LIMIT = 28 << 20
FLOPS_PER_MICRO = 1.15e9
X_BIT, Z_BIT = 1, 4
BLOCK = 128


def dot_nn(left, right):
    return lax.dot_general(left, right, (((1,), (0,)), ((), ())), preferred_element_type=F32)


def dot_nt(left, right):
    return lax.dot_general(left, right, (((1,), (1,)), ((), ())), preferred_element_type=F32)


def dot_tn(left, right):
    return lax.dot_general(left, right, (((0,), (0,)), ((), ())), preferred_element_type=F32)


def split2(value):
    high = value.astype(BF16)
    return high, (value - high.astype(F32)).astype(BF16)


def iota(shape, dim):
    return lax.broadcasted_iota(jnp.int32, shape, dim)


def normed_of(summed):
    inv_rms = lax.rsqrt(jnp.mean(summed * summed, axis=-1, keepdims=True) + EPSILON)
    return inv_rms, summed * inv_rms


def gelu_of(u):
    tanh_val = jnp.tanh(GELU_SCALE * (u + CUBIC * (u * u * u)))
    return tanh_val, 0.5 * u * (1.0 + tanh_val)


def pick(index, values):
    out = jnp.int32(values[0])
    for at, value in enumerate(values[1:], 1):
        out = jnp.where(index == at, jnp.int32(value), out)
    return out


def start_copies(pairs, sems):
    copies = [pltpu.make_async_copy(src, dst, sems.at[i]) for i, (src, dst) in enumerate(pairs)]
    for copy in copies:
        copy.start()
    return copies


def act_kernel(
    kernel, pool, tok_rows, feat_hbm, base_hbm, table_hbm, gain_hbm, cot_hbm,
    taps, sums, normed_out, inv_out, gain, cot, feat, base, table, act_buf, spread, embed, sems,
):
    half = kernel // 2
    rows, channels = feat.shape
    block = BLOCK
    count = rows // block
    small = ((base_hbm, base), (table_hbm, table), (gain_hbm, gain))
    parts = tuple(
        (feat_hbm.at[pl.ds(i * block, block)], feat.at[pl.ds(i * block, block)]) for i in range(count)
    )
    copies = start_copies(small + parts + ((cot_hbm, cot),), sems)
    padded = taps.shape[0] // kernel
    shape = (kernel * padded, rows)
    row = iota(shape, 0)
    tap = sum((row >= padded * j).astype(jnp.int32) for j in range(1, kernel))
    token = row - tap * padded
    known = token < tok_rows + 2
    token = jnp.where(token == tok_rows, -1, jnp.where(token == tok_rows + 1, tok_rows, token))
    offset = iota(shape, 1) - tap + half - token * pool
    spread[...] = ((offset >= 0) & (offset < pool) & known).astype(BF16)
    for copy in copies[: len(small)]:
        copy.wait()
    gain_f = gain[...].reshape(1, channels).astype(F32)
    onehot = (iota((table.shape[0], rows), 0) == base[...]).astype(BF16)
    embed[...] = dot_tn(onehot, table[...])
    for copy in copies[len(small) : len(small) + count]:
        copy.wait()

    summed = feat[...].astype(F32) + embed[...]
    inv_rms, normed = normed_of(summed)
    act_buf[...] = gelu_of(normed * gain_f)[1].astype(BF16)
    normed_out[...] = normed
    inv_out[...] = jnp.broadcast_to(inv_rms, inv_out.shape)
    taps[...] = dot_nn(spread[...], act_buf[...])
    plain = spread[half * padded : (half + 1) * padded, :]
    counts = dot_nt(plain, onehot).astype(BF16)
    sums[...] = dot_nn(plain, feat[...]) + dot_nn(counts, table[...])

    for copy in copies[len(small) + count :]:
        copy.wait()


def taps_kernel(kernel, blocks, taps, pairs, *rest):
    outs, turn = rest[:blocks], rest[blocks]
    me = lax.axis_index("ctx")
    padded = taps.shape[0] // kernel
    highs = []
    for j in range(kernel):
        high, low = split2(taps[j * padded : (j + 1) * padded, :])
        highs.append(high)
        pairs[j] = jnp.concatenate([high, low], axis=0)
    width = taps.shape[1] // blocks
    for b in range(blocks):
        turn[b ^ me] = jnp.concatenate([h[:, b * width : (b + 1) * width] for h in highs], axis=1)
    for b in range(blocks):
        outs[b][...] = turn[b]


def pool_kernel(pool, tok_rows, pairs, sums, weights, cot, rows):
    padded = sums.shape[0]
    total = dot_nn(pairs[0], weights[0])
    for j in range(1, pairs.shape[0]):
        total = total + dot_nn(pairs[j], weights[j])
    conv = total[:padded] + total[padded:]
    value = (sums[...] + conv) * (1.0 / pool)
    high, low = split2(value)
    rows[:padded, :] = high
    rows[padded : padded + tok_rows, :] = cot[...]
    low_f = low.astype(F32)
    ends = [low_f[:1], low_f[tok_rows - 1 : tok_rows + 2]]
    ends = jnp.concatenate(ends + [jnp.zeros((4, low.shape[1]), F32)], axis=0)
    rows[padded + tok_rows :, :] = ends.astype(BF16)


def neighbours(me, order, count, befores, afters, ends):
    zero = jnp.zeros(ends.shape[1:], F32)
    ends[0] = zero
    ends[count + 1] = zero
    for rel, before, after in zip(order, befores, afters):
        owner = me ^ rel
        ends[owner + 1, 0:1, :] = before
        ends[owner + 1, 1:2, :] = after
    return [(ends[me ^ rel, 1:2, :], ends[(me ^ rel) + 2, 0:1, :]) for rel in order]


def pack_kernel(order, tok_rows, *refs):
    *parts, out, buf, ends = refs
    me = lax.axis_index("ctx")
    tails = [part[tok_rows : tok_rows + 8, :].astype(F32) for part in parts]
    extra = neighbours(
        me, order, len(parts), [tail[0:1] for tail in tails], [tail[1:2] for tail in tails], ends
    )
    for at, (part, (first, last)) in enumerate(zip(parts, extra)):
        value = part[:tok_rows, :].astype(F32)
        row = iota(value.shape, 0)
        value = value + jnp.where(row == 0, first, 0.0) + jnp.where(row == tok_rows - 1, last, 0.0)
        buf[at * tok_rows : (at + 1) * tok_rows, :] = value.astype(BF16)
    total = buf.shape[0]
    eye = (iota((total, total), 0) == iota((total, total), 1)).astype(BF16)
    out[...] = dot_tn(buf[...], eye).astype(BF16)


def attention_kernel(pool, order, tok_rows, near_rels, late, *refs):
    blocks = len(order)
    parts, refs = refs[:blocks], refs[blocks:]
    (wq, wk, wv_hbm, wo_hbm), refs = refs[:4], refs[4:]
    g_out, refs = refs[0], refs[1:]
    gts, refs = refs[: len(near_rels)], refs[len(near_rels) :]
    p_buf, c_buf, q_buf, k_buf, v_buf, ga_buf, gq_buf, gk_buf, gv_buf = refs[:9]
    probs_buf, turn, ends, wv, wo, sems = refs[9:]
    copies = start_copies(((wv_hbm, wv), (wo_hbm, wo)), sems)
    padded = parts[0].shape[0] - tok_rows - 8
    befores, afters, firsts, lasts = [], [], [], []
    for part in parts:
        tail = part[tok_rows : tok_rows + 8, :].astype(F32)
        lows = part[padded + tok_rows :, :].astype(F32)
        firsts.append(part[:8, :].astype(F32)[0:1] + lows[0:1])
        lasts.append(part[tok_rows - 8 : tok_rows, :].astype(F32)[7:8] + lows[1:2])
        befores.append(tail[0:1] + lows[2:3])
        afters.append(tail[1:2] + lows[3:4])
    extra = neighbours(lax.axis_index("ctx"), order, blocks, befores, afters, ends)
    for at, (part, first, last, (to_first, to_last)) in enumerate(zip(parts, firsts, lasts, extra)):
        value = part[:tok_rows, :].astype(F32)
        row = iota(value.shape, 0)
        value = jnp.where(row == 0, first + to_first, value)
        value = jnp.where(row == tok_rows - 1, last + to_last, value)
        here = slice(at * tok_rows, (at + 1) * tok_rows)
        p_buf[here, :] = value.astype(BF16)
        c_buf[here, :] = part[padded : padded + tok_rows, :]
    q_buf[...] = dot_nn(p_buf[...], wq[...]).astype(BF16)
    k_buf[...] = dot_nn(p_buf[...], wk[...]).astype(BF16)
    scale = 1.0 / DH**0.5
    heads = [slice(h * DH, (h + 1) * DH) for h in range(HEADS)]
    scores = [dot_nt(k_buf[:, cols], q_buf[:, cols]) * scale for cols in heads]
    for h, score in enumerate(scores):
        expo = jnp.exp(score - jnp.max(score, axis=0, keepdims=True))
        probs_buf[h] = expo / jnp.sum(expo, axis=0, keepdims=True)
    copies[0].wait()
    v_buf[...] = dot_nn(p_buf[...], wv[...]).astype(BF16)
    copies[1].wait()
    ga_buf[...] = dot_nt(wo[...], c_buf[...]).astype(BF16)
    probs_b = [probs_buf[h].astype(BF16) for h in range(HEADS)]
    outs = [dot_tn(v_buf[:, cols], p).astype(BF16) for cols, p in zip(heads, probs_b)]
    terms = [dot_nn(v_buf[:, cols], ga_buf[cols, :]) for cols in heads]
    for cols, p in zip(heads, probs_b):
        gv_buf[:, cols] = dot_nt(p, ga_buf[cols, :]).astype(BF16)
    slopes = []
    for h, cols in enumerate(heads):
        delta = jnp.sum(ga_buf[cols, :].astype(F32) * outs[h].astype(F32), axis=0, keepdims=True)
        slopes.append((probs_buf[h] * (terms[h] - delta) * scale).astype(BF16))
    for cols, slope in zip(heads, slopes):
        gk_buf[:, cols] = dot_nn(slope, q_buf[:, cols]).astype(BF16)
        gq_buf[:, cols] = dot_tn(slope, k_buf[:, cols]).astype(BF16)
    grad = jnp.transpose(c_buf[...].astype(F32))
    for src, weight in ((gq_buf, wq), (gk_buf, wk), (gv_buf, wv)):
        grad = grad + dot_nt(weight[...], src[...])
    turned = (grad * (1.0 / pool)).astype(BF16)
    g_out[...] = turned
    count = turn.shape[0]
    span = turned.shape[0] // count
    me = lax.axis_index("dp")
    for o in range(count):
        turn[o ^ me] = turned[o * span : (o + 1) * span, :]
    for at, rel in enumerate(late):
        gts[0][at * span : (at + 1) * span, :] = turn[rel]
    half = len(late) // 2
    core = lax.axis_index("ctx") % 2
    for gt, base in zip(gts[1:], near_rels[1:]):
        for at in range(half):
            rel = pick(core, [late[at], late[half + at]])
            gt[at * span : (at + 1) * span, :] = turn[base ^ rel]


def spread_kernel(kernel, tok_rows, befores, afters, g_ref, weights, highs, lows, near):
    tokens = g_ref.shape[1]
    padded = near.shape[0]
    me = lax.axis_index("ctx")
    row = iota((padded, tokens), 0)
    source = jnp.where(
        row == 0, pick(me, befores), jnp.where(row == tok_rows + 1, pick(me, afters), row - 1)
    )
    source = jnp.where(row > tok_rows + 1, -1, source)
    chosen = (source == iota((padded, tokens), 1)).astype(BF16)
    rows = dot_nt(chosen, g_ref[...]).astype(BF16)
    near[...] = rows
    for j in range(kernel):
        part = slice(j * padded, (j + 1) * padded)
        highs[part, :], lows[part, :] = split2(dot_nt(rows, weights[j]))


def input_grad_kernel(
    kernel, pool, highs, lows, near, normed_ref, inv_ref, gain, out
):
    half = kernel // 2
    rows, channels = out.shape
    padded = near.shape[0]
    start = pl.program_id(0) * rows
    here = pl.ds(pl.multiple_of(start, rows), rows)
    shape = (rows, kernel * padded)
    col = iota(shape, 1)
    tap = sum((col >= padded * j).astype(jnp.int32) for j in range(1, kernel))
    token = col - tap * padded - 1
    offset = iota(shape, 0) + start - tap + half - token * pool
    spread = ((offset >= 0) & (offset < pool)).astype(BF16)
    grad_act = dot_nn(spread, highs[...]) + dot_nn(spread, lows[...])
    plain = spread[:, half * padded : (half + 1) * padded]
    grad_rows = dot_nn(plain, near[...])
    gain_f = gain[...].reshape(1, channels).astype(F32)
    unit = normed_ref[here, :]
    u = unit * gain_f
    tanh_val = gelu_of(u)[0]
    slopes = 0.5 * (1.0 + tanh_val) + 0.5 * u * (1.0 - tanh_val * tanh_val) * GELU_SCALE * (
        1.0 + 3.0 * CUBIC * (u * u)
    )
    grad_norm = grad_act * slopes * gain_f
    mean = jnp.mean(grad_norm * unit, axis=-1, keepdims=True)
    out[...] = (grad_rows + inv_ref[here, :1] * (grad_norm - unit * mean)).astype(BF16)


def cut_kernel(value, *outs):
    at = 0
    for out in outs:
        out[...] = value[at : at + out.shape[0], :]
        at += out.shape[0]


def merge_kernel(*refs):
    *parts, out, turned = refs
    at = 0
    for part in parts:
        here = slice(at, at + part.shape[0])
        value = part[...]
        out[here, :] = value
        turned[here, :] = pltpu.roll(value.astype(F32), value.shape[1] // 2, axis=1).astype(BF16)
        at += part.shape[0]


def kernel_grad_kernel(factor, begin, *refs):
    *acts, own, here, other, mine, theirs = refs
    first = lax.axis_index("ctx") % 2 == 0
    gts = [own[...]]
    step = mine.shape[0]
    for at in range(0, here.shape[0], step):
        a, b = here[at : at + step, :], other[at : at + step, :]
        gts.append(jnp.concatenate([jnp.where(first, a, b), jnp.where(first, b, a)], axis=0))
    span, size = mine.shape
    total = None
    for act, gt in zip(acts, gts):
        at = begin if act.shape[0] > size else 0
        term = dot_nt(gt, act[at : at + size, :])
        total = term if total is None else total + term
    total = total * factor
    mine[...] = total[:span, :]
    theirs[...] = total[span:, :].astype(BF16)


def fold_kernel(mine, other, kept, sent):
    span = kept.shape[0]
    kept[...] = mine[:span, :] + other[:span, :].astype(F32)
    sent[...] = (mine[span:, :] + other[span:, :].astype(F32)).astype(BF16)


def join_kernel(kernel, *refs):
    *parts, out, buf, sems = refs
    width = out.shape[1]
    half = len(parts) // 2
    sums = [a[...] + b[...].astype(F32) for a, b in zip(parts[:half], parts[half:])]
    total = jnp.transpose(jnp.concatenate(sums, axis=1))
    copies = [pltpu.make_async_copy(buf.at[j], out.at[j], sems.at[j]) for j in range(kernel)]
    for j in range(kernel):
        buf[j] = total[j * width : (j + 1) * width, :]
        copies[j].start()
    for copy in copies:
        copy.wait()


def xor_order(count):
    order = [0]
    bit = count // 2
    while bit:
        order = order + [v ^ bit for v in order]
        bit //= 2
    return order


def swap(value, axis, bit):
    count = lax.axis_size(axis)
    return lax.ppermute(value, axis, [(i, i ^ bit) for i in range(count)])


WHOLE = pl.BlockSpec(memory_space=pltpu.VMEM)


def call(body, args, outs, scratch=(), micros=1, **options):
    options.setdefault("in_specs", [WHOLE] * len(args))
    options.setdefault("out_specs", [WHOLE] * len(outs))
    return pl.pallas_call(
        body,
        out_shape=list(outs),
        scratch_shapes=list(scratch),
        compiler_params=pltpu.CompilerParams(vmem_limit_bytes=VMEM_LIMIT),
        cost_estimate=pl.CostEstimate(
            flops=int(micros * FLOPS_PER_MICRO), bytes_accessed=0, transcendentals=0
        ),
        **options,
    )(*args)


def outside(*values):
    return [pltpu.with_memory_space_constraint(value, pltpu.HBM) for value in values]


def bits_of(count):
    return [1 << at for at in range(count.bit_length() - 1)]


def sums_of(bits):
    out = [0]
    for bit in bits:
        out = out + [bit + value for value in out]
    return out


def per_device(
    features, bases, dna_table, norm_gain, w_conv, w_query, w_key, w_value, w_out, cotangent
):
    feat, cot = features[0], cotangent[0]
    kernel = w_conv.shape[0]
    length, channels = feat.shape
    tok_rows = cot.shape[0]
    pool = length // tok_rows
    n_ctx, n_dp = lax.axis_size("ctx"), lax.axis_size("dp")
    tokens = n_ctx * tok_rows
    width = channels // n_ctx
    narrow = channels // n_dp
    near_rels = [0, X_BIT, Z_BIT, X_BIT + Z_BIT]
    late = sums_of([bit for bit in bits_of(n_dp) if bit not in (X_BIT, Z_BIT)])

    order = xor_order(n_ctx)
    place = {rel: at for at, rel in enumerate(order)}
    befores = [-1] + [place[c ^ (c - 1)] * tok_rows + tok_rows - 1 for c in range(1, n_ctx)]
    afters = [place[c ^ (c + 1)] * tok_rows for c in range(n_ctx - 1)] + [-1]

    hbm = pl.BlockSpec(memory_space=pltpu.HBM)
    block = BLOCK
    wide = -(-(tok_rows + 2) // 8) * 8
    taps, sums, normed, inv_rms, gain_v, cot_v = call(
        functools.partial(act_kernel, kernel, pool, tok_rows),
        outside(feat, bases, dna_table, norm_gain, cot),
        [
            pltpu.VMEM((kernel * wide, channels), F32),
            pltpu.VMEM((wide, channels), F32),
            pltpu.VMEM((length, channels), F32),
            pltpu.VMEM((length, 128), F32),
            pltpu.VMEM(norm_gain.shape, BF16),
            pltpu.VMEM(cot.shape, BF16),
        ],
        [
            pltpu.VMEM(feat.shape, BF16),
            pltpu.VMEM(bases.shape, jnp.int32),
            pltpu.VMEM(dna_table.shape, BF16),
            pltpu.VMEM(feat.shape, BF16),
            pltpu.VMEM((kernel * wide, length), BF16),
            pltpu.VMEM((length, channels), F32),
        ]
        + [pltpu.SemaphoreType.DMA((4 + length // block,))],
        in_specs=[hbm] * 5,
        micros=3,
    )
    pairs, *acts = call(
        functools.partial(taps_kernel, kernel, n_ctx),
        (taps,),
        [pltpu.VMEM((kernel, 2 * wide, channels), BF16)]
        + [pltpu.VMEM((wide, kernel * width), BF16)] * n_ctx,
        [pltpu.VMEM((n_ctx, wide, kernel * width), BF16)],
    )
    swapped = [acts[0]]
    for rel in order[1:]:
        swapped.append(swap(acts[rel], "ctx", rel))
    acts = swapped
    pooled = call(
        functools.partial(pool_kernel, pool, tok_rows),
        (pairs, sums, w_conv, cot_v),
        [pltpu.VMEM((wide + tok_rows + 8, channels), BF16)],
    )[0]
    rows = [pooled]
    bit = n_ctx // 2
    while bit:
        rows = rows + [swap(value, "ctx", bit) for value in rows]
        bit //= 2

    act = call(
        functools.partial(pack_kernel, order, tok_rows),
        acts,
        [pltpu.VMEM((kernel * width, tokens), BF16)],
        [
            pltpu.VMEM((tokens, kernel * width), BF16),
            pltpu.VMEM((n_ctx + 2, 8, kernel * width), F32),
        ],
    )[0]

    act_z = swap(act, "dp", Z_BIT)
    act_x = swap(act, "dp", X_BIT)

    g_all, *gts = call(
        functools.partial(attention_kernel, pool, order, tok_rows, near_rels, late),
        [*rows, w_query, w_key] + outside(w_value, w_out),
        [pltpu.VMEM((channels, tokens), BF16), pltpu.VMEM((len(late) * narrow, tokens), BF16)]
        + [pltpu.VMEM((len(late) // 2 * narrow, tokens), BF16)] * (len(near_rels) - 1),
        [pltpu.VMEM((tokens, channels), BF16)] * 5
        + [pltpu.VMEM((channels, tokens), BF16)]
        + [pltpu.VMEM((tokens, channels), BF16)] * 3
        + [
            pltpu.VMEM((HEADS, tokens, tokens), F32),
            pltpu.VMEM((n_dp, narrow, tokens), BF16),
            pltpu.VMEM((n_ctx + 2, 8, channels), F32),
            pltpu.VMEM(w_value.shape, BF16),
            pltpu.VMEM(w_out.shape, BF16),
            pltpu.SemaphoreType.DMA((2,)),
        ],
        in_specs=[WHOLE] * (n_ctx + 2) + [hbm] * 2,
        micros=5,
    )

    depth = kernel * width
    cuts = [0, -(-depth // 32) * 16, depth]
    sizes = [end - begin for begin, end in zip(cuts, cuts[1:])]
    act_zx = call(cut_kernel, (act_z,), [pltpu.VMEM((size, tokens), BF16) for size in sizes])
    act_zx = list(act_zx)
    for at, value in enumerate(act_zx):
        act_zx[at] = swap(value, "dp", X_BIT)
    swapped = []
    for at, rel in enumerate(near_rels[1:], 1):
        swapped.append(swap(gts[at], "dp", rel))
    merged, turned = call(
        merge_kernel,
        swapped,
        [pltpu.VMEM((sum(value.shape[0] for value in swapped), tokens), BF16)] * 2,
    )
    shared = swap(turned, "ctx", 1)

    padded = -(-(tok_rows + 2) // 8) * 8
    highs, lows, near_g = call(
        functools.partial(spread_kernel, kernel, tok_rows, befores, afters),
        (g_all, w_conv),
        [pltpu.VMEM((kernel * padded, channels), BF16)] * 2
        + [pltpu.VMEM((padded, channels), BF16)],
    )
    factor = 1.0 / (n_dp * length * n_ctx) ** 0.5
    mines, others = [], []
    for at, size in enumerate(sizes):
        kept = len(late) // 2
        mine, theirs = call(
            functools.partial(kernel_grad_kernel, factor, cuts[at]),
            (act, act_x, act_z, act_zx[at], gts[0], merged, shared),
            [pltpu.VMEM((kept * narrow, size), F32), pltpu.VMEM((kept * narrow, size), BF16)],
        )
        other = swap(theirs, "dp", late[kept])
        while kept > 1:
            kept //= 2
            mine, theirs = call(
                fold_kernel,
                (mine, other),
                [pltpu.VMEM((kept * narrow, size), F32), pltpu.VMEM((kept * narrow, size), BF16)],
            )
            other = swap(theirs, "dp", late[kept])
        mines.append(mine)
        others.append(other)

    by_rows = pl.BlockSpec((block, channels), lambda i: (i, 0))
    grad_in = call(
        functools.partial(input_grad_kernel, kernel, pool),
        (highs, lows, near_g, normed, inv_rms, gain_v),
        [jax.ShapeDtypeStruct((length, channels), BF16)],
        grid=(length // block,),
        out_specs=[by_rows],
    )[0]
    grad_conv = call(
        functools.partial(join_kernel, kernel),
        (*mines, *others),
        [jax.ShapeDtypeStruct((kernel, width, narrow), F32)],
        [pltpu.VMEM((kernel, width, narrow), F32), pltpu.SemaphoreType.DMA((kernel,))],
        out_specs=[hbm],
    )[0]
    return grad_in[None], jnp.transpose(grad_conv, (1, 0, 2))


def solution(mesh):
    in_specs = (
        P("dp", "ctx", None),
        P("dp", "ctx"),
        P(),
        P(),
        P(),
        P(),
        P(),
        P(),
        P(),
        P("dp", "ctx", None),
    )
    out_specs = (P("dp", "ctx", None), P("ctx", None, "dp"))
    return jax.shard_map(
        per_device, mesh=mesh, in_specs=in_specs, out_specs=out_specs, check_vma=False
    )
```

```python
import functools

import jax
import jax.numpy as jnp
from jax import lax
from jax.experimental import pallas as pl
from jax.experimental.pallas import tpu as pltpu
from jax.sharding import PartitionSpec as P


HEADS = 6
DH = 128

EPSILON = 1e-06
GELU_SCALE = 0.7978845608028654
CUBIC = 0.044715
F32 = jnp.float32
BF16 = jnp.bfloat16
VMEM_LIMIT = 28 << 20
FLOPS_PER_MICRO = 1.15e9
X_BIT, Z_BIT = 1, 4
BLOCK = 128


def dot_nn(left, right):
    return lax.dot_general(left, right, (((1,), (0,)), ((), ())), preferred_element_type=F32)


def dot_nt(left, right):
    return lax.dot_general(left, right, (((1,), (1,)), ((), ())), preferred_element_type=F32)


def dot_tn(left, right):
    return lax.dot_general(left, right, (((0,), (0,)), ((), ())), preferred_element_type=F32)


def split2(value):
    high = value.astype(BF16)
    return high, (value - high.astype(F32)).astype(BF16)


def iota(shape, dim):
    return lax.broadcasted_iota(jnp.int32, shape, dim)


def normed_of(summed):
    inv_rms = lax.rsqrt(jnp.mean(summed * summed, axis=-1, keepdims=True) + EPSILON)
    return inv_rms, summed * inv_rms


def gelu_of(u):
    tanh_val = jnp.tanh(GELU_SCALE * (u + CUBIC * (u * u * u)))
    return tanh_val, 0.5 * u * (1.0 + tanh_val)


def pick(index, values):
    out = jnp.int32(values[0])
    for at, value in enumerate(values[1:], 1):
        out = jnp.where(index == at, jnp.int32(value), out)
    return out


def start_copies(pairs, sems):
    copies = [pltpu.make_async_copy(src, dst, sems.at[i]) for i, (src, dst) in enumerate(pairs)]
    for copy in copies:
        copy.start()
    return copies


def act_kernel(
    kernel, pool, tok_rows, feat_hbm, base_hbm, table_hbm, gain_hbm, cot_hbm,
    taps, sums, normed_out, inv_out, gain, cot, feat, base, table, act_buf, spread, embed, sems,
):
    half = kernel // 2
    rows, channels = feat.shape
    block = BLOCK
    count = rows // block
    small = ((base_hbm, base), (table_hbm, table), (gain_hbm, gain))
    parts = tuple(
        (feat_hbm.at[pl.ds(i * block, block)], feat.at[pl.ds(i * block, block)]) for i in range(count)
    )
    copies = start_copies(small + parts + ((cot_hbm, cot),), sems)
    padded = taps.shape[0] // kernel
    shape = (kernel * padded, rows)
    row = iota(shape, 0)
    tap = sum((row >= padded * j).astype(jnp.int32) for j in range(1, kernel))
    token = row - tap * padded
    known = token < tok_rows + 2
    token = jnp.where(token == tok_rows, -1, jnp.where(token == tok_rows + 1, tok_rows, token))
    offset = iota(shape, 1) - tap + half - token * pool
    spread[...] = ((offset >= 0) & (offset < pool) & known).astype(BF16)
    for copy in copies[: len(small)]:
        copy.wait()
    gain_f = gain[...].reshape(1, channels).astype(F32)
    onehot = (iota((table.shape[0], rows), 0) == base[...]).astype(BF16)
    embed[...] = dot_tn(onehot, table[...])
    for copy in copies[len(small) : len(small) + count]:
        copy.wait()

    summed = feat[...].astype(F32) + embed[...]
    inv_rms, normed = normed_of(summed)
    act_buf[...] = gelu_of(normed * gain_f)[1].astype(BF16)
    normed_out[...] = normed
    inv_out[...] = jnp.broadcast_to(inv_rms, inv_out.shape)
    taps[...] = dot_nn(spread[...], act_buf[...])
    plain = spread[half * padded : (half + 1) * padded, :]
    counts = dot_nt(plain, onehot).astype(BF16)
    sums[...] = dot_nn(plain, feat[...]) + dot_nn(counts, table[...])

    for copy in copies[len(small) + count :]:
        copy.wait()


def taps_kernel(kernel, blocks, taps, pairs, *rest):
    outs, turn = rest[:blocks], rest[blocks]
    me = lax.axis_index("ctx")
    padded = taps.shape[0] // kernel
    highs = []
    for j in range(kernel):
        high, low = split2(taps[j * padded : (j + 1) * padded, :])
        highs.append(high)
        pairs[j] = jnp.concatenate([high, low], axis=0)
    width = taps.shape[1] // blocks
    for b in range(blocks):
        turn[b ^ me] = jnp.concatenate([h[:, b * width : (b + 1) * width] for h in highs], axis=1)
    for b in range(blocks):
        outs[b][...] = turn[b]


def pool_kernel(pool, tok_rows, pairs, sums, weights, cot, rows):
    padded = sums.shape[0]
    total = dot_nn(pairs[0], weights[0])
    for j in range(1, pairs.shape[0]):
        total = total + dot_nn(pairs[j], weights[j])
    conv = total[:padded] + total[padded:]
    value = (sums[...] + conv) * (1.0 / pool)
    high, low = split2(value)
    rows[:padded, :] = high
    rows[padded : padded + tok_rows, :] = cot[...]
    low_f = low.astype(F32)
    ends = [low_f[:1], low_f[tok_rows - 1 : tok_rows + 2]]
    ends = jnp.concatenate(ends + [jnp.zeros((4, low.shape[1]), F32)], axis=0)
    rows[padded + tok_rows :, :] = ends.astype(BF16)


def neighbours(me, order, count, befores, afters, ends):
    zero = jnp.zeros(ends.shape[1:], F32)
    ends[0] = zero
    ends[count + 1] = zero
    for rel, before, after in zip(order, befores, afters):
        owner = me ^ rel
        ends[owner + 1, 0:1, :] = before
        ends[owner + 1, 1:2, :] = after
    return [(ends[me ^ rel, 1:2, :], ends[(me ^ rel) + 2, 0:1, :]) for rel in order]


def pack_kernel(order, tok_rows, *refs):
    *parts, out, buf, ends = refs
    me = lax.axis_index("ctx")
    tails = [part[tok_rows : tok_rows + 8, :].astype(F32) for part in parts]
    extra = neighbours(
        me, order, len(parts), [tail[0:1] for tail in tails], [tail[1:2] for tail in tails], ends
    )
    for at, (part, (first, last)) in enumerate(zip(parts, extra)):
        value = part[:tok_rows, :].astype(F32)
        row = iota(value.shape, 0)
        value = value + jnp.where(row == 0, first, 0.0) + jnp.where(row == tok_rows - 1, last, 0.0)
        buf[at * tok_rows : (at + 1) * tok_rows, :] = value.astype(BF16)
    total = buf.shape[0]
    eye = (iota((total, total), 0) == iota((total, total), 1)).astype(BF16)
    out[...] = dot_tn(buf[...], eye).astype(BF16)


def attention_kernel(pool, order, tok_rows, near_rels, late, *refs):
    blocks = len(order)
    parts, refs = refs[:blocks], refs[blocks:]
    (wq, wk, wv, wo), refs = refs[:4], refs[4:]
    g_out, refs = refs[0], refs[1:]
    gts, refs = refs[: len(near_rels)], refs[len(near_rels) :]
    p_buf, c_buf, q_buf, k_buf, v_buf, ga_buf, gq_buf, gk_buf, gv_buf = refs[:9]
    probs_buf, turn, ends = refs[9:]
    padded = parts[0].shape[0] - tok_rows - 8
    befores, afters, firsts, lasts = [], [], [], []
    for part in parts:
        tail = part[tok_rows : tok_rows + 8, :].astype(F32)
        lows = part[padded + tok_rows :, :].astype(F32)
        firsts.append(part[:8, :].astype(F32)[0:1] + lows[0:1])
        lasts.append(part[tok_rows - 8 : tok_rows, :].astype(F32)[7:8] + lows[1:2])
        befores.append(tail[0:1] + lows[2:3])
        afters.append(tail[1:2] + lows[3:4])
    extra = neighbours(lax.axis_index("ctx"), order, blocks, befores, afters, ends)
    for at, (part, first, last, (to_first, to_last)) in enumerate(zip(parts, firsts, lasts, extra)):
        value = part[:tok_rows, :].astype(F32)
        row = iota(value.shape, 0)
        value = jnp.where(row == 0, first + to_first, value)
        value = jnp.where(row == tok_rows - 1, last + to_last, value)
        here = slice(at * tok_rows, (at + 1) * tok_rows)
        p_buf[here, :] = value.astype(BF16)
        c_buf[here, :] = part[padded : padded + tok_rows, :]
    q_buf[...] = dot_nn(p_buf[...], wq[...]).astype(BF16)
    k_buf[...] = dot_nn(p_buf[...], wk[...]).astype(BF16)
    scale = 1.0 / DH**0.5
    heads = [slice(h * DH, (h + 1) * DH) for h in range(HEADS)]
    scores = [dot_nt(k_buf[:, cols], q_buf[:, cols]) * scale for cols in heads]
    for h, score in enumerate(scores):
        expo = jnp.exp(score - jnp.max(score, axis=0, keepdims=True))
        probs_buf[h] = expo / jnp.sum(expo, axis=0, keepdims=True)
    v_buf[...] = dot_nn(p_buf[...], wv[...]).astype(BF16)
    ga_buf[...] = dot_nt(wo[...], c_buf[...]).astype(BF16)
    probs_b = [probs_buf[h].astype(BF16) for h in range(HEADS)]
    outs = [dot_tn(v_buf[:, cols], p).astype(BF16) for cols, p in zip(heads, probs_b)]
    terms = [dot_nn(v_buf[:, cols], ga_buf[cols, :]) for cols in heads]
    for cols, p in zip(heads, probs_b):
        gv_buf[:, cols] = dot_nt(p, ga_buf[cols, :]).astype(BF16)
    slopes = []
    for h, cols in enumerate(heads):
        delta = jnp.sum(ga_buf[cols, :].astype(F32) * outs[h].astype(F32), axis=0, keepdims=True)
        slopes.append((probs_buf[h] * (terms[h] - delta) * scale).astype(BF16))
    for cols, slope in zip(heads, slopes):
        gk_buf[:, cols] = dot_nn(slope, q_buf[:, cols]).astype(BF16)
        gq_buf[:, cols] = dot_tn(slope, k_buf[:, cols]).astype(BF16)
    grad = jnp.transpose(c_buf[...].astype(F32))
    for src, weight in ((gq_buf, wq), (gk_buf, wk), (gv_buf, wv)):
        grad = grad + dot_nt(weight[...], src[...])
    turned = (grad * (1.0 / pool)).astype(BF16)
    g_out[...] = turned
    count = turn.shape[0]
    span = turned.shape[0] // count
    me = lax.axis_index("dp")
    for o in range(count):
        turn[o ^ me] = turned[o * span : (o + 1) * span, :]
    for at, rel in enumerate(late):
        gts[0][at * span : (at + 1) * span, :] = turn[rel]
    half = len(late) // 2
    core = lax.axis_index("ctx") % 2
    for gt, base in zip(gts[1:], near_rels[1:]):
        for at in range(half):
            rel = pick(core, [late[at], late[half + at]])
            gt[at * span : (at + 1) * span, :] = turn[base ^ rel]


def spread_kernel(kernel, tok_rows, befores, afters, g_ref, weights, highs, lows, near):
    tokens = g_ref.shape[1]
    padded = near.shape[0]
    me = lax.axis_index("ctx")
    row = iota((padded, tokens), 0)
    source = jnp.where(
        row == 0, pick(me, befores), jnp.where(row == tok_rows + 1, pick(me, afters), row - 1)
    )
    source = jnp.where(row > tok_rows + 1, -1, source)
    chosen = (source == iota((padded, tokens), 1)).astype(BF16)
    rows = dot_nt(chosen, g_ref[...]).astype(BF16)
    near[...] = rows
    for j in range(kernel):
        part = slice(j * padded, (j + 1) * padded)
        highs[part, :], lows[part, :] = split2(dot_nt(rows, weights[j]))


def input_grad_kernel(
    kernel, pool, highs, lows, near, normed_ref, inv_ref, gain, out
):
    half = kernel // 2
    rows, channels = out.shape
    padded = near.shape[0]
    start = pl.program_id(0) * rows
    here = pl.ds(pl.multiple_of(start, rows), rows)
    shape = (rows, kernel * padded)
    col = iota(shape, 1)
    tap = sum((col >= padded * j).astype(jnp.int32) for j in range(1, kernel))
    token = col - tap * padded - 1
    offset = iota(shape, 0) + start - tap + half - token * pool
    spread = ((offset >= 0) & (offset < pool)).astype(BF16)
    grad_act = dot_nn(spread, highs[...]) + dot_nn(spread, lows[...])
    plain = spread[:, half * padded : (half + 1) * padded]
    grad_rows = dot_nn(plain, near[...])
    gain_f = gain[...].reshape(1, channels).astype(F32)
    unit = normed_ref[here, :]
    u = unit * gain_f
    tanh_val = gelu_of(u)[0]
    slopes = 0.5 * (1.0 + tanh_val) + 0.5 * u * (1.0 - tanh_val * tanh_val) * GELU_SCALE * (
        1.0 + 3.0 * CUBIC * (u * u)
    )
    grad_norm = grad_act * slopes * gain_f
    mean = jnp.mean(grad_norm * unit, axis=-1, keepdims=True)
    out[...] = (grad_rows + inv_ref[here, :1] * (grad_norm - unit * mean)).astype(BF16)


def cut_kernel(value, *outs):
    at = 0
    for out in outs:
        out[...] = value[at : at + out.shape[0], :]
        at += out.shape[0]


def merge_kernel(*refs):
    *parts, out, turned = refs
    at = 0
    for part in parts:
        here = slice(at, at + part.shape[0])
        value = part[...]
        out[here, :] = value
        turned[here, :] = pltpu.roll(value.astype(F32), value.shape[1] // 2, axis=1).astype(BF16)
        at += part.shape[0]


def kernel_grad_kernel(factor, begin, *refs):
    *acts, own, here, other, mine, theirs = refs
    first = lax.axis_index("ctx") % 2 == 0
    gts = [own[...]]
    step = mine.shape[0]
    for at in range(0, here.shape[0], step):
        a, b = here[at : at + step, :], other[at : at + step, :]
        gts.append(jnp.concatenate([jnp.where(first, a, b), jnp.where(first, b, a)], axis=0))
    span, size = mine.shape
    total = None
    for act, gt in zip(acts, gts):
        at = begin if act.shape[0] > size else 0
        term = dot_nt(gt, act[at : at + size, :])
        total = term if total is None else total + term
    total = total * factor
    mine[...] = total[:span, :]
    theirs[...] = total[span:, :].astype(BF16)


def fold_kernel(mine, other, kept, sent):
    span = kept.shape[0]
    kept[...] = mine[:span, :] + other[:span, :].astype(F32)
    sent[...] = (mine[span:, :] + other[span:, :].astype(F32)).astype(BF16)


def join_kernel(kernel, *refs):
    *parts, out, buf, sems = refs
    width = out.shape[1]
    half = len(parts) // 2
    sums = [a[...] + b[...].astype(F32) for a, b in zip(parts[:half], parts[half:])]
    total = jnp.transpose(jnp.concatenate(sums, axis=1))
    copies = [pltpu.make_async_copy(buf.at[j], out.at[j], sems.at[j]) for j in range(kernel)]
    for j in range(kernel):
        buf[j] = total[j * width : (j + 1) * width, :]
        copies[j].start()
    for copy in copies:
        copy.wait()


def xor_order(count):
    order = [0]
    bit = count // 2
    while bit:
        order = order + [v ^ bit for v in order]
        bit //= 2
    return order


def swap(value, axis, bit):
    count = lax.axis_size(axis)
    return lax.ppermute(value, axis, [(i, i ^ bit) for i in range(count)])


WHOLE = pl.BlockSpec(memory_space=pltpu.VMEM)


def call(body, args, outs, scratch=(), micros=1, **options):
    options.setdefault("in_specs", [WHOLE] * len(args))
    options.setdefault("out_specs", [WHOLE] * len(outs))
    return pl.pallas_call(
        body,
        out_shape=list(outs),
        scratch_shapes=list(scratch),
        compiler_params=pltpu.CompilerParams(vmem_limit_bytes=VMEM_LIMIT),
        cost_estimate=pl.CostEstimate(
            flops=int(micros * FLOPS_PER_MICRO), bytes_accessed=0, transcendentals=0
        ),
        **options,
    )(*args)


def outside(*values):
    return [pltpu.with_memory_space_constraint(value, pltpu.HBM) for value in values]


def bits_of(count):
    return [1 << at for at in range(count.bit_length() - 1)]


def sums_of(bits):
    out = [0]
    for bit in bits:
        out = out + [bit + value for value in out]
    return out


def per_device(
    features, bases, dna_table, norm_gain, w_conv, w_query, w_key, w_value, w_out, cotangent
):
    feat, cot = features[0], cotangent[0]
    kernel = w_conv.shape[0]
    length, channels = feat.shape
    tok_rows = cot.shape[0]
    pool = length // tok_rows
    n_ctx, n_dp = lax.axis_size("ctx"), lax.axis_size("dp")
    tokens = n_ctx * tok_rows
    width = channels // n_ctx
    narrow = channels // n_dp
    near_rels = [0, X_BIT, Z_BIT, X_BIT + Z_BIT]
    late = sums_of([bit for bit in bits_of(n_dp) if bit not in (X_BIT, Z_BIT)])

    order = xor_order(n_ctx)
    place = {rel: at for at, rel in enumerate(order)}
    befores = [-1] + [place[c ^ (c - 1)] * tok_rows + tok_rows - 1 for c in range(1, n_ctx)]
    afters = [place[c ^ (c + 1)] * tok_rows for c in range(n_ctx - 1)] + [-1]

    hbm = pl.BlockSpec(memory_space=pltpu.HBM)
    block = BLOCK
    wide = -(-(tok_rows + 2) // 8) * 8
    taps, sums, normed, inv_rms, gain_v, cot_v = call(
        functools.partial(act_kernel, kernel, pool, tok_rows),
        outside(feat, bases, dna_table, norm_gain, cot),
        [
            pltpu.VMEM((kernel * wide, channels), F32),
            pltpu.VMEM((wide, channels), F32),
            pltpu.VMEM((length, channels), F32),
            pltpu.VMEM((length, 128), F32),
            pltpu.VMEM(norm_gain.shape, BF16),
            pltpu.VMEM(cot.shape, BF16),
        ],
        [
            pltpu.VMEM(feat.shape, BF16),
            pltpu.VMEM(bases.shape, jnp.int32),
            pltpu.VMEM(dna_table.shape, BF16),
            pltpu.VMEM(feat.shape, BF16),
            pltpu.VMEM((kernel * wide, length), BF16),
            pltpu.VMEM((length, channels), F32),
        ]
        + [pltpu.SemaphoreType.DMA((4 + length // block,))],
        in_specs=[hbm] * 5,
        micros=3,
    )
    pairs, *acts = call(
        functools.partial(taps_kernel, kernel, n_ctx),
        (taps,),
        [pltpu.VMEM((kernel, 2 * wide, channels), BF16)]
        + [pltpu.VMEM((wide, kernel * width), BF16)] * n_ctx,
        [pltpu.VMEM((n_ctx, wide, kernel * width), BF16)],
    )
    swapped = [acts[0]]
    for rel in order[1:]:
        swapped.append(swap(acts[rel], "ctx", rel))
    acts = swapped
    pooled = call(
        functools.partial(pool_kernel, pool, tok_rows),
        (pairs, sums, w_conv, cot_v),
        [pltpu.VMEM((wide + tok_rows + 8, channels), BF16)],
    )[0]
    rows = [pooled]
    bit = n_ctx // 2
    while bit:
        rows = rows + [swap(value, "ctx", bit) for value in rows]
        bit //= 2

    act = call(
        functools.partial(pack_kernel, order, tok_rows),
        acts,
        [pltpu.VMEM((kernel * width, tokens), BF16)],
        [
            pltpu.VMEM((tokens, kernel * width), BF16),
            pltpu.VMEM((n_ctx + 2, 8, kernel * width), F32),
        ],
    )[0]

    act_z = swap(act, "dp", Z_BIT)
    act_x = swap(act, "dp", X_BIT)

    g_all, *gts = call(
        functools.partial(attention_kernel, pool, order, tok_rows, near_rels, late),
        (*rows, w_query, w_key, w_value, w_out),
        [pltpu.VMEM((channels, tokens), BF16), pltpu.VMEM((len(late) * narrow, tokens), BF16)]
        + [pltpu.VMEM((len(late) // 2 * narrow, tokens), BF16)] * (len(near_rels) - 1),
        [pltpu.VMEM((tokens, channels), BF16)] * 5
        + [pltpu.VMEM((channels, tokens), BF16)]
        + [pltpu.VMEM((tokens, channels), BF16)] * 3
        + [
            pltpu.VMEM((HEADS, tokens, tokens), F32),
            pltpu.VMEM((n_dp, narrow, tokens), BF16),
            pltpu.VMEM((n_ctx + 2, 8, channels), F32),
        ],
        micros=5,
    )

    depth = kernel * width
    cuts = [0, -(-depth // 32) * 16, depth]
    sizes = [end - begin for begin, end in zip(cuts, cuts[1:])]
    act_zx = call(cut_kernel, (act_z,), [pltpu.VMEM((size, tokens), BF16) for size in sizes])
    act_zx = list(act_zx)
    for at, value in enumerate(act_zx):
        act_zx[at] = swap(value, "dp", X_BIT)
    swapped = []
    for at, rel in enumerate(near_rels[1:], 1):
        swapped.append(swap(gts[at], "dp", rel))
    merged, turned = call(
        merge_kernel,
        swapped,
        [pltpu.VMEM((sum(value.shape[0] for value in swapped), tokens), BF16)] * 2,
    )
    shared = swap(turned, "ctx", 1)

    padded = -(-(tok_rows + 2) // 8) * 8
    highs, lows, near_g = call(
        functools.partial(spread_kernel, kernel, tok_rows, befores, afters),
        (g_all, w_conv),
        [pltpu.VMEM((kernel * padded, channels), BF16)] * 2
        + [pltpu.VMEM((padded, channels), BF16)],
    )
    factor = 1.0 / (n_dp * length * n_ctx) ** 0.5
    mines, others = [], []
    for at, size in enumerate(sizes):
        kept = len(late) // 2
        mine, theirs = call(
            functools.partial(kernel_grad_kernel, factor, cuts[at]),
            (act, act_x, act_z, act_zx[at], gts[0], merged, shared),
            [pltpu.VMEM((kept * narrow, size), F32), pltpu.VMEM((kept * narrow, size), BF16)],
        )
        other = swap(theirs, "dp", late[kept])
        while kept > 1:
            kept //= 2
            mine, theirs = call(
                fold_kernel,
                (mine, other),
                [pltpu.VMEM((kept * narrow, size), F32), pltpu.VMEM((kept * narrow, size), BF16)],
            )
            other = swap(theirs, "dp", late[kept])
        mines.append(mine)
        others.append(other)

    by_rows = pl.BlockSpec((block, channels), lambda i: (i, 0))
    grad_in = call(
        functools.partial(input_grad_kernel, kernel, pool),
        (highs, lows, near_g, normed, inv_rms, gain_v),
        [jax.ShapeDtypeStruct((length, channels), BF16)],
        grid=(length // block,),
        out_specs=[by_rows],
    )[0]
    grad_conv = call(
        functools.partial(join_kernel, kernel),
        (*mines, *others),
        [jax.ShapeDtypeStruct((kernel, width, narrow), F32)],
        [pltpu.VMEM((kernel, width, narrow), F32), pltpu.SemaphoreType.DMA((kernel,))],
        out_specs=[hbm],
    )[0]
    return grad_in[None], jnp.transpose(grad_conv, (1, 0, 2))


def solution(mesh):
    in_specs = (
        P("dp", "ctx", None),
        P("dp", "ctx"),
        P(),
        P(),
        P(),
        P(),
        P(),
        P(),
        P(),
        P("dp", "ctx", None),
    )
    out_specs = (P("dp", "ctx", None), P("ctx", None, "dp"))
    return jax.shard_map(
        per_device, mesh=mesh, in_specs=in_specs, out_specs=out_specs, check_vma=False
    )
```

```python
import functools

import jax
import jax.numpy as jnp
from jax import lax
from jax.experimental import pallas as pl
from jax.experimental.pallas import tpu as pltpu
from jax.sharding import PartitionSpec as P


HEADS = 6
DH = 128

EPSILON = 1e-06
GELU_SCALE = 0.7978845608028654
CUBIC = 0.044715
F32 = jnp.float32
BF16 = jnp.bfloat16
VMEM_LIMIT = 28 << 20
FLOPS_PER_MICRO = 1.15e9
X_BIT, Z_BIT = 1, 4
BLOCK = 128


def dot_nn(left, right):
    return lax.dot_general(left, right, (((1,), (0,)), ((), ())), preferred_element_type=F32)


def dot_nt(left, right):
    return lax.dot_general(left, right, (((1,), (1,)), ((), ())), preferred_element_type=F32)


def dot_tn(left, right):
    return lax.dot_general(left, right, (((0,), (0,)), ((), ())), preferred_element_type=F32)


def split2(value):
    high = value.astype(BF16)
    return high, (value - high.astype(F32)).astype(BF16)


def iota(shape, dim):
    return lax.broadcasted_iota(jnp.int32, shape, dim)


def normed_of(summed):
    inv_rms = lax.rsqrt(jnp.mean(summed * summed, axis=-1, keepdims=True) + EPSILON)
    return inv_rms, summed * inv_rms


def gelu_of(u):
    tanh_val = jnp.tanh(GELU_SCALE * (u + CUBIC * (u * u * u)))
    return tanh_val, 0.5 * u * (1.0 + tanh_val)


def pick(index, values):
    out = jnp.int32(values[0])
    for at, value in enumerate(values[1:], 1):
        out = jnp.where(index == at, jnp.int32(value), out)
    return out


def start_copies(pairs, sems):
    copies = [pltpu.make_async_copy(src, dst, sems.at[i]) for i, (src, dst) in enumerate(pairs)]
    for copy in copies:
        copy.start()
    return copies


def act_kernel(
    kernel, pool, tok_rows, feat_hbm, base_hbm, table_hbm, gain_hbm, cot_hbm,
    taps, sums, normed_out, inv_out, gain, cot, feat, base, table, act_buf, spread, embed, sems,
):
    half = kernel // 2
    rows, channels = feat.shape
    block = BLOCK
    count = rows // block
    small = ((base_hbm, base), (table_hbm, table), (gain_hbm, gain))
    parts = tuple(
        (feat_hbm.at[pl.ds(i * block, block)], feat.at[pl.ds(i * block, block)]) for i in range(count)
    )
    copies = start_copies(small + parts + ((cot_hbm, cot),), sems)
    padded = taps.shape[0] // kernel
    shape = (kernel * padded, rows)
    row = iota(shape, 0)
    tap = sum((row >= padded * j).astype(jnp.int32) for j in range(1, kernel))
    token = row - tap * padded
    known = token < tok_rows + 2
    token = jnp.where(token == tok_rows, -1, jnp.where(token == tok_rows + 1, tok_rows, token))
    offset = iota(shape, 1) - tap + half - token * pool
    spread[...] = ((offset >= 0) & (offset < pool) & known).astype(BF16)
    for copy in copies[: len(small)]:
        copy.wait()
    gain_f = gain[...].reshape(1, channels).astype(F32)
    onehot = (iota((table.shape[0], rows), 0) == base[...]).astype(BF16)
    embed[...] = dot_tn(onehot, table[...])
    for copy in copies[len(small) : len(small) + count]:
        copy.wait()

    summed = feat[...].astype(F32) + embed[...]
    inv_rms, normed = normed_of(summed)
    act_buf[...] = gelu_of(normed * gain_f)[1].astype(BF16)
    normed_out[...] = normed
    inv_out[...] = jnp.broadcast_to(inv_rms, inv_out.shape)
    taps[...] = dot_nn(spread[...], act_buf[...])
    plain = spread[half * padded : (half + 1) * padded, :]
    counts = dot_nt(plain, onehot).astype(BF16)
    sums[...] = dot_nn(plain, feat[...]) + dot_nn(counts, table[...])

    for copy in copies[len(small) + count :]:
        copy.wait()


def taps_kernel(kernel, blocks, taps, pairs, *rest):
    outs, turn = rest[:blocks], rest[blocks]
    me = lax.axis_index("ctx")
    padded = taps.shape[0] // kernel
    highs = []
    for j in range(kernel):
        high, low = split2(taps[j * padded : (j + 1) * padded, :])
        highs.append(high)
        pairs[j] = jnp.concatenate([high, low], axis=0)
    width = taps.shape[1] // blocks
    for b in range(blocks):
        turn[b ^ me] = jnp.concatenate([h[:, b * width : (b + 1) * width] for h in highs], axis=1)
    for b in range(blocks):
        outs[b][...] = turn[b]


def pool_kernel(pool, tok_rows, pairs, sums, weights, cot, rows):
    padded = sums.shape[0]
    total = dot_nn(pairs[0], weights[0])
    for j in range(1, pairs.shape[0]):
        total = total + dot_nn(pairs[j], weights[j])
    conv = total[:padded] + total[padded:]
    value = (sums[...] + conv) * (1.0 / pool)
    high, low = split2(value)
    rows[:padded, :] = high
    rows[padded : padded + tok_rows, :] = cot[...]
    low_f = low.astype(F32)
    ends = [low_f[:1], low_f[tok_rows - 1 : tok_rows + 2]]
    ends = jnp.concatenate(ends + [jnp.zeros((4, low.shape[1]), F32)], axis=0)
    rows[padded + tok_rows :, :] = ends.astype(BF16)


def neighbours(me, order, count, befores, afters, ends):
    zero = jnp.zeros(ends.shape[1:], F32)
    ends[0] = zero
    ends[count + 1] = zero
    for rel, before, after in zip(order, befores, afters):
        owner = me ^ rel
        ends[owner + 1, 0:1, :] = before
        ends[owner + 1, 1:2, :] = after
    return [(ends[me ^ rel, 1:2, :], ends[(me ^ rel) + 2, 0:1, :]) for rel in order]


def pack_kernel(order, tok_rows, *refs):
    *parts, out, buf, ends = refs
    me = lax.axis_index("ctx")
    tails = [part[tok_rows : tok_rows + 8, :].astype(F32) for part in parts]
    extra = neighbours(
        me, order, len(parts), [tail[0:1] for tail in tails], [tail[1:2] for tail in tails], ends
    )
    for at, (part, (first, last)) in enumerate(zip(parts, extra)):
        value = part[:tok_rows, :].astype(F32)
        row = iota(value.shape, 0)
        value = value + jnp.where(row == 0, first, 0.0) + jnp.where(row == tok_rows - 1, last, 0.0)
        buf[at * tok_rows : (at + 1) * tok_rows, :] = value.astype(BF16)
    total = buf.shape[0]
    eye = (iota((total, total), 0) == iota((total, total), 1)).astype(BF16)
    out[...] = dot_tn(buf[...], eye).astype(BF16)


def attention_kernel(pool, order, tok_rows, late, *refs):
    blocks = len(order)
    parts, refs = refs[:blocks], refs[blocks:]
    (wq, wk, wv, wo), refs = refs[:4], refs[4:]
    g_out, refs = refs[0], refs[1:]
    gts, refs = refs[:3], refs[3:]
    p_buf, c_buf, q_buf, k_buf, v_buf, ga_buf, gq_buf, gk_buf, gv_buf = refs[:9]
    probs_buf, turn, ends = refs[9:]
    padded = parts[0].shape[0] - tok_rows - 8
    befores, afters, firsts, lasts = [], [], [], []
    for part in parts:
        tail = part[tok_rows : tok_rows + 8, :].astype(F32)
        lows = part[padded + tok_rows :, :].astype(F32)
        firsts.append(part[:8, :].astype(F32)[0:1] + lows[0:1])
        lasts.append(part[tok_rows - 8 : tok_rows, :].astype(F32)[7:8] + lows[1:2])
        befores.append(tail[0:1] + lows[2:3])
        afters.append(tail[1:2] + lows[3:4])
    extra = neighbours(lax.axis_index("ctx"), order, blocks, befores, afters, ends)
    for at, (part, first, last, (to_first, to_last)) in enumerate(zip(parts, firsts, lasts, extra)):
        value = part[:tok_rows, :].astype(F32)
        row = iota(value.shape, 0)
        value = jnp.where(row == 0, first + to_first, value)
        value = jnp.where(row == tok_rows - 1, last + to_last, value)
        here = slice(at * tok_rows, (at + 1) * tok_rows)
        p_buf[here, :] = value.astype(BF16)
        c_buf[here, :] = part[padded : padded + tok_rows, :]
    q_buf[...] = dot_nn(p_buf[...], wq[...]).astype(BF16)
    k_buf[...] = dot_nn(p_buf[...], wk[...]).astype(BF16)
    scale = 1.0 / DH**0.5
    heads = [slice(h * DH, (h + 1) * DH) for h in range(HEADS)]
    scores = [dot_nt(k_buf[:, cols], q_buf[:, cols]) * scale for cols in heads]
    for h, score in enumerate(scores):
        expo = jnp.exp(score - jnp.max(score, axis=0, keepdims=True))
        probs_buf[h] = expo / jnp.sum(expo, axis=0, keepdims=True)
    v_buf[...] = dot_nn(p_buf[...], wv[...]).astype(BF16)
    ga_buf[...] = dot_nt(wo[...], c_buf[...]).astype(BF16)
    probs_b = [probs_buf[h].astype(BF16) for h in range(HEADS)]
    outs = [dot_tn(v_buf[:, cols], p).astype(BF16) for cols, p in zip(heads, probs_b)]
    terms = [dot_nn(v_buf[:, cols], ga_buf[cols, :]) for cols in heads]
    for cols, p in zip(heads, probs_b):
        gv_buf[:, cols] = dot_nt(p, ga_buf[cols, :]).astype(BF16)
    slopes = []
    for h, cols in enumerate(heads):
        delta = jnp.sum(ga_buf[cols, :].astype(F32) * outs[h].astype(F32), axis=0, keepdims=True)
        slopes.append((probs_buf[h] * (terms[h] - delta) * scale).astype(BF16))
    for cols, slope in zip(heads, slopes):
        gk_buf[:, cols] = dot_nn(slope, q_buf[:, cols]).astype(BF16)
        gq_buf[:, cols] = dot_tn(slope, k_buf[:, cols]).astype(BF16)
    grad = jnp.transpose(c_buf[...].astype(F32))
    for src, weight in ((gq_buf, wq), (gk_buf, wk), (gv_buf, wv)):
        grad = grad + dot_nt(weight[...], src[...])
    turned = (grad * (1.0 / pool)).astype(BF16)
    g_out[...] = turned
    count = turn.shape[0]
    span = turned.shape[0] // count
    me = lax.axis_index("dp")
    for o in range(count):
        turn[o ^ me] = turned[o * span : (o + 1) * span, :]
    for at, rel in enumerate(late):
        gts[0][at * span : (at + 1) * span, :] = turn[rel]
    half = len(late) // 2
    core = lax.axis_index("ctx") % 2
    for gt, bases in zip(gts[1:], ((X_BIT, X_BIT + Z_BIT), (Z_BIT,))):
        for step, base in enumerate(bases):
            for at in range(half):
                rel = pick(core, [late[at], late[half + at]])
                begin = (step * half + at) * span
                gt[begin : begin + span, :] = turn[base ^ rel]


def spread_kernel(kernel, tok_rows, befores, afters, g_ref, weights, highs, lows, near):
    tokens = g_ref.shape[1]
    padded = near.shape[0]
    me = lax.axis_index("ctx")
    row = iota((padded, tokens), 0)
    source = jnp.where(
        row == 0, pick(me, befores), jnp.where(row == tok_rows + 1, pick(me, afters), row - 1)
    )
    source = jnp.where(row > tok_rows + 1, -1, source)
    chosen = (source == iota((padded, tokens), 1)).astype(BF16)
    rows = dot_nt(chosen, g_ref[...]).astype(BF16)
    near[...] = rows
    for j in range(kernel):
        part = slice(j * padded, (j + 1) * padded)
        highs[part, :], lows[part, :] = split2(dot_nt(rows, weights[j]))


def input_grad_kernel(
    kernel, pool, highs, lows, near, normed_ref, inv_ref, gain, out
):
    half = kernel // 2
    rows, channels = out.shape
    padded = near.shape[0]
    start = pl.program_id(0) * rows
    here = pl.ds(pl.multiple_of(start, rows), rows)
    shape = (rows, kernel * padded)
    col = iota(shape, 1)
    tap = sum((col >= padded * j).astype(jnp.int32) for j in range(1, kernel))
    token = col - tap * padded - 1
    offset = iota(shape, 0) + start - tap + half - token * pool
    spread = ((offset >= 0) & (offset < pool)).astype(BF16)
    grad_act = dot_nn(spread, highs[...]) + dot_nn(spread, lows[...])
    plain = spread[:, half * padded : (half + 1) * padded]
    grad_rows = dot_nn(plain, near[...])
    gain_f = gain[...].reshape(1, channels).astype(F32)
    unit = normed_ref[here, :]
    u = unit * gain_f
    tanh_val = gelu_of(u)[0]
    slopes = 0.5 * (1.0 + tanh_val) + 0.5 * u * (1.0 - tanh_val * tanh_val) * GELU_SCALE * (
        1.0 + 3.0 * CUBIC * (u * u)
    )
    grad_norm = grad_act * slopes * gain_f
    mean = jnp.mean(grad_norm * unit, axis=-1, keepdims=True)
    out[...] = (grad_rows + inv_ref[here, :1] * (grad_norm - unit * mean)).astype(BF16)


def cut_kernel(value, *outs):
    at = 0
    for out in outs:
        out[...] = value[at : at + out.shape[0], :]
        at += out.shape[0]


def relay_kernel(own, received, out):
    half = own.shape[0]
    out[:half, :] = own[...]
    out[half:, :] = received[half:, :]


def merge_kernel(from_x, from_z, out, turned):
    at = 0
    for part in (from_x[: from_x.shape[0] // 2, :], from_z[...]):
        here = slice(at, at + part.shape[0])
        out[here, :] = part
        turned[here, :] = pltpu.roll(part.astype(F32), part.shape[1] // 2, axis=1).astype(BF16)
        at += part.shape[0]


def kernel_grad_kernel(factor, begin, *refs):
    *acts, own, here, other, mine, theirs = refs
    first = lax.axis_index("ctx") % 2 == 0
    gts = [own[...]]
    step = mine.shape[0]
    for at in range(0, here.shape[0], step):
        a, b = here[at : at + step, :], other[at : at + step, :]
        gts.append(jnp.concatenate([jnp.where(first, a, b), jnp.where(first, b, a)], axis=0))
    span, size = mine.shape
    total = None
    for act, gt in zip(acts, gts):
        at = begin if act.shape[0] > size else 0
        term = dot_nt(gt, act[at : at + size, :])
        total = term if total is None else total + term
    total = total * factor
    mine[...] = total[:span, :]
    theirs[...] = total[span:, :].astype(BF16)


def fold_kernel(mine, other, kept, sent):
    span = kept.shape[0]
    kept[...] = mine[:span, :] + other[:span, :].astype(F32)
    sent[...] = (mine[span:, :] + other[span:, :].astype(F32)).astype(BF16)


def join_kernel(kernel, *refs):
    *parts, out, buf, sems = refs
    width = out.shape[1]
    half = len(parts) // 2
    sums = [a[...] + b[...].astype(F32) for a, b in zip(parts[:half], parts[half:])]
    total = jnp.transpose(jnp.concatenate(sums, axis=1))
    copies = [pltpu.make_async_copy(buf.at[j], out.at[j], sems.at[j]) for j in range(kernel)]
    for j in range(kernel):
        buf[j] = total[j * width : (j + 1) * width, :]
        copies[j].start()
    for copy in copies:
        copy.wait()


def xor_order(count):
    order = [0]
    bit = count // 2
    while bit:
        order = order + [v ^ bit for v in order]
        bit //= 2
    return order


def swap(value, axis, bit):
    count = lax.axis_size(axis)
    return lax.ppermute(value, axis, [(i, i ^ bit) for i in range(count)])


WHOLE = pl.BlockSpec(memory_space=pltpu.VMEM)


def call(body, args, outs, scratch=(), micros=1, **options):
    options.setdefault("in_specs", [WHOLE] * len(args))
    options.setdefault("out_specs", [WHOLE] * len(outs))
    return pl.pallas_call(
        body,
        out_shape=list(outs),
        scratch_shapes=list(scratch),
        compiler_params=pltpu.CompilerParams(vmem_limit_bytes=VMEM_LIMIT),
        cost_estimate=pl.CostEstimate(
            flops=int(micros * FLOPS_PER_MICRO), bytes_accessed=0, transcendentals=0
        ),
        **options,
    )(*args)


def outside(*values):
    return [pltpu.with_memory_space_constraint(value, pltpu.HBM) for value in values]


def bits_of(count):
    return [1 << at for at in range(count.bit_length() - 1)]


def sums_of(bits):
    out = [0]
    for bit in bits:
        out = out + [bit + value for value in out]
    return out


def per_device(
    features, bases, dna_table, norm_gain, w_conv, w_query, w_key, w_value, w_out, cotangent
):
    feat, cot = features[0], cotangent[0]
    kernel = w_conv.shape[0]
    length, channels = feat.shape
    tok_rows = cot.shape[0]
    pool = length // tok_rows
    n_ctx, n_dp = lax.axis_size("ctx"), lax.axis_size("dp")
    tokens = n_ctx * tok_rows
    width = channels // n_ctx
    narrow = channels // n_dp
    late = sums_of([bit for bit in bits_of(n_dp) if bit not in (X_BIT, Z_BIT)])

    order = xor_order(n_ctx)
    place = {rel: at for at, rel in enumerate(order)}
    befores = [-1] + [place[c ^ (c - 1)] * tok_rows + tok_rows - 1 for c in range(1, n_ctx)]
    afters = [place[c ^ (c + 1)] * tok_rows for c in range(n_ctx - 1)] + [-1]

    hbm = pl.BlockSpec(memory_space=pltpu.HBM)
    block = BLOCK
    wide = -(-(tok_rows + 2) // 8) * 8
    taps, sums, normed, inv_rms, gain_v, cot_v = call(
        functools.partial(act_kernel, kernel, pool, tok_rows),
        outside(feat, bases, dna_table, norm_gain, cot),
        [
            pltpu.VMEM((kernel * wide, channels), F32),
            pltpu.VMEM((wide, channels), F32),
            pltpu.VMEM((length, channels), F32),
            pltpu.VMEM((length, 128), F32),
            pltpu.VMEM(norm_gain.shape, BF16),
            pltpu.VMEM(cot.shape, BF16),
        ],
        [
            pltpu.VMEM(feat.shape, BF16),
            pltpu.VMEM(bases.shape, jnp.int32),
            pltpu.VMEM(dna_table.shape, BF16),
            pltpu.VMEM(feat.shape, BF16),
            pltpu.VMEM((kernel * wide, length), BF16),
            pltpu.VMEM((length, channels), F32),
        ]
        + [pltpu.SemaphoreType.DMA((4 + length // block,))],
        in_specs=[hbm] * 5,
        micros=3,
    )
    pairs, *acts = call(
        functools.partial(taps_kernel, kernel, n_ctx),
        (taps,),
        [pltpu.VMEM((kernel, 2 * wide, channels), BF16)]
        + [pltpu.VMEM((wide, kernel * width), BF16)] * n_ctx,
        [pltpu.VMEM((n_ctx, wide, kernel * width), BF16)],
    )
    swapped = [acts[0]]
    for rel in order[1:]:
        swapped.append(swap(acts[rel], "ctx", rel))
    acts = swapped
    pooled = call(
        functools.partial(pool_kernel, pool, tok_rows),
        (pairs, sums, w_conv, cot_v),
        [pltpu.VMEM((wide + tok_rows + 8, channels), BF16)],
    )[0]
    rows = [pooled]
    bit = n_ctx // 2
    while bit:
        rows = rows + [swap(value, "ctx", bit) for value in rows]
        bit //= 2

    act = call(
        functools.partial(pack_kernel, order, tok_rows),
        acts,
        [pltpu.VMEM((kernel * width, tokens), BF16)],
        [
            pltpu.VMEM((tokens, kernel * width), BF16),
            pltpu.VMEM((n_ctx + 2, 8, kernel * width), F32),
        ],
    )[0]

    act_z = swap(act, "dp", Z_BIT)
    act_x = swap(act, "dp", X_BIT)

    g_all, *gts = call(
        functools.partial(attention_kernel, pool, order, tok_rows, late),
        (*rows, w_query, w_key, w_value, w_out),
        [pltpu.VMEM((channels, tokens), BF16), pltpu.VMEM((len(late) * narrow, tokens), BF16)]
        + [pltpu.VMEM((len(late) // 2 * narrow * steps, tokens), BF16) for steps in (2, 1)],
        [pltpu.VMEM((tokens, channels), BF16)] * 5
        + [pltpu.VMEM((channels, tokens), BF16)]
        + [pltpu.VMEM((tokens, channels), BF16)] * 3
        + [
            pltpu.VMEM((HEADS, tokens, tokens), F32),
            pltpu.VMEM((n_dp, narrow, tokens), BF16),
            pltpu.VMEM((n_ctx + 2, 8, channels), F32),
        ],
        micros=5,
    )

    depth = kernel * width
    cuts = [0, -(-depth // 32) * 16, depth]
    sizes = [end - begin for begin, end in zip(cuts, cuts[1:])]
    act_zx = call(cut_kernel, (act_z,), [pltpu.VMEM((size, tokens), BF16) for size in sizes])
    act_zx = list(act_zx)
    for at, value in enumerate(act_zx):
        act_zx[at] = swap(value, "dp", X_BIT)
    from_x = swap(gts[1], "dp", X_BIT)
    to_z = call(relay_kernel, (gts[2], from_x), [pltpu.VMEM(gts[1].shape, BF16)])[0]
    from_z = swap(to_z, "dp", Z_BIT)
    merged, turned = call(
        merge_kernel, (from_x, from_z), [pltpu.VMEM((3 * gts[2].shape[0], tokens), BF16)] * 2
    )
    shared = swap(turned, "ctx", 1)

    padded = -(-(tok_rows + 2) // 8) * 8
    highs, lows, near_g = call(
        functools.partial(spread_kernel, kernel, tok_rows, befores, afters),
        (g_all, w_conv),
        [pltpu.VMEM((kernel * padded, channels), BF16)] * 2
        + [pltpu.VMEM((padded, channels), BF16)],
    )
    factor = 1.0 / (n_dp * length * n_ctx) ** 0.5
    mines, others = [], []
    for at, size in enumerate(sizes):
        kept = len(late) // 2
        mine, theirs = call(
            functools.partial(kernel_grad_kernel, factor, cuts[at]),
            (act, act_x, act_z, act_zx[at], gts[0], merged, shared),
            [pltpu.VMEM((kept * narrow, size), F32), pltpu.VMEM((kept * narrow, size), BF16)],
        )
        other = swap(theirs, "dp", late[kept])
        while kept > 1:
            kept //= 2
            mine, theirs = call(
                fold_kernel,
                (mine, other),
                [pltpu.VMEM((kept * narrow, size), F32), pltpu.VMEM((kept * narrow, size), BF16)],
            )
            other = swap(theirs, "dp", late[kept])
        mines.append(mine)
        others.append(other)

    by_rows = pl.BlockSpec((block, channels), lambda i: (i, 0))
    grad_in = call(
        functools.partial(input_grad_kernel, kernel, pool),
        (highs, lows, near_g, normed, inv_rms, gain_v),
        [jax.ShapeDtypeStruct((length, channels), BF16)],
        grid=(length // block,),
        out_specs=[by_rows],
    )[0]
    grad_conv = call(
        functools.partial(join_kernel, kernel),
        (*mines, *others),
        [jax.ShapeDtypeStruct((kernel, width, narrow), F32)],
        [pltpu.VMEM((kernel, width, narrow), F32), pltpu.SemaphoreType.DMA((kernel,))],
        out_specs=[hbm],
    )[0]
    return grad_in[None], jnp.transpose(grad_conv, (1, 0, 2))


def solution(mesh):
    in_specs = (
        P("dp", "ctx", None),
        P("dp", "ctx"),
        P(),
        P(),
        P(),
        P(),
        P(),
        P(),
        P(),
        P("dp", "ctx", None),
    )
    out_specs = (P("dp", "ctx", None), P("ctx", None, "dp"))
    return jax.shard_map(
        per_device, mesh=mesh, in_specs=in_specs, out_specs=out_specs, check_vma=False
    )
```
